256 devices in a mesh: dp: 32 (over x, y, core), head: 8 (over z).
Axes of the slice: x: 4, y: 4, z: 8, core: 2. Of those that a mesh axis runs over, the one named last changes fastest.
Arguments:
- queries: bfloat16 [1280, 128, 1024], P('dp', None, 'head'), may hold values from -8 to 8
- resp_keys: bfloat16 [1280, 128, 128], P('dp'), may hold values from -6 to 6
- resp_values: bfloat16 [1280, 128, 128], P('dp'), may hold values from -6 to 6
- prompt_keys: bfloat16 [128, 512, 128], P('dp'), may hold values from -8 to 8
- prompt_values: bfloat16 [128, 512, 128], P('dp'), may hold values from -6 to 6
- grad_out: bfloat16 [1280, 128, 1024], P('dp', None, 'head'), may hold values from -6 to 6
- slot_prompt: int32 [1280], P('dp'), may hold values from -1 to 127, as said below
- slot_length: int32 [1280], P('dp'), may hold values from 0 to 128, as said below
Outputs:
- attn_out: bfloat16 [1280, 128, 1024], P('dp', None, 'head')
- grad_queries: bfloat16 [1280, 128, 1024], P('dp', None, 'head')
- grad_resp_keys: float32 [1280, 128, 128], P('dp', 'head')
- grad_resp_values: float32 [1280, 128, 128], P('dp', 'head')
- grad_prompt_keys: float32 [128, 512, 128], P('dp')
- grad_prompt_values: float32 [128, 512, 128], P('dp')
The draws below stay inside these ranges and needn't reach their ends.
Inputs may be any that keep to these rules, and one draw needn't show every extreme that they name: `slot_prompt`: prompt p is held by index p // 4 of dp. Every prompt is named by exactly 8 slots. At most 2 slots of one device name prompts held by one same device, and this is reached. On some device all 40 slots are live. `slot_length`: 0 exactly in the slots where slot_prompt is -1, else 1 or more; 128 is reached.
All inputs are finite; a program needn't handle non-finite values.
Results may differ from the reference program's by a relative error of at most 0.015.
Values may be sent and summed in bfloat16 or wider, within the bound.
A program may use at most 128 MiB of HBM per device.

```python
import jax
import jax.numpy as jnp
from jax import lax

HD = 128
HQ = 8
PLEN = 512
RLEN = 128
FANOUT = 8
PR_DEV = 4
CAP = 2
SLOTS = 40
PROMPTS = 128
SLOTS_ALL = 1280
N_DP = 32


def draw_queries(key, part):
    values = jax.random.normal(jax.random.fold_in(key, 101), (SLOTS_ALL, RLEN, HQ * HD), jnp.float32)
    return jnp.clip(values, -8.0, 8.0).astype(jnp.bfloat16)


def draw_prompt_keys(key, part):
    values = jax.random.normal(jax.random.fold_in(key, 201), (PROMPTS, PLEN, HD), jnp.float32)
    return jnp.clip(values, -8.0, 8.0).astype(jnp.bfloat16)


def slot_layout(key):
    seed_key = jax.random.fold_in(key, 5150)
    key_list = jax.random.split(seed_key, 5)
    owner_count = FANOUT * PR_DEV // CAP
    widest = min(owner_count + owner_count // 4, N_DP)
    ranking = jnp.arange(N_DP, dtype=jnp.int32)
    mirror = jnp.minimum(ranking, N_DP - 1 - ranking)
    shift_by = (widest - owner_count) * (N_DP - 1 - 2 * mirror) // max(N_DP - 1, 1)
    load_rank = jnp.where(ranking < N_DP // 2, owner_count + shift_by, owner_count - shift_by)
    device_order = jax.random.permutation(key_list[0], N_DP).astype(jnp.int32)
    bounds = jnp.cumsum(load_rank)
    pick_ids = jnp.arange(N_DP * owner_count, dtype=jnp.int32)
    pick_rank = jnp.sum((bounds[None, :] <= pick_ids[:, None]).astype(jnp.int32), axis=1)
    pick_device = device_order[pick_rank]
    owner_table = jnp.transpose(pick_device.reshape(owner_count, N_DP))
    row_order = jax.random.permutation(key_list[1], N_DP).astype(jnp.int32)
    owners = owner_table[row_order]
    per_holder = FANOUT * PR_DEV
    draw_scores = jax.random.randint(key_list[2], (N_DP, per_holder), 0, 4096, jnp.int32) * per_holder + jnp.arange(per_holder, dtype=jnp.int32)[None, :]
    placing = jnp.argsort(jnp.argsort(draw_scores, axis=1), axis=1).astype(jnp.int32)
    pair_index = placing // CAP
    owner_resp = jnp.take_along_axis(owners, pair_index, axis=1).reshape(-1)
    prompt_resp = (jnp.arange(N_DP, dtype=jnp.int32)[:, None] * PR_DEV + jnp.arange(per_holder, dtype=jnp.int32)[None, :] // FANOUT).reshape(-1)
    resp_count = N_DP * per_holder
    order_key = jax.random.randint(key_list[3], (resp_count,), 0, 4096, jnp.int32) * resp_count + jnp.arange(resp_count, dtype=jnp.int32)
    within = jnp.sum(((owner_resp[None, :] == owner_resp[:, None]) & (order_key[None, :] < order_key[:, None])).astype(jnp.int32), axis=1)
    position = owner_resp * SLOTS + within
    lengths = jax.random.randint(key_list[4], (resp_count,), 1, RLEN + 1, jnp.int32)
    lengths = jnp.where(jnp.arange(resp_count, dtype=jnp.int32) % 5 == 0, RLEN, lengths)
    slot_prompt = jnp.full((SLOTS_ALL,), -1, jnp.int32).at[position].set(prompt_resp)
    slot_length = jnp.zeros((SLOTS_ALL,), jnp.int32).at[position].set(lengths)
    return (slot_prompt, slot_length)


def draw_slot_prompt(key, part):
    return slot_layout(key)[0]


def draw_slot_length(key, part):
    return slot_layout(key)[1]


def level_of(key, shape, pieces, low, largest):
    level = 1.0
    for dim, blocks in pieces:
        steps = jax.random.uniform(jax.random.fold_in(jax.random.fold_in(key, 6), dim), (blocks,), jnp.float32, low / len(pieces), largest / len(pieces))
        level = level * jnp.repeat(jnp.exp(steps), shape[dim] // blocks).reshape((-1,) + (1,) * (len(shape) - 1 - dim))
    return level


def scatter_about(own_key, dims, width, bound, shards=(), held_as=jnp.bfloat16):
    entries = jax.random.normal(own_key, dims, jnp.float32) * width
    if len(shards) > 0:
        entries = level_of(own_key, dims, shards, -0.22, 0.18) * entries
    return jnp.clip(entries, min=-bound, max=bound).astype(held_as)


def setup_inputs(seed: int = 0) -> dict:
    key_of = jax.random.split(jax.random.key(seed), 9)
    queries = draw_queries(jax.random.fold_in(key_of[8], 71), 0)
    resp_keys = scatter_about(key_of[1], (SLOTS_ALL, RLEN, HD), 1.0, 6.0, ((0, 32),))
    resp_values = scatter_about(key_of[2], (SLOTS_ALL, RLEN, HD), 1.0, 6.0, ((0, 32),))
    prompt_keys = draw_prompt_keys(jax.random.fold_in(key_of[8], 71), 0)
    prompt_values = scatter_about(key_of[4], (PROMPTS, PLEN, HD), 1.0, 6.0, ((0, 32),))
    grad_out = scatter_about(key_of[5], (SLOTS_ALL, RLEN, HQ * HD), 1.0, 6.0, ((0, 32), (2, 8)))
    slot_prompt = draw_slot_prompt(jax.random.fold_in(key_of[8], 71), 0)
    slot_length = draw_slot_length(jax.random.fold_in(key_of[8], 71), 0)
    return {"queries": queries, "resp_keys": resp_keys, "resp_values": resp_values, "prompt_keys": prompt_keys, "prompt_values": prompt_values, "grad_out": grad_out, "slot_prompt": slot_prompt, "slot_length": slot_length}


def keep_bf16(value):
    return lax.optimization_barrier(value.astype(jnp.bfloat16)).astype(jnp.float32)


def causal_table(resp_len):
    positions = jnp.arange(resp_len, dtype=jnp.int32)
    return positions[:, None] >= positions[None, :]


def prefix_forward(query_rows, key_rows, value_rows, factor):
    scores = jnp.einsum("rhd,nd->hrn", query_rows, key_rows) * factor
    maximum = jnp.max(scores, axis=2)
    exp_terms = jnp.exp(scores - maximum[:, :, None])
    row_sums = jnp.sum(exp_terms, axis=2)
    result = jnp.einsum("hrn,nd->rhd", keep_bf16(exp_terms), value_rows)
    return result / jnp.transpose(row_sums)[:, :, None], maximum + jnp.log(row_sums)


def prefix_backward(query_rows, grad_rows, log_total, delta_rows, key_rows, value_rows, factor):
    scores = jnp.einsum("rhd,nd->hrn", query_rows, key_rows) * factor
    prob_rows = jnp.exp(scores - log_total[:, :, None])
    dprob_rows = jnp.einsum("rhd,nd->hrn", grad_rows, value_rows)
    dscore = keep_bf16(prob_rows * (dprob_rows - delta_rows[:, :, None]))
    grad_query = keep_bf16(jnp.einsum("hrn,nd->rhd", dscore, key_rows) * factor)
    grad_keys = jnp.einsum("hrn,rhd->nd", dscore, query_rows) * factor
    grad_values = jnp.einsum("hrn,rhd->nd", keep_bf16(prob_rows), grad_rows)
    return grad_query, grad_keys, grad_values


def response_forward(query_rows, key_rows, value_rows, factor):
    causal = causal_table(query_rows.shape[1])
    scores = jnp.einsum("sthd,sud->shtu", query_rows, key_rows) * factor
    masked = jnp.where(causal, scores, -1e30)
    maximum = jnp.max(masked, axis=3)
    exp_terms = jnp.where(causal, jnp.exp(masked - maximum[..., None]), 0.0)
    row_sums = jnp.sum(exp_terms, axis=3)
    result = jnp.einsum("shtu,sud->sthd", keep_bf16(exp_terms), value_rows)
    return result / jnp.transpose(row_sums, (0, 2, 1))[..., None], maximum + jnp.log(row_sums)


def response_backward(query_rows, grad_rows, log_total, delta_rows, key_rows, value_rows, factor):
    causal = causal_table(query_rows.shape[1])
    scores = jnp.einsum("sthd,sud->shtu", query_rows, key_rows) * factor
    prob_rows = jnp.where(causal, jnp.exp(jnp.where(causal, scores, -1e30) - log_total[..., None]), 0.0)
    dprob_rows = jnp.einsum("sthd,sud->shtu", grad_rows, value_rows)
    dscore = keep_bf16(prob_rows * (dprob_rows - delta_rows[..., None]))
    grad_query = jnp.einsum("shtu,sud->sthd", dscore, key_rows) * factor
    grad_keys = jnp.einsum("shtu,sthd->sud", dscore, query_rows) * factor
    grad_values = jnp.einsum("shtu,sthd->sud", keep_bf16(prob_rows), grad_rows)
    return grad_query, grad_keys, grad_values


def reference(queries, resp_keys, resp_values, prompt_keys, prompt_values, grad_out, slot_prompt, slot_length):
    total_slots, resp_len, row_width = queries.shape
    head_dim = prompt_keys.shape[2]
    head_count = row_width // head_dim
    factor = head_dim ** -0.5
    group_rows = FANOUT * resp_len
    positions = jnp.arange(resp_len, dtype=jnp.int32)
    is_live = (positions[None, :] < slot_length[:, None]) & (slot_prompt[:, None] >= 0)
    grad_live = jnp.where(is_live[:, :, None], grad_out, jnp.zeros_like(grad_out))
    prompt_ids = jnp.arange(PROMPTS, dtype=jnp.int32)
    member = slot_prompt[:, None] == prompt_ids[None, :]
    ranking = jnp.sum(jnp.where(member, jnp.cumsum(member.astype(jnp.int32), axis=0) - 1, 0), axis=1).astype(jnp.int32)
    slot_ids = jnp.arange(total_slots, dtype=jnp.int32)
    chosen = member[:, :, None] & (ranking[:, None, None] == jnp.arange(FANOUT, dtype=jnp.int32)[None, None, :])
    group_slot = jnp.sum(jnp.where(chosen, slot_ids[:, None, None], 0), axis=0).reshape(PROMPTS * FANOUT).astype(jnp.int32)
    flat_index = (jnp.maximum(slot_prompt, 0) * FANOUT + ranking).astype(jnp.int32)

    group_query = queries[group_slot].reshape(PROMPTS, group_rows, head_count, head_dim)

    def forward_prompt(inputs):
        return prefix_forward(inputs[0].astype(jnp.float32), inputs[1].astype(jnp.float32), inputs[2].astype(jnp.float32), factor)

    prefix_out, prefix_lse = lax.map(forward_prompt, (group_query, prompt_keys, prompt_values))
    part_out = prefix_out.reshape(PROMPTS * FANOUT, resp_len, head_count, head_dim)[flat_index]
    part_lse = jnp.transpose(prefix_lse.reshape(PROMPTS, head_count, FANOUT, resp_len), (0, 2, 1, 3)).reshape(PROMPTS * FANOUT, head_count, resp_len)[flat_index]

    block = total_slots // N_DP

    def split_blocks(value):
        return value.reshape((N_DP, block) + value.shape[1:])

    def local_block(inputs):
        query_rows, key_rows, value_rows, grad_rows, outside, outside_lse, live_rows = inputs
        query4 = query_rows.astype(jnp.float32).reshape(block, resp_len, head_count, head_dim)
        key32 = key_rows.astype(jnp.float32)
        value32 = value_rows.astype(jnp.float32)
        local_out, local_lse = response_forward(query4, key32, value32, factor)
        log_total = jnp.logaddexp(outside_lse, local_lse)
        weight_part = jnp.transpose(jnp.exp(outside_lse - log_total), (0, 2, 1))[..., None]
        weight_local = jnp.transpose(jnp.exp(local_lse - log_total), (0, 2, 1))[..., None]
        merged = weight_part * outside + weight_local * local_out
        attn_rows = keep_bf16(jnp.where(live_rows[:, :, None, None], merged, 0.0))
        grad4 = grad_rows.astype(jnp.float32).reshape(block, resp_len, head_count, head_dim)
        delta_rows = jnp.transpose(jnp.sum(grad4 * attn_rows, axis=3), (0, 2, 1))
        local_dq, local_dk, local_dv = response_backward(query4, grad4, log_total, delta_rows, key32, value32, factor)
        return attn_rows.astype(jnp.bfloat16).reshape(block, resp_len, row_width), log_total, delta_rows, local_dq, local_dk, local_dv

    mapped = lax.map(local_block, (split_blocks(queries), split_blocks(resp_keys), split_blocks(resp_values), split_blocks(grad_live), split_blocks(part_out), split_blocks(part_lse), split_blocks(is_live)))
    attn_out = mapped[0].reshape(total_slots, resp_len, row_width)
    log_total = mapped[1].reshape(total_slots, head_count, resp_len)
    delta = mapped[2].reshape(total_slots, head_count, resp_len)
    local_dq = mapped[3].reshape(total_slots, resp_len, head_count, head_dim)
    grad_resp_keys = mapped[4].reshape(total_slots, resp_len, head_dim)
    grad_resp_values = mapped[5].reshape(total_slots, resp_len, head_dim)

    group_grad = grad_live[group_slot].reshape(PROMPTS, group_rows, head_count, head_dim)

    def group_stat(value):
        return jnp.transpose(value[group_slot].reshape(PROMPTS, FANOUT, head_count, resp_len), (0, 2, 1, 3)).reshape(PROMPTS, head_count, group_rows)

    def backward_prompt(inputs):
        return prefix_backward(inputs[0].astype(jnp.float32), inputs[1].astype(jnp.float32), inputs[2], inputs[3], inputs[4].astype(jnp.float32), inputs[5].astype(jnp.float32), factor)

    prefix_dq, grad_prompt_keys, grad_prompt_values = lax.map(backward_prompt, (group_query, group_grad, group_stat(log_total), group_stat(delta), prompt_keys, prompt_values))
    part_dq = prefix_dq.reshape(PROMPTS * FANOUT, resp_len, head_count, head_dim)[flat_index]
    has_prompt = (slot_prompt >= 0)[:, None, None, None]
    grad_queries = jnp.where(has_prompt, part_dq + local_dq, 0.0).astype(jnp.bfloat16).reshape(total_slots, resp_len, row_width)
    return attn_out, grad_queries, grad_resp_keys, grad_resp_values, grad_prompt_keys, grad_prompt_values
```

```python
import functools
import math

import jax
import jax.numpy as jnp
from jax import lax
from jax.experimental import pallas as pl
from jax.experimental.pallas import tpu as pltpu
from jax.sharding import PartitionSpec as P

FANOUT = 8
LOG2E = math.log2(math.e)
F32 = jnp.float32
BF16 = jnp.bfloat16
STAT = 16


def dot(a, b, dims):
    return lax.dot_general(a, b, (dims, ((), ())), preferred_element_type=F32)


NT = ((1,), (1,))
NN = ((1,), (0,))
TN = ((0,), (0,))


def two_parts(value):
    high = value.astype(BF16)
    low = (value - high.astype(F32)).astype(BF16)
    return high.astype(F32), low.astype(F32)


def pack_rows(first, second):
    width = first.shape[1]
    rows = lax.broadcasted_iota(jnp.int32, (STAT, width), 0)
    a, b = two_parts(first)
    c, d = two_parts(second)
    packed = jnp.where(rows == 0, a, jnp.where(rows == 1, b, jnp.where(rows == 2, c, d)))
    return jnp.where(rows < 4, packed, 0.0).astype(BF16)


def unpack_rows(packed):
    rows = packed.astype(F32)
    return rows[0:1] + rows[1:2], rows[2:3] + rows[3:4]


def live_rows(grad, length):
    row = lax.broadcasted_iota(jnp.int32, grad.shape, 0)
    return jnp.where(row < length, grad, jnp.zeros_like(grad))


def causal(shape):
    return lax.broadcasted_iota(jnp.int32, shape, 0) <= lax.broadcasted_iota(jnp.int32, shape, 1)


def pack_kernel(scale, per_step, slot_ref, length_ref, q_ref, g_ref, k_ref, v_ref, send_ref):
    rows = q_ref.shape[1]
    step = pl.program_id(0)
    for j in range(per_step):
        slot = slot_ref[step * per_step + j]
        query = q_ref[slot]
        grad = live_rows(g_ref[slot], length_ref[slot])
        scores = dot(k_ref[slot], query, NT) * scale
        scores = jnp.where(causal(scores.shape), scores, -1e30)
        top = jnp.max(scores, axis=0, keepdims=True)
        exps = jnp.exp2(scores - top)
        total = jnp.sum(exps, axis=0, keepdims=True)
        grad_prob = dot(v_ref[slot], grad, NT)
        row_sum = jnp.sum(exps * grad_prob, axis=0, keepdims=True) / total
        send_ref[j, 0:rows, :] = query
        send_ref[j, rows : 2 * rows, :] = grad
        send_ref[j, 2 * rows :, :] = pack_rows(top + jnp.log2(total), row_sum)


def pack(slots, lengths, queries, grads, keys, values, scale):
    items = slots.shape[0]
    count, rows, dim = queries.shape
    per_step = 8
    whole = pl.BlockSpec((count, rows, dim), lambda i, a, b: (0, 0, 0))
    return pl.pallas_call(
        functools.partial(pack_kernel, scale, per_step),
        out_shape=jax.ShapeDtypeStruct((items, 2 * rows + STAT, dim), BF16),
        grid_spec=pltpu.PrefetchScalarGridSpec(
            num_scalar_prefetch=2,
            grid=(items // per_step,),
            in_specs=[whole] * 4,
            out_specs=pl.BlockSpec((per_step, 2 * rows + STAT, dim), lambda i, a, b: (i, 0, 0)),
        ),
    )(slots, lengths, queries, grads, keys, values)


def holder_kernel(scale, factor, item_ref, a_ref, b_ref, k_ref, v_ref, out_ref, stat_ref, dk_ref, dv_ref, kt, vt):
    step = pl.program_id(1)

    @pl.when(step == 0)
    def _():
        kt[...] = jnp.transpose(k_ref[0])
        vt[...] = jnp.transpose(v_ref[0])
        dk_ref[...] = jnp.zeros_like(dk_ref)
        dv_ref[...] = jnp.zeros_like(dv_ref)

    half = a_ref.shape[1]
    rows = (half - STAT) // 2
    query = jnp.concatenate([a_ref[0, 0:rows, :], b_ref[0, 0:rows, :]], axis=0)
    grad = jnp.concatenate([a_ref[0, rows : 2 * rows, :], b_ref[0, rows : 2 * rows, :]], axis=0)
    lse_a, sum_a = unpack_rows(a_ref[0, 2 * rows :, :])
    lse_b, sum_b = unpack_rows(b_ref[0, 2 * rows :, :])
    resp_lse = jnp.concatenate([lse_a, lse_b], axis=1)
    resp_sum = jnp.concatenate([sum_a, sum_b], axis=1)
    scores = dot(k_ref[0], query, NT) * scale
    grad_prob = dot(v_ref[0], grad, NT)
    top = jnp.max(scores, axis=0, keepdims=True)
    exps = jnp.exp2(scores - top)
    total = jnp.sum(exps, axis=0, keepdims=True)
    row_sum = jnp.sum(exps * grad_prob, axis=0, keepdims=True)
    prefix_lse = top + jnp.log2(total)
    high = jnp.maximum(prefix_lse, resp_lse)
    lse = high + jnp.log2(jnp.exp2(prefix_lse - high) + jnp.exp2(resp_lse - high))
    weight = jnp.exp2(prefix_lse - lse) / total
    delta = weight * row_sum + jnp.exp2(resp_lse - lse) * resp_sum
    prob = exps * weight
    dscore = (prob * (grad_prob - delta)).astype(BF16)
    prob = prob.astype(BF16)
    dk_ref[0] += dot(dscore, query, NN) * factor
    dv_ref[0] += dot(prob, grad, NN)
    out = jnp.transpose(dot(vt[...], prob, NN)).astype(BF16)
    dq = jnp.transpose(dot(kt[...], dscore, NN) * factor).astype(BF16)
    for j in range(2):
        part = slice(j * rows, (j + 1) * rows)
        out_ref[j, 0:rows, :] = out[part]
        out_ref[j, rows:, :] = dq[part]
        stat_ref[j] = pack_rows(lse[:, part], delta[:, part])


def holder(items, received, keys, values, scale, factor):
    count, height, dim = received.shape
    held, length, _ = keys.shape
    rows = (height - STAT) // 2
    steps = FANOUT // 2
    slot = lambda k: pl.BlockSpec((1, height, dim), lambda p, j, ids: (ids[p * FANOUT + 2 * j + k], 0, 0))
    whole = pl.BlockSpec((1, length, dim), lambda p, j, ids: (p, 0, 0))
    return pl.pallas_call(
        functools.partial(holder_kernel, scale, factor),
        out_shape=(
            jax.ShapeDtypeStruct((held * FANOUT, 2 * rows, dim), BF16),
            jax.ShapeDtypeStruct((held * FANOUT, STAT, dim), BF16),
            jax.ShapeDtypeStruct((held, length, dim), F32),
            jax.ShapeDtypeStruct((held, length, dim), F32),
        ),
        grid_spec=pltpu.PrefetchScalarGridSpec(
            num_scalar_prefetch=1,
            grid=(held, steps),
            in_specs=[slot(0), slot(1), whole, whole],
            out_specs=(
                pl.BlockSpec((2, 2 * rows, dim), lambda p, j, ids: (p * steps + j, 0, 0)),
                pl.BlockSpec((2, STAT, dim), lambda p, j, ids: (p * steps + j, 0, 0)),
                whole,
                whole,
            ),
            scratch_shapes=[pltpu.VMEM((dim, length), BF16)] * 2,
        ),
    )(items, received, received, keys, values)


def local_kernel(
    scale, factor, per_step, fetch_ref, prompt_ref, length_ref, stat_ref, q_ref, g_ref, k_ref, v_ref, out_ref, dq_ref, dkv_ref
):
    step = pl.program_id(0)
    for j in range(per_step):
        slot = step * per_step + j
        live = prompt_ref[slot] >= 0
        lse, delta = unpack_rows(stat_ref[fetch_ref[slot]])
        lse = jnp.where(live, lse, 1e30)
        delta = jnp.where(live, delta, 0.0)
        query = q_ref[j]
        grad = live_rows(g_ref[j], length_ref[slot])
        scores = dot(k_ref[j], query, NT) * scale
        mask = causal(scores.shape)
        prob = jnp.where(mask, jnp.exp2(jnp.where(mask, scores, -1e30) - lse), 0.0)
        grad_prob = dot(v_ref[j], grad, NT)
        dscore = (prob * (grad_prob - delta)).astype(BF16)
        prob = prob.astype(BF16)
        dkv_ref[0, j] = dot(dscore, query, NN) * factor
        dkv_ref[1, j] = dot(prob, grad, NN)
        out_ref[j] = dot(prob, v_ref[j], TN).astype(BF16)
        dq_ref[j] = (dot(dscore, k_ref[j], TN) * factor).astype(BF16)


def local(fetch, prompts, lengths, stats, queries, grads, keys, values, scale, factor):
    count, rows, dim = queries.shape
    per_step = 5
    some = pl.BlockSpec((per_step, rows, dim), lambda i, a, b, c: (i, 0, 0))
    return pl.pallas_call(
        functools.partial(local_kernel, scale, factor, per_step),
        out_shape=(
            jax.ShapeDtypeStruct((count, rows, dim), BF16),
            jax.ShapeDtypeStruct((count, rows, dim), BF16),
            jax.ShapeDtypeStruct((2, count, rows, dim), F32),
        ),
        grid_spec=pltpu.PrefetchScalarGridSpec(
            num_scalar_prefetch=3,
            grid=(count // per_step,),
            in_specs=[pl.BlockSpec(stats.shape, lambda i, a, b, c: (0, 0, 0)), some, some, some, some],
            out_specs=(some, some, pl.BlockSpec((2, per_step, rows, dim), lambda i, a, b, c: (0, i, 0, 0))),
        ),
    )(fetch, prompts, lengths, stats, queries, grads, keys, values)


def merge_kernel(per_step, fetch_ref, prompt_ref, length_ref, *refs):
    back_refs = refs[:per_step]
    out_part, dq_part, out_ref, dq_ref = refs[per_step:]
    rows = out_part.shape[1]
    step = pl.program_id(0)
    for j in range(per_step):
        slot = step * per_step + j
        live = prompt_ref[slot] >= 0
        row = lax.broadcasted_iota(jnp.int32, out_part.shape[1:], 0)
        back = back_refs[j]
        out = back[0, 0:rows, :].astype(F32) + out_part[j].astype(F32)
        dq = back[0, rows : 2 * rows, :].astype(F32) + dq_part[j].astype(F32)
        length = jnp.where(live, length_ref[slot], 0)
        out_ref[j] = jnp.where(row < length, out, 0.0).astype(BF16)
        dq_ref[j] = jnp.where(row < length, dq, 0.0).astype(BF16)


def merge(fetch, prompts, lengths, back, out_part, dq_part):
    count, rows, dim = out_part.shape
    per_step = 8
    some = pl.BlockSpec((per_step, rows, dim), lambda i, a, b, c: (i, 0, 0))

    def one(j):
        return pl.BlockSpec((1, 2 * rows, dim), lambda i, a, b, c: (a[i * per_step + j], 0, 0))

    return pl.pallas_call(
        functools.partial(merge_kernel, per_step),
        out_shape=(jax.ShapeDtypeStruct((count, rows, dim), BF16),) * 2,
        grid_spec=pltpu.PrefetchScalarGridSpec(
            num_scalar_prefetch=3,
            grid=(count // per_step,),
            in_specs=[one(j) for j in range(per_step)] + [some, some],
            out_specs=(some, some),
        ),
    )(fetch, prompts, lengths, *([back] * per_step), out_part, dq_part)


def exchange(value):
    count = lax.axis_size("dp")
    shaped = value.reshape((count, -1) + value.shape[2:])
    return lax.all_to_all(shaped, "dp", split_axis=0, concat_axis=0, tiled=True).reshape(value.shape)


def body(queries, resp_keys, resp_values, prompt_keys, prompt_values, grad_out, slot_prompt, slot_length):
    dp_count = lax.axis_size("dp")
    slot_count, resp_len, dim = queries.shape
    held_count, prompt_len, _ = prompt_keys.shape
    factor = dim ** (-0.5)
    scale = factor * LOG2E
    pair_limit = max(2, FANOUT * held_count // dp_count)
    item_count = dp_count * pair_limit
    slot_ids = jnp.arange(slot_count, dtype=jnp.int32)
    item_ids = jnp.arange(item_count, dtype=jnp.int32)
    holder_own = jnp.where(slot_prompt >= 0, slot_prompt // held_count, -1)
    before = slot_ids[None, :] < slot_ids[:, None]
    order_own = jnp.sum((holder_own[:, None] == holder_own[None, :]) & before, axis=1, dtype=jnp.int32)
    target = jnp.where(holder_own >= 0, holder_own * pair_limit + order_own, -1)
    fetch = jnp.maximum(target, 0)
    send_hit = target[None, :] == item_ids[:, None]
    send_slot = jnp.sum(jnp.where(send_hit, slot_ids[None, :], 0), axis=1, dtype=jnp.int32)
    send_prompt = jnp.sum(jnp.where(send_hit, (slot_prompt % held_count)[None, :] + 1, 0), axis=1, dtype=jnp.int32) - 1
    item_prompt = exchange(send_prompt.reshape(item_count, 1)).reshape(item_count)
    earlier = item_ids[None, :] < item_ids[:, None]
    order_in = jnp.sum((item_prompt[:, None] == item_prompt[None, :]) & earlier, axis=1, dtype=jnp.int32)
    place = jnp.where(item_prompt >= 0, item_prompt * FANOUT + order_in, -1)
    group_ids = jnp.arange(held_count * FANOUT, dtype=jnp.int32)
    group_hit = place[None, :] == group_ids[:, None]
    group_item = jnp.sum(jnp.where(group_hit, item_ids[None, :], 0), axis=1, dtype=jnp.int32)
    back_index = jnp.maximum(place, 0)

    packed = pack(send_slot, slot_length, queries, grad_out, resp_keys, resp_values, scale)
    received = exchange(packed)
    result, stats, prefix_dk, prefix_dv = holder(group_item, received, prompt_keys, prompt_values, scale, factor)
    back_stats = exchange(stats[back_index])
    back = exchange(result[back_index])
    local_out, local_dq, local_dkv = local(
        fetch, slot_prompt, slot_length, back_stats, queries, grad_out, resp_keys, resp_values, scale, factor
    )
    attn_out, grad_queries = merge(fetch, slot_prompt, slot_length, back, local_out, local_dq)
    grad_prompt_keys, grad_prompt_values = lax.psum((prefix_dk, prefix_dv), "head")
    shared = lax.psum_scatter(local_dkv, "head", scatter_dimension=2, tiled=True)
    return (attn_out, grad_queries, shared[0], shared[1], grad_prompt_keys, grad_prompt_values)


def solution(mesh):
    return jax.shard_map(
        body,
        mesh=mesh,
        in_specs=(
            P("dp", None, "head"),
            P("dp", None, None),
            P("dp", None, None),
            P("dp", None, None),
            P("dp", None, None),
            P("dp", None, "head"),
            P("dp"),
            P("dp"),
        ),
        out_specs=(
            P("dp", None, "head"),
            P("dp", None, "head"),
            P("dp", "head", None),
            P("dp", "head", None),
            P("dp", None, None),
            P("dp", None, None),
        ),
        check_vma=False,
    )
```

```python
import functools
import math

import jax
import jax.numpy as jnp
from jax import lax
from jax.experimental import pallas as pl
from jax.experimental.pallas import tpu as pltpu
from jax.sharding import PartitionSpec as P

FANOUT = 8
LOG2E = math.log2(math.e)
F32 = jnp.float32
BF16 = jnp.bfloat16
STAT = 16


MESH = pl.DeviceIdType.MESH
SIDE = 4

def place():
    me = lax.axis_index("dp")
    core = lax.rem(me, 2)
    y = lax.rem(me // 2, SIDE)
    x = me // (2 * SIDE)
    return x, y, core

def device(k, a, b, core):
    x, y = (a, b) if k == 0 else (b, a)
    return {"dp": (x * SIDE + y) * 2 + core}

def step_by(value, by):
    return lax.rem(value + by + SIDE, SIDE)

def neighbours():
    x, y, core = place()
    out = [device(0, x, y, 1 - core)]
    for by in (1, -1):
        for c in range(2):
            out.append(device(0, step_by(x, by), y, c))
            out.append(device(0, x, step_by(y, by), c))
    return out

def everyone():
    x, y, core = place()
    me = (x * SIDE + y) * 2 + core
    return [{"dp": lax.rem(me + k, 2 * SIDE * SIDE)} for k in range(1, 2 * SIDE * SIDE)]


def greet(near):
    barrier = pltpu.get_barrier_semaphore()
    for who in near:
        pl.semaphore_signal(barrier, inc=1, device_id=who, device_id_type=MESH)
    pl.semaphore_wait(barrier, len(near))

def remote(src, dst, send, recv, who):
    return pltpu.make_async_remote_copy(src_ref=src, dst_ref=dst, send_sem=send, recv_sem=recv, device_id=who, device_id_type=MESH)

class Route:
    def __init__(self, k, send, final, mid, rel1, rel2, sems):
        self.k, self.send, self.final, self.mid, self.rel1, self.rel2 = k, send, final, mid, rel1, rel2
        x, y, self.c = place()
        self.a, self.b = (x, y) if k == 0 else (y, x)
        (self.s1, self.r1, self.s1d, self.r1d, self.s1f, self.r1f,
         self.s2, self.r2, self.s2d, self.r2d, self.s2f, self.r2f, self.s0, self.r0, self.local) = sems
    def to_a(self, by): return device(self.k, step_by(self.a, by), self.b, self.c)
    def to_b(self, by, c): return device(self.k, self.a, step_by(self.b, by), c)
    def first_direct(self, side, j):
        by = 1 if side == 0 else -1
        b = step_by(self.b, j)
        r = 3 if side == 0 else 1
        return remote(self.send.at[step_by(self.a, by), b], self.mid.at[r - 1, b], self.s1.at[side, j], self.r1.at[side, j], self.to_a(by))
    def first_far(self, side, j):
        by = 1 if side == 0 else -1
        b = 2 * side + j
        return remote(self.send.at[step_by(self.a, 2), b], self.rel1.at[side, j], self.s1d.at[side, j], self.r1d.at[side, j], self.to_a(by))
    def first_forward(self, side, j):
        by = 1 if side == 0 else -1
        b = 2 * side + j
        return remote(self.rel1.at[side, j], self.mid.at[1, b], self.s1f.at[side, j], self.r1f.at[side, j], self.to_a(by))
    def source(self, r, b):
        return self.send.at[self.a, b] if r == 0 else self.mid.at[r - 1, b]
    def second_direct(self, r, side, c):
        by = 1 if side == 0 else -1
        rb = 3 if side == 0 else 1
        return remote(self.source(r, step_by(self.b, by)).at[c], self.final.at[r, rb, self.c], self.s2.at[r, side, c], self.r2.at[r, side, self.c], self.to_b(by, c))
    def second_far(self, r):
        side = r // 2
        by = 1 if side == 0 else -1
        return remote(self.source(r, step_by(self.b, 2)), self.rel2.at[side, r % 2], self.s2d.at[r], self.r2d.at[r], self.to_b(by, self.c))
    def second_forward(self, r, c):
        side = r // 2
        by = 1 if side == 0 else -1
        return remote(self.rel2.at[side, r % 2, c], self.final.at[r, 2, self.c], self.s2f.at[r, c], self.r2f.at[r, self.c], self.to_b(by, c))
    def cross(self, r):
        return remote(self.source(r, self.b).at[1 - self.c], self.final.at[r, 0, self.c], self.s0.at[r], self.r0.at[r], self.to_b(0, 1 - self.c))
    def own(self, r):
        return pltpu.make_async_copy(self.source(r, self.b).at[self.c], self.final.at[r, 0, self.c], self.local.at[r])

def wait_second_direct(route, r, side):
    for c in range(2):
        by = 1 if side == 0 else -1
        rb = 3 if side == 0 else 1
        d = route.final.at[r, rb, c]
        remote(d, d, route.s2.at[r, side, c], route.r2.at[r, side, c], route.to_b(by, c)).wait_recv()

def wait_second_forward(route, r):
    side = r // 2
    by = 1 if side == 0 else -1
    for c in range(2):
        d = route.final.at[r, 2, c]
        remote(d, d, route.s2f.at[r, c], route.r2f.at[r, c], route.to_b(by, c)).wait_recv()

def wait_cross(route, r):
    d = route.final.at[r, 0, 1 - route.c]
    remote(d, d, route.s0.at[r], route.r0.at[r], route.to_b(0, 1 - route.c)).wait_recv()

def route_sems():
    D = pltpu.SemaphoreType.DMA
    return [D((2, 4)), D((2, 4)), D((2, 2)), D((2, 2)), D((2, 2)), D((2, 2)),
            D((4, 2, 2)), D((4, 2, 2)), D((4,)), D((4,)), D((4, 2)), D((4, 2)), D((4,)), D((4,)), D((4,))]

def route_scratch(height, dim, dtype):
    V = pltpu.VMEM
    return [V((3, 4, 2, height, dim), dtype), V((2, 2, 2, height, dim), dtype), V((2, 2, 2, height, dim), dtype)]

def stages(routes):
    started = []
    def go(copy):
        copy.start(); started.append(copy)
    def second(route, r):
        go(route.second_far(r))
        for side in range(2):
            for c in range(2):
                go(route.second_direct(r, side, c))
        go(route.cross(r)); go(route.own(r))
    def s0():
        for j in range(2):
            for side in range(2):
                for route in routes: go(route.first_far(side, j))
        for route in routes: second(route, 0)
        for j in (2, 1, 3, 0):
            for side in range(2):
                for route in routes: go(route.first_direct(side, j))
    def s1():
        for j in range(2):
            for side in range(2):
                for route in routes:
                    route.first_far(side, j).wait_recv()
                    go(route.first_forward(side, j))
    def relay(route, r):
        route.second_far(r).wait_recv()
        for c in range(2): go(route.second_forward(r, c))
    def s2():
        for route in routes: relay(route, 0)
    def s3():
        for side in range(2):
            r = 3 if side == 0 else 1
            for route in routes:
                for j in range(4): route.first_direct(side, j).wait_recv()
                second(route, r)
    def s4():
        for route in routes:
            for side in range(2):
                for j in range(2): route.first_forward(side, j).wait_recv()
            second(route, 2)
    def s5():
        for r in (3, 1, 2):
            for route in routes: relay(route, r)
    def s6():
        for r in (0, 3, 1, 2):
            for route in routes:
                for side in range(2): wait_second_direct(route, r, side)
                wait_second_forward(route, r); wait_cross(route, r)
    def s7():
        for copy in started:
            if copy.is_remote: copy.wait_send()
            else: copy.wait()
    return [s0, s1, s2, s3, s4, s5, s6, s7]

def exchange_kernel(send_ref, final_ref, *scratch):
    greet(neighbours())
    n = 3 + 15
    routes = []
    for k in range(2):
        part = scratch[k * n:(k + 1) * n]
        routes.append(Route(k, send_ref.at[k], final_ref.at[k], part[0], part[1], part[2], part[3:]))
    for stage in stages(routes): stage()

def torus_exchange(send, cid):
    h, d = send.shape[-2:]
    scratch = []
    for _ in range(2): scratch += route_scratch(h, d, send.dtype) + route_sems()
    return pl.pallas_call(exchange_kernel, out_shape=jax.ShapeDtypeStruct(send.shape, send.dtype),
        in_specs=[pl.BlockSpec(memory_space=pl.ANY)], out_specs=pl.BlockSpec(memory_space=pl.ANY),
        scratch_shapes=scratch, compiler_params=pltpu.CompilerParams(collective_id=cid, has_side_effects=True))(send)


def dot(a, b, dims):
    return lax.dot_general(a, b, (dims, ((), ())), preferred_element_type=F32)


NT = ((1,), (1,))
NN = ((1,), (0,))
TN = ((0,), (0,))


def two_parts(value):
    high = value.astype(BF16)
    low = (value - high.astype(F32)).astype(BF16)
    return high.astype(F32), low.astype(F32)


def pack_rows(first, second, third=0.0):
    width = first.shape[1]
    rows = lax.broadcasted_iota(jnp.int32, (STAT, width), 0)
    a, b = two_parts(first)
    c, d = two_parts(second)
    packed = jnp.where(rows == 0, a, jnp.where(rows == 1, b, jnp.where(rows == 2, c, d)))
    return jnp.where(rows < 4, packed, third).astype(BF16)


def unpack_rows(packed):
    rows = packed.astype(F32)
    return rows[0:1] + rows[1:2], rows[2:3] + rows[3:4]


def live_rows(grad, length):
    row = lax.broadcasted_iota(jnp.int32, grad.shape, 0)
    return jnp.where(row < length, grad, jnp.zeros_like(grad))


def causal(shape):
    return lax.broadcasted_iota(jnp.int32, shape, 0) <= lax.broadcasted_iota(jnp.int32, shape, 1)


def pack_kernel(scale, per_step, slot_ref, prompt_ref, length_ref, q_ref, g_ref, k_ref, v_ref, send_ref):
    rows = q_ref.shape[1]
    step = pl.program_id(0)
    for j in range(per_step):
        slot = slot_ref[step * per_step + j]
        query = q_ref[slot]
        grad = live_rows(g_ref[slot], length_ref[slot])
        scores = dot(k_ref[slot], query, NT) * scale
        scores = jnp.where(causal(scores.shape), scores, -1e30)
        top = jnp.max(scores, axis=0, keepdims=True)
        exps = jnp.exp2(scores - top)
        total = jnp.sum(exps, axis=0, keepdims=True)
        grad_prob = dot(v_ref[slot], grad, NT)
        row_sum = jnp.sum(exps * grad_prob, axis=0, keepdims=True) / total
        send_ref[j, 0:rows, :] = query
        send_ref[j, rows : 2 * rows, :] = grad
        prompt = prompt_ref[step * per_step + j].astype(F32)
        send_ref[j, 2 * rows :, :] = pack_rows(top + jnp.log2(total), row_sum, prompt)


def pack(slots, prompts, lengths, queries, grads, keys, values, scale):
    items = slots.shape[0]
    count, rows, dim = queries.shape
    per_step = 8
    whole = pl.BlockSpec((count, rows, dim), lambda i, a, b, c: (0, 0, 0))
    return pl.pallas_call(
        functools.partial(pack_kernel, scale, per_step),
        out_shape=jax.ShapeDtypeStruct((items, 2 * rows + STAT, dim), BF16),
        grid_spec=pltpu.PrefetchScalarGridSpec(
            num_scalar_prefetch=3,
            grid=(items // per_step,),
            in_specs=[whole] * 4,
            out_specs=pl.BlockSpec((per_step, 2 * rows + STAT, dim), lambda i, a, b, c: (i, 0, 0)),
        ),
    )(slots, prompts, lengths, queries, grads, keys, values)


def holder_kernel(
    scale, factor, item_ref, back_ref, stat_to_ref, a_ref, b_ref, k_ref, v_ref,
    out_ref, stat_ref, dk_ref, dv_ref, kt, vt, out_buf, stat_buf, out_sem, stat_sem,
):
    prompt, step = pl.program_id(0), pl.program_id(1)
    count = pl.num_programs(1)
    index = prompt * count + step

    @pl.when(step == 0)
    def _():
        kt[...] = jnp.transpose(k_ref[0])
        vt[...] = jnp.transpose(v_ref[0])
        dk_ref[...] = jnp.zeros_like(dk_ref)
        dv_ref[...] = jnp.zeros_like(dv_ref)

    def leaving(at, j):
        slot = lax.rem(at, 2)
        item = item_ref[2 * at + j]
        return (
            pltpu.make_async_copy(out_buf.at[slot, j], out_ref.at[back_ref[item]], out_sem.at[slot, j]),
            pltpu.make_async_copy(stat_buf.at[slot, j], stat_ref.at[stat_to_ref[item]], stat_sem.at[slot, j]),
        )

    half = a_ref.shape[1]
    rows = (half - STAT) // 2
    query = jnp.concatenate([a_ref[0, 0:rows, :], b_ref[0, 0:rows, :]], axis=0)
    grad = jnp.concatenate([a_ref[0, rows : 2 * rows, :], b_ref[0, rows : 2 * rows, :]], axis=0)
    lse_a, sum_a = unpack_rows(a_ref[0, 2 * rows :, :])
    lse_b, sum_b = unpack_rows(b_ref[0, 2 * rows :, :])
    resp_lse = jnp.concatenate([lse_a, lse_b], axis=1)
    resp_sum = jnp.concatenate([sum_a, sum_b], axis=1)
    scores = dot(k_ref[0], query, NT) * scale
    grad_prob = dot(v_ref[0], grad, NT)
    top = jnp.max(scores, axis=0, keepdims=True)
    exps = jnp.exp2(scores - top)
    total = jnp.sum(exps, axis=0, keepdims=True)
    row_sum = jnp.sum(exps * grad_prob, axis=0, keepdims=True)
    prefix_lse = top + jnp.log2(total)
    high = jnp.maximum(prefix_lse, resp_lse)
    lse = high + jnp.log2(jnp.exp2(prefix_lse - high) + jnp.exp2(resp_lse - high))
    weight = jnp.exp2(prefix_lse - lse) / total
    delta = weight * row_sum + jnp.exp2(resp_lse - lse) * resp_sum
    prob = exps * weight
    dscore = (prob * (grad_prob - delta)).astype(BF16)
    prob = prob.astype(BF16)
    dk_ref[0] += dot(dscore, query, NN) * factor
    dv_ref[0] += dot(prob, grad, NN)
    out = jnp.transpose(dot(vt[...], prob, NN)).astype(BF16)
    dq = jnp.transpose(dot(kt[...], dscore, NN) * factor).astype(BF16)

    @pl.when(index >= 2)
    def _():
        for j in range(2):
            for copy in leaving(index - 2, j):
                copy.wait()

    slot = lax.rem(index, 2)
    for j in range(2):
        part = slice(j * rows, (j + 1) * rows)
        out_buf[slot, j, 0:rows, :] = out[part]
        out_buf[slot, j, rows:, :] = dq[part]
        stat_buf[slot, j] = pack_rows(lse[:, part], delta[:, part])
        for copy in leaving(index, j):
            copy.start()

    @pl.when(index == pl.num_programs(0) * count - 1)
    def _():
        for at in (index - 1, index):
            for j in range(2):
                for copy in leaving(at, j):
                    copy.wait()


def holder(items, back_to, stat_to, received, keys, values, scale, factor):
    count, height, dim = received.shape
    held, length, _ = keys.shape
    rows = (height - STAT) // 2
    steps = FANOUT // 2

    def one(k):
        return pl.BlockSpec((1, height, dim), lambda p, j, ids, b, c: (ids[p * FANOUT + 2 * j + k], 0, 0))

    whole = pl.BlockSpec((1, length, dim), lambda p, j, ids, b, c: (p, 0, 0))
    return pl.pallas_call(
        functools.partial(holder_kernel, scale, factor),
        out_shape=(
            jax.ShapeDtypeStruct((count, 2 * rows, dim), BF16),
            jax.ShapeDtypeStruct((count, STAT, dim), BF16),
            jax.ShapeDtypeStruct((held, length, dim), F32),
            jax.ShapeDtypeStruct((held, length, dim), F32),
        ),
        grid_spec=pltpu.PrefetchScalarGridSpec(
            num_scalar_prefetch=3,
            grid=(held, steps),
            in_specs=[one(0), one(1), whole, whole],
            out_specs=(
                pl.BlockSpec(memory_space=pl.ANY),
                pl.BlockSpec(memory_space=pl.ANY),
                whole,
                whole,
            ),
            scratch_shapes=[
                pltpu.VMEM((dim, length), BF16),
                pltpu.VMEM((dim, length), BF16),
                pltpu.VMEM((2, 2, 2 * rows, dim), BF16),
                pltpu.VMEM((2, 2, STAT, dim), BF16),
                pltpu.SemaphoreType.DMA((2, 2)),
                pltpu.SemaphoreType.DMA((2, 2)),
            ],
        ),
    )(items, back_to, stat_to, received, received, keys, values)


HEADS = 8


class Ring:
    def __init__(self, own, right, left, sent, came, send_sem, recv_sem):
        self.own, self.sent, self.came, self.send_sem, self.recv_sem = own, sent, came, send_sem, recv_sem
        self.me = lax.axis_index("head")
        self.lanes = ((1, right, 0), (-1, left, right))

    def copy(self, by, at):
        who = {"head": lax.rem(self.me + by + HEADS, HEADS)}
        return remote(self.sent.at[at], self.came.at[at], self.send_sem.at[at], self.recv_sem.at[at], who)

    def step(self, number):
        for by, hops, base in self.lanes:
            if number <= hops:
                target = lax.rem(self.me + by * (hops + 1 - number) + HEADS, HEADS)
                value = self.own(target)
                at = base + number - 1
                if number > 1:
                    self.copy(by, at - 1).wait_recv()
                    value = value + self.came[at - 1].astype(F32)
                self.sent[at] = value.astype(BF16)
                self.copy(by, at).start()

    def result(self):
        value = self.own(self.me)
        for by, hops, base in self.lanes:
            at = base + hops - 1
            self.copy(by, at).wait_recv()
            value = value + self.came[at].astype(F32)
        return value

    def close(self):
        for by, hops, base in self.lanes:
            for at in range(base, base + hops):
                self.copy(by, at).wait_send()


class Spread:
    def __init__(self, all_parts, right, left, send_sem, recv_sem):
        self.all_parts, self.send_sem, self.recv_sem = all_parts, send_sem, recv_sem
        self.me = lax.axis_index("head")
        self.lanes = ((1, right, 0), (-1, left, right))

    def copy(self, by, number, base):
        whose = lax.rem(self.me - by * (number - 1) + HEADS, HEADS)
        who = {"head": lax.rem(self.me + by + HEADS, HEADS)}
        at = base + number - 1
        part = self.all_parts.at[whose]
        return remote(part, part, self.send_sem.at[at], self.recv_sem.at[at], who)

    def arrival(self, by, number, base):
        whose = lax.rem(self.me - by * number + HEADS, HEADS)
        who = {"head": lax.rem(self.me + by + HEADS, HEADS)}
        at = base + number - 1
        part = self.all_parts.at[whose]
        return remote(part, part, self.send_sem.at[at], self.recv_sem.at[at], who)

    def step(self, number):
        for by, hops, base in self.lanes:
            if number <= hops:
                if number > 1:
                    self.arrival(by, number - 1, base).wait_recv()
                self.copy(by, number, base).start()

    def close(self):
        for by, hops, base in self.lanes:
            self.arrival(by, hops, base).wait_recv()
            for number in range(1, hops + 1):
                self.copy(by, number, base).wait_send()


def return_kernel(
    scale, factor, fetch_ref, prompt_ref, length_ref,
    back_ref, stat_ref, pdk_ref, pdv_ref, q_ref, g_ref, k_ref, v_ref,
    final_ref, out_ref, dq_ref, drk_ref, drv_ref, all_k, all_v,
    q, g, k, v, pdk, pdv, dk, dv, stat_in, load_sem, stat_send, stat_recv, *scratch
):
    loads = [
        pltpu.make_async_copy(src, dst, load_sem.at[i])
        for i, (src, dst) in enumerate(
            ((pdk_ref, pdk), (pdv_ref, pdv), (q_ref, q), (g_ref, g), (k_ref, k), (v_ref, v))
        )
    ]
    for load in loads:
        load.start()
    x, y, core = place()
    me = (x * SIDE + y) * 2 + core
    n_dp = 2 * SIDE * SIDE
    head = lax.axis_index("head")
    around = [{"head": lax.rem(head + by, HEADS)} for by in (1, HEADS - 1)]
    greet(everyone() + around)

    own_stat = pltpu.make_async_copy(stat_ref.at[me], stat_in.at[me], load_sem.at[6])
    own_stat.start()
    stats = []
    for i in range(1, n_dp):
        peer = lax.rem(me + i, n_dp)
        copy = remote(stat_ref.at[peer], stat_in.at[me], stat_send.at[i], stat_recv.at[i], {"dp": peer})
        copy.start()
        stats.append(copy)

    n = 3 + 15
    routes = []
    for half in range(2):
        part = scratch[half * n : (half + 1) * n]
        routes.append(Route(half, back_ref.at[half], final_ref.at[half], part[0], part[1], part[2], part[3:]))
    ring_scratch = scratch[2 * n :]
    bulk = stages(routes)
    bulk[0]()

    prompt_rows = pdk.shape[1] // HEADS
    slot_rows = q.shape[1] // HEADS

    def prompt_part(ref):
        return lambda t: ref[:, pl.ds(pl.multiple_of(t * prompt_rows, prompt_rows), prompt_rows), :]

    def slot_part(ref):
        return lambda t: ref[:, pl.ds(pl.multiple_of(t * slot_rows, slot_rows), slot_rows), :]

    rings = []
    for i, own in enumerate((prompt_part(pdk), prompt_part(pdv), slot_part(dk), slot_part(dv))):
        right, left = (4, 3) if i % 2 == 0 else (3, 4)
        rings.append(Ring(own, right, left, *ring_scratch[4 * i : 4 * i + 4]))
    spreads = [
        Spread(all_k, 4, 3, *ring_scratch[16:18]),
        Spread(all_v, 3, 4, *ring_scratch[18:20]),
    ]

    loads[0].wait()
    loads[1].wait()
    for ring in rings[:2]:
        ring.step(1)
    for load in loads[2:]:
        load.wait()
    bulk[1]()
    for ring in rings[:2]:
        ring.step(2)
    own_stat.wait()
    for copy in stats:
        copy.wait_recv()
    bulk[2]()

    def local_slot(slot):
        live = prompt_ref[slot] >= 0
        lse, delta = unpack_rows(stat_in[fetch_ref[slot] // 2, lax.rem(fetch_ref[slot], 2)])
        lse = jnp.where(live, lse, 1e30)
        delta = jnp.where(live, delta, 0.0)
        query = q[slot]
        grad = live_rows(g[slot], length_ref[slot])
        scores = dot(k[slot], query, NT) * scale
        mask = causal(scores.shape)
        prob = jnp.where(mask, jnp.exp2(jnp.where(mask, scores, -1e30) - lse), 0.0)
        grad_prob = dot(v[slot], grad, NT)
        dscore = (prob * (grad_prob - delta)).astype(BF16)
        prob = prob.astype(BF16)
        dk[slot] = dot(dscore, query, NN) * factor
        dv[slot] = dot(prob, grad, NN)
        out_ref[slot] = dot(prob, v[slot], TN).astype(BF16)
        dq_ref[slot] = (dot(dscore, k[slot], TN) * factor).astype(BF16)

    count = q.shape[0]
    per = 5
    pieces = 4

    def local_piece(piece):
        def go(i, carry):
            for j in range(per):
                local_slot((piece * (count // per // pieces) + i) * per + j)
            return carry

        lax.fori_loop(0, count // per // pieces, go, 0)

    local_piece(0)
    for ring in rings[:2]:
        ring.step(3)
    local_piece(1)
    for ring in rings[:2]:
        ring.step(4)
    bulk[3]()
    local_piece(2)
    all_k[head] = rings[0].result().astype(BF16)
    all_v[head] = rings[1].result().astype(BF16)
    for spread in spreads:
        spread.step(1)
    local_piece(3)
    for ring in rings[2:]:
        ring.step(1)
    bulk[4]()
    for spread in spreads:
        spread.step(2)
    for ring in rings[2:]:
        ring.step(2)
    for spread in spreads:
        spread.step(3)
    bulk[5]()
    for ring in rings[2:]:
        ring.step(3)
    for spread in spreads:
        spread.step(4)
    for ring in rings[2:]:
        ring.step(4)
    drk_ref[...] = rings[2].result()
    drv_ref[...] = rings[3].result()
    for spread in spreads:
        spread.close()
    bulk[6]()
    bulk[7]()
    for ring in rings:
        ring.close()
    for copy in stats:
        copy.wait_send()


def give_back(fetch, prompts, lengths, back, stats, pdk, pdv, queries, grads, keys, values, scale, factor):
    count, rows, dim = queries.shape
    held, length, _ = pdk.shape
    height = back.shape[-2]
    n_dp = 2 * SIDE * SIDE
    V, D = pltpu.VMEM, pltpu.SemaphoreType.DMA
    resp = (count, rows, dim)
    scratch = [V(resp, BF16)] * 4 + [V(pdk.shape, F32)] * 2 + [V(resp, F32)] * 2
    scratch += [V((n_dp, 2, STAT, dim), BF16), D((7,)), D((n_dp,)), D((n_dp,))]
    for _ in range(2):
        scratch += route_scratch(height, dim, BF16) + route_sems()
    for shape in ((held, length // HEADS, dim),) * 2 + ((count, rows // HEADS, dim),) * 2:
        scratch += [V((7,) + shape, BF16), V((7,) + shape, BF16), D((7,)), D((7,))]
    scratch += [D((7,))] * 4
    smem = pl.BlockSpec(memory_space=pltpu.SMEM)
    anywhere = pl.BlockSpec(memory_space=pl.ANY)
    vmem = pl.BlockSpec(memory_space=pltpu.VMEM)
    part = jax.ShapeDtypeStruct((count, rows // HEADS, dim), F32)
    parts = jax.ShapeDtypeStruct((HEADS, held, length // HEADS, dim), BF16)
    return pl.pallas_call(
        functools.partial(return_kernel, scale, factor),
        out_shape=(
            jax.ShapeDtypeStruct(back.shape, BF16),
            jax.ShapeDtypeStruct(resp, BF16),
            jax.ShapeDtypeStruct(resp, BF16),
            part,
            part,
            parts,
            parts,
        ),
        in_specs=[smem] * 3 + [anywhere] * 8,
        out_specs=(anywhere, vmem, vmem, vmem, vmem, vmem, vmem),
        scratch_shapes=scratch,
        compiler_params=pltpu.CompilerParams(collective_id=2, has_side_effects=True),
    )(fetch, prompts, lengths, back, stats, pdk, pdv, queries, grads, keys, values)


def merge_kernel(per_step, fetch_ref, prompt_ref, length_ref, *refs):
    back_refs = refs[:per_step]
    out_part, dq_part, out_ref, dq_ref = refs[per_step:]
    rows = out_part.shape[1]
    step = pl.program_id(0)
    for j in range(per_step):
        slot = step * per_step + j
        live = prompt_ref[slot] >= 0
        row = lax.broadcasted_iota(jnp.int32, out_part.shape[1:], 0)
        back = back_refs[j]
        out = back[0, 0:rows, :].astype(F32) + out_part[j].astype(F32)
        dq = back[0, rows : 2 * rows, :].astype(F32) + dq_part[j].astype(F32)
        length = jnp.where(live, length_ref[slot], 0)
        out_ref[j] = jnp.where(row < length, out, 0.0).astype(BF16)
        dq_ref[j] = jnp.where(row < length, dq, 0.0).astype(BF16)


def merge(fetch, prompts, lengths, back, out_part, dq_part):
    count, rows, dim = out_part.shape
    per_step = 8
    some = pl.BlockSpec((per_step, rows, dim), lambda i, a, b, c: (i, 0, 0))

    def one(j):
        return pl.BlockSpec((1, 2 * rows, dim), lambda i, a, b, c: (a[i * per_step + j], 0, 0))

    return pl.pallas_call(
        functools.partial(merge_kernel, per_step),
        out_shape=(jax.ShapeDtypeStruct((count, rows, dim), BF16),) * 2,
        grid_spec=pltpu.PrefetchScalarGridSpec(
            num_scalar_prefetch=3,
            grid=(count // per_step,),
            in_specs=[one(j) for j in range(per_step)] + [some, some],
            out_specs=(some, some),
        ),
    )(fetch, prompts, lengths, *([back] * per_step), out_part, dq_part)


def body(queries, resp_keys, resp_values, prompt_keys, prompt_values, grad_out, slot_prompt, slot_length):
    slot_count, rows, dim = queries.shape
    held, length, _ = prompt_keys.shape
    factor = dim ** (-0.5)
    scale = factor * LOG2E
    n_dp = 2 * SIDE * SIDE
    items = 2 * n_dp
    x, y, core = place()
    ids = jnp.arange(slot_count, dtype=jnp.int32)
    at = jnp.arange(items, dtype=jnp.int32)
    own = jnp.where(slot_prompt >= 0, slot_prompt // held, -1)
    before = ids[None, :] < ids[:, None]
    order = jnp.sum((own[:, None] == own[None, :]) & before, axis=1, dtype=jnp.int32)
    hx, hy, hc = own // (2 * SIDE), own // 2 % SIDE, own % 2
    first, second = jnp.where(order == 0, hx, hy), jnp.where(order == 0, hy, hx)
    here_first, here_second = jnp.where(order == 0, x, y), jnp.where(order == 0, y, x)
    live = own >= 0
    target = jnp.where(live, ((order * SIDE + first) * SIDE + second) * 2 + hc, -1)
    near_first, near_second = (first - here_first + SIDE) % SIDE, (second - here_second + SIDE) % SIDE
    fetch = jnp.where(live, ((order * SIDE + near_first) * SIDE + near_second) * 2 + hc, 0)
    stat_fetch = jnp.where(live, own * 2 + order, 0)
    hit = target[None, :] == at[:, None]
    send_slot = jnp.sum(jnp.where(hit, ids[None, :], 0), axis=1, dtype=jnp.int32)
    send_prompt = jnp.sum(jnp.where(hit, (slot_prompt % held)[None, :] + 1, 0), axis=1, dtype=jnp.int32) - 1
    half, r_first, r_second, from_core = at // n_dp, at // (2 * SIDE) % SIDE, at // 2 % SIDE, at % 2
    from_first = (jnp.where(half == 0, x, y) + r_first) % SIDE
    from_second = (jnp.where(half == 0, y, x) + r_second) % SIDE
    back_to = ((half * SIDE + from_first) * SIDE + from_second) * 2 + from_core
    from_x, from_y = jnp.where(half == 0, from_first, from_second), jnp.where(half == 0, from_second, from_first)
    stat_to = ((from_x * SIDE + from_y) * 2 + from_core) * 2 + half

    packed = pack(send_slot, send_prompt, slot_length, queries, grad_out, resp_keys, resp_values, scale)
    grid = (2, SIDE, SIDE, 2)
    received = torus_exchange(packed.reshape(grid + packed.shape[1:]), 1).reshape(packed.shape)
    item_prompt = received[:, 2 * rows + 4, 0].astype(jnp.int32)
    order_in = jnp.sum((item_prompt[:, None] == item_prompt[None, :]) & (at[None, :] < at[:, None]), axis=1, dtype=jnp.int32)
    spot = jnp.where(item_prompt >= 0, item_prompt * FANOUT + order_in, -1)
    group_hit = spot[None, :] == jnp.arange(held * FANOUT, dtype=jnp.int32)[:, None]
    group_item = jnp.sum(jnp.where(group_hit, at[None, :], 0), axis=1, dtype=jnp.int32)

    result, stats, pdk, pdv = holder(
        group_item, back_to, stat_to, received, prompt_keys, prompt_values, scale, factor
    )
    back, local_out, local_dq, drk, drv, all_k, all_v = give_back(
        stat_fetch, slot_prompt, slot_length, result.reshape(grid + result.shape[1:]),
        stats.reshape((n_dp, 2) + stats.shape[1:]), pdk, pdv, queries, grad_out, resp_keys, resp_values, scale, factor,
    )
    attn_out, grad_queries = merge(fetch, slot_prompt, slot_length, back.reshape(result.shape), local_out, local_dq)

    def joined(parts):
        return jnp.swapaxes(parts, 0, 1).reshape(held, length, dim).astype(F32)

    return (attn_out, grad_queries, drk, drv, joined(all_k), joined(all_v))


def solution(mesh):
    return jax.shard_map(
        body,
        mesh=mesh,
        in_specs=(
            P("dp", None, "head"),
            P("dp", None, None),
            P("dp", None, None),
            P("dp", None, None),
            P("dp", None, None),
            P("dp", None, "head"),
            P("dp"),
            P("dp"),
        ),
        out_specs=(
            P("dp", None, "head"),
            P("dp", None, "head"),
            P("dp", "head", None),
            P("dp", "head", None),
            P("dp", None, None),
            P("dp", None, None),
        ),
        check_vma=False,
    )
```

```python
import functools
import math

import jax
import jax.numpy as jnp
from jax import lax
from jax.experimental import pallas as pl
from jax.experimental.pallas import tpu as pltpu
from jax.sharding import PartitionSpec as P

FANOUT = 8
LOG2E = math.log2(math.e)
F32 = jnp.float32
BF16 = jnp.bfloat16
STAT = 16


MESH = pl.DeviceIdType.MESH
SIDE = 4

def place():
    me = lax.axis_index("dp")
    core = lax.rem(me, 2)
    y = lax.rem(me // 2, SIDE)
    x = me // (2 * SIDE)
    return x, y, core

def device(k, a, b, core):
    x, y = (a, b) if k == 0 else (b, a)
    return {"dp": (x * SIDE + y) * 2 + core}

def step_by(value, by):
    return lax.rem(value + by + SIDE, SIDE)

def everyone():
    x, y, core = place()
    me = (x * SIDE + y) * 2 + core
    return [{"dp": lax.rem(me + k, 2 * SIDE * SIDE)} for k in range(1, 2 * SIDE * SIDE)]


def greet_start(near):
    barrier = pltpu.get_barrier_semaphore()
    for who in near:
        pl.semaphore_signal(barrier, inc=1, device_id=who, device_id_type=MESH)


def greet_end(near):
    pl.semaphore_wait(pltpu.get_barrier_semaphore(), len(near))

def remote(src, dst, send, recv, who):
    return pltpu.make_async_remote_copy(src_ref=src, dst_ref=dst, send_sem=send, recv_sem=recv, device_id=who, device_id_type=MESH)

class Route:
    def __init__(self, k, send, final, mid, rel1, rel2, sems):
        self.k, self.send, self.final, self.mid, self.rel1, self.rel2 = k, send, final, mid, rel1, rel2
        x, y, self.c = place()
        self.a, self.b = (x, y) if k == 0 else (y, x)
        (self.s1, self.r1, self.s1d, self.r1d, self.s1f, self.r1f,
         self.s2, self.r2, self.s2d, self.r2d, self.s2f, self.r2f, self.s0, self.r0, self.local) = sems
    def to_a(self, by): return device(self.k, step_by(self.a, by), self.b, self.c)
    def to_b(self, by, c): return device(self.k, self.a, step_by(self.b, by), c)
    def first_direct(self, side, j):
        by = 1 if side == 0 else -1
        b = step_by(self.b, j)
        r = 3 if side == 0 else 1
        return remote(self.send.at[step_by(self.a, by), b], self.mid.at[r - 1, b], self.s1.at[side, j], self.r1.at[side, j], self.to_a(by))
    def first_far(self, side, j):
        by = 1 if side == 0 else -1
        b = 2 * side + j
        return remote(self.send.at[step_by(self.a, 2), b], self.rel1.at[side, j], self.s1d.at[side, j], self.r1d.at[side, j], self.to_a(by))
    def first_forward(self, side, j):
        by = 1 if side == 0 else -1
        b = 2 * side + j
        return remote(self.rel1.at[side, j], self.mid.at[1, b], self.s1f.at[side, j], self.r1f.at[side, j], self.to_a(by))
    def source(self, r, b):
        return self.send.at[self.a, b] if r == 0 else self.mid.at[r - 1, b]
    def second_direct(self, r, side, c):
        by = 1 if side == 0 else -1
        rb = 3 if side == 0 else 1
        return remote(self.source(r, step_by(self.b, by)).at[c], self.final.at[r, rb, self.c], self.s2.at[r, side, c], self.r2.at[r, side, self.c], self.to_b(by, c))
    def second_far(self, r):
        side = r // 2
        by = 1 if side == 0 else -1
        return remote(self.source(r, step_by(self.b, 2)), self.rel2.at[side, r % 2], self.s2d.at[r], self.r2d.at[r], self.to_b(by, self.c))
    def second_forward(self, r, c):
        side = r // 2
        by = 1 if side == 0 else -1
        return remote(self.rel2.at[side, r % 2, c], self.final.at[r, 2, self.c], self.s2f.at[r, c], self.r2f.at[r, self.c], self.to_b(by, c))
    def cross(self, r):
        return remote(self.source(r, self.b).at[1 - self.c], self.final.at[r, 0, self.c], self.s0.at[r], self.r0.at[r], self.to_b(0, 1 - self.c))
    def own(self, r):
        return pltpu.make_async_copy(self.source(r, self.b).at[self.c], self.final.at[r, 0, self.c], self.local.at[r])

def wait_second_direct(route, r, side):
    for c in range(2):
        by = 1 if side == 0 else -1
        rb = 3 if side == 0 else 1
        d = route.final.at[r, rb, c]
        remote(d, d, route.s2.at[r, side, c], route.r2.at[r, side, c], route.to_b(by, c)).wait_recv()

def wait_second_forward(route, r):
    side = r // 2
    by = 1 if side == 0 else -1
    for c in range(2):
        d = route.final.at[r, 2, c]
        remote(d, d, route.s2f.at[r, c], route.r2f.at[r, c], route.to_b(by, c)).wait_recv()

def wait_cross(route, r):
    d = route.final.at[r, 0, 1 - route.c]
    remote(d, d, route.s0.at[r], route.r0.at[r], route.to_b(0, 1 - route.c)).wait_recv()

def route_sems():
    D = pltpu.SemaphoreType.DMA
    return [D((2, 4)), D((2, 4)), D((2, 2)), D((2, 2)), D((2, 2)), D((2, 2)),
            D((4, 2, 2)), D((4, 2, 2)), D((4,)), D((4,)), D((4, 2)), D((4, 2)), D((4,)), D((4,)), D((4,))]

def route_scratch(height, dim, dtype):
    V = pltpu.VMEM
    return [V((3, 4, 2, height, dim), dtype), V((2, 2, 2, height, dim), dtype), V((2, 2, 2, height, dim), dtype)]

def stages(routes):
    started = []

    def go(copy):
        copy.start()
        started.append(copy)

    def second_near(route, r, side):
        for c in range(2):
            go(route.second_direct(r, side, c))

    def second_here(route, r):
        go(route.cross(r))
        go(route.own(r))

    def relay(route, r):
        route.second_far(r).wait_recv()
        for c in range(2):
            go(route.second_forward(r, c))

    def begin():
        for j in range(2):
            for side in range(2):
                for route in routes:
                    go(route.first_far(side, j))
        for route in routes:
            go(route.second_far(0))
            for side in range(2):
                second_near(route, 0, side)
        for side in range(2):
            for route in routes:
                go(route.first_direct(side, 2))
        for route in routes:
            second_here(route, 0)

    def forward():
        for j in range(2):
            for side in range(2):
                for route in routes:
                    route.first_far(side, j).wait_recv()
                    go(route.first_forward(side, j))
        for j in (1, 3, 0):
            for side in range(2):
                for route in routes:
                    go(route.first_direct(side, j))

    def relay_own():
        for route in routes:
            relay(route, 0)

    def turn_far():
        for side in range(2):
            for route in routes:
                route.first_direct(side, 2).wait_recv()
                go(route.second_far(3 if side == 0 else 1))

    def turn_forwarded():
        for route in routes:
            for side in range(2):
                for j in range(2):
                    route.first_forward(side, j).wait_recv()
            go(route.second_far(2))
            for side in range(2):
                second_near(route, 2, side)
            second_here(route, 2)

    def turn_near():
        for j, way in ((1, 0), (3, 1)):
            for side in range(2):
                for route in routes:
                    route.first_direct(side, j).wait_recv()
                    second_near(route, 3 if side == 0 else 1, way)
        for side in range(2):
            for route in routes:
                route.first_direct(side, 0).wait_recv()
                second_here(route, 3 if side == 0 else 1)

    def relay_rest():
        for r in (3, 1, 2):
            for route in routes:
                relay(route, r)

    def arrive():
        for r in (0, 3, 1, 2):
            for route in routes:
                for side in range(2):
                    wait_second_direct(route, r, side)
                wait_second_forward(route, r)
                wait_cross(route, r)
                route.own(r).wait()

    def close():
        for copy in started:
            if copy.is_remote:
                copy.wait_send()

    return [begin, forward, relay_own, turn_far, turn_forwarded, turn_near, relay_rest, arrive, close]


def dot(a, b, dims):
    return lax.dot_general(a, b, (dims, ((), ())), preferred_element_type=F32)


NT = ((1,), (1,))
NN = ((1,), (0,))
TN = ((0,), (0,))


def two_parts(value):
    high = value.astype(BF16)
    low = (value - high.astype(F32)).astype(BF16)
    return high.astype(F32), low.astype(F32)


def pack_rows(first, second, third=0.0):
    width = first.shape[1]
    rows = lax.broadcasted_iota(jnp.int32, (STAT, width), 0)
    a, b = two_parts(first)
    c, d = two_parts(second)
    packed = jnp.where(rows == 0, a, jnp.where(rows == 1, b, jnp.where(rows == 2, c, d)))
    return jnp.where(rows < 4, packed, third).astype(BF16)


def unpack_rows(packed):
    rows = packed.astype(F32)
    return rows[0:1] + rows[1:2], rows[2:3] + rows[3:4]


def live_rows(grad, length):
    row = lax.broadcasted_iota(jnp.int32, grad.shape, 0)
    return jnp.where(row < length, grad, jnp.zeros_like(grad))


def causal(shape):
    return lax.broadcasted_iota(jnp.int32, shape, 0) <= lax.broadcasted_iota(jnp.int32, shape, 1)


def swap_stats(stat_send, stat_in, own_sem, send_sem, recv_sem):
    x, y, core = place()
    me = (x * SIDE + y) * 2 + core
    n_dp = 2 * SIDE * SIDE
    own = pltpu.make_async_copy(stat_send.at[me], stat_in.at[me], own_sem)
    own.start()
    copies = []
    for i in range(1, n_dp):
        peer = lax.rem(me + i, n_dp)
        copy = remote(stat_send.at[peer], stat_in.at[me], send_sem.at[i], recv_sem.at[i], {"dp": peer})
        copy.start()
        copies.append(copy)
    return own, copies


def forward_slots(slots, scale, q, g, k, v):
    query = [q[s] for s in slots]
    grad = [g[s] for s in slots]
    key = [k[s] for s in slots]
    value = [v[s] for s in slots]
    scores = [dot(a, b, NT) * scale for a, b in zip(key, query)]
    grad_prob = [dot(a, b, NT) for a, b in zip(value, grad)]
    mask = causal(scores[0].shape)
    scores = [jnp.where(mask, a, -1e30) for a in scores]
    top = [jnp.max(a, axis=0, keepdims=True) for a in scores]
    exps = [jnp.exp2(a - b) for a, b in zip(scores, top)]
    total = [jnp.sum(a, axis=0, keepdims=True) for a in exps]
    row_sum = [jnp.sum(a * b, axis=0, keepdims=True) / c for a, b, c in zip(exps, grad_prob, total)]
    return [(a + jnp.log2(b), c) for a, b, c in zip(top, total, row_sum)]


def send_kernel(
    scale, slot_ref, stat_slot_ref, prompt_ref, length_ref, q_ref, g_ref, k_ref, v_ref, final_ref, stat_in,
    q, g, k, v, packed, stat, stat_send, load_sem, stat_s, stat_r, *scratch
):
    loads = [
        pltpu.make_async_copy(src, dst, load_sem.at[i])
        for i, (src, dst) in enumerate(((q_ref, q), (g_ref, g), (k_ref, k), (v_ref, v)))
    ]
    for load in loads:
        load.start()
    count, rows, _ = q.shape
    n_dp = 2 * SIDE * SIDE
    per = 5
    greet_start(everyone())
    loads[0].wait()
    loads[1].wait()

    def mask_rows(i, carry):
        for j in range(per):
            slot = i * per + j
            g[slot] = live_rows(g[slot], length_ref[slot])
        return carry

    lax.fori_loop(0, count // per, mask_rows, 0)

    def fill(i, carry):
        for half in range(2):
            for c in range(2):
                slot = slot_ref[half * n_dp + i * 2 + c]
                at = (half, i // SIDE, lax.rem(i, SIDE), c)
                packed[at + (slice(0, rows), slice(None))] = q[slot]
                packed[at + (slice(rows, 2 * rows), slice(None))] = g[slot]
        return carry

    lax.fori_loop(0, SIDE * SIDE, fill, 0)
    greet_end(everyone())
    n = 3 + 15
    routes = []
    for half in range(2):
        part = scratch[half * n : (half + 1) * n]
        routes.append(Route(half, packed.at[half], final_ref.at[half], part[0], part[1], part[2], part[3:]))
    bulk = stages(routes)
    bulk[0]()
    loads[2].wait()
    loads[3].wait()

    def forward(i, carry):
        slots = [i * per + j for j in range(per)]
        for slot, (lse, row_sum) in zip(slots, forward_slots(slots, scale, q, g, k, v)):
            stat[slot] = pack_rows(lse, row_sum, prompt_ref[slot].astype(F32))
        return carry

    steps = count // per
    lax.fori_loop(0, steps // 2, forward, 0)
    bulk[1]()
    lax.fori_loop(steps // 2, steps, forward, 0)

    def fill_stats(i, carry):
        for half in range(2):
            slot = stat_slot_ref[i * 2 + half]
            row = lax.broadcasted_iota(jnp.int32, stat.shape[1:], 0)
            block = stat[jnp.maximum(slot, 0)].astype(F32)
            stat_send[i, half] = jnp.where((row >= 4) & (slot < 0), -1.0, block).astype(BF16)
        return carry

    lax.fori_loop(0, n_dp, fill_stats, 0)
    bulk[2]()
    own, copies = swap_stats(stat_send, stat_in, load_sem.at[4], stat_s, stat_r)
    for stage in bulk[3:8]:
        stage()
    own.wait()
    for copy in copies:
        copy.wait_recv()
    bulk[8]()
    for copy in copies:
        copy.wait_send()


def send_out(slots, stat_slots, prompts, lengths, queries, grads, keys, values, scale):
    count, rows, dim = queries.shape
    n_dp = 2 * SIDE * SIDE
    V, D = pltpu.VMEM, pltpu.SemaphoreType.DMA
    resp = (count, rows, dim)
    shape = (2, SIDE, SIDE, 2, 2 * rows, dim)
    scratch = [V(resp, BF16)] * 4 + [V(shape, BF16), V((count, STAT, dim), BF16), V((n_dp, 2, STAT, dim), BF16)]
    scratch += [D((5,)), D((n_dp,)), D((n_dp,))]
    for _ in range(2):
        scratch += route_scratch(2 * rows, dim, BF16) + route_sems()
    smem = pl.BlockSpec(memory_space=pltpu.SMEM)
    anywhere = pl.BlockSpec(memory_space=pl.ANY)
    return pl.pallas_call(
        functools.partial(send_kernel, scale),
        out_shape=(jax.ShapeDtypeStruct(shape, BF16), jax.ShapeDtypeStruct((n_dp, 2, STAT, dim), BF16)),
        in_specs=[smem] * 4 + [anywhere] * 4,
        out_specs=(anywhere, anywhere),
        scratch_shapes=scratch,
        compiler_params=pltpu.CompilerParams(collective_id=1, has_side_effects=True),
    )(slots, stat_slots, prompts, lengths, queries, grads, keys, values)


def holder_kernel(
    scale, factor, item_ref, stat_at_ref, back_ref, a_ref, b_ref, sa_ref, sb_ref, k_ref, v_ref,
    out_ref, stat_ref, dk_ref, dv_ref, kt, vt, out_buf, stat_buf, out_sem, stat_sem,
):
    prompt, step = pl.program_id(0), pl.program_id(1)
    count = pl.num_programs(1)
    index = prompt * count + step

    @pl.when(step == 0)
    def _():
        kt[...] = jnp.transpose(k_ref[0])
        vt[...] = jnp.transpose(v_ref[0])
        dk_ref[...] = jnp.zeros_like(dk_ref)
        dv_ref[...] = jnp.zeros_like(dv_ref)

    def leaving(at, j):
        slot = lax.rem(at, 2)
        item = stat_at_ref[2 * at + j]
        return (
            pltpu.make_async_copy(out_buf.at[slot, j], out_ref.at[back_ref[item]], out_sem.at[slot, j]),
            pltpu.make_async_copy(stat_buf.at[slot, j], stat_ref.at[item], stat_sem.at[slot, j]),
        )

    rows = a_ref.shape[1] // 2
    query = jnp.concatenate([a_ref[0, 0:rows, :], b_ref[0, 0:rows, :]], axis=0)
    grad = jnp.concatenate([a_ref[0, rows : 2 * rows, :], b_ref[0, rows : 2 * rows, :]], axis=0)
    lse_a, sum_a = unpack_rows(sa_ref[0])
    lse_b, sum_b = unpack_rows(sb_ref[0])
    resp_lse = jnp.concatenate([lse_a, lse_b], axis=1)
    resp_sum = jnp.concatenate([sum_a, sum_b], axis=1)
    scores = dot(k_ref[0], query, NT) * scale
    grad_prob = dot(v_ref[0], grad, NT)
    top = jnp.max(scores, axis=0, keepdims=True)
    exps = jnp.exp2(scores - top)
    total = jnp.sum(exps, axis=0, keepdims=True)
    row_sum = jnp.sum(exps * grad_prob, axis=0, keepdims=True)
    prefix_lse = top + jnp.log2(total)
    high = jnp.maximum(prefix_lse, resp_lse)
    lse = high + jnp.log2(jnp.exp2(prefix_lse - high) + jnp.exp2(resp_lse - high))
    weight = jnp.exp2(prefix_lse - lse) / total
    delta = weight * row_sum + jnp.exp2(resp_lse - lse) * resp_sum
    prob = exps * weight
    dscore = (prob * (grad_prob - delta)).astype(BF16)
    prob = prob.astype(BF16)
    dk_ref[0] += dot(dscore, query, NN) * factor
    dv_ref[0] += dot(prob, grad, NN)
    out = jnp.transpose(dot(vt[...], prob, NN)).astype(BF16)
    dq = jnp.transpose(dot(kt[...], dscore, NN) * factor).astype(BF16)

    @pl.when(index >= 2)
    def _():
        for j in range(2):
            for copy in leaving(index - 2, j):
                copy.wait()

    slot = lax.rem(index, 2)
    for j in range(2):
        part = slice(j * rows, (j + 1) * rows)
        out_buf[slot, j, 0:rows, :] = out[part]
        out_buf[slot, j, rows:, :] = dq[part]
        stat_buf[slot, j] = pack_rows(lse[:, part], delta[:, part])
        for copy in leaving(index, j):
            copy.start()

    @pl.when(index == pl.num_programs(0) * count - 1)
    def _():
        for at in (index - 1, index):
            for j in range(2):
                for copy in leaving(at, j):
                    copy.wait()


def holder(items, stat_at, back_to, received, stats, keys, values, scale, factor):
    count, height, dim = received.shape
    held, length, _ = keys.shape
    rows = height // 2
    steps = FANOUT // 2

    def one(k):
        return pl.BlockSpec((1, height, dim), lambda p, j, ids, b, c: (ids[p * FANOUT + 2 * j + k], 0, 0))

    def stat(k):
        return pl.BlockSpec((1, STAT, dim), lambda p, j, ids, b, c: (b[p * FANOUT + 2 * j + k], 0, 0))

    whole = pl.BlockSpec((1, length, dim), lambda p, j, ids, b, c: (p, 0, 0))
    return pl.pallas_call(
        functools.partial(holder_kernel, scale, factor),
        out_shape=(
            jax.ShapeDtypeStruct((count, 2 * rows, dim), BF16),
            jax.ShapeDtypeStruct((count, STAT, dim), BF16),
            jax.ShapeDtypeStruct((held, length, dim), F32),
            jax.ShapeDtypeStruct((held, length, dim), F32),
        ),
        grid_spec=pltpu.PrefetchScalarGridSpec(
            num_scalar_prefetch=3,
            grid=(held, steps),
            in_specs=[one(0), one(1), stat(0), stat(1), whole, whole],
            out_specs=(
                pl.BlockSpec(memory_space=pl.ANY),
                pl.BlockSpec(memory_space=pl.ANY),
                whole,
                whole,
            ),
            scratch_shapes=[
                pltpu.VMEM((dim, length), BF16),
                pltpu.VMEM((dim, length), BF16),
                pltpu.VMEM((2, 2, 2 * rows, dim), BF16),
                pltpu.VMEM((2, 2, STAT, dim), BF16),
                pltpu.SemaphoreType.DMA((2, 2)),
                pltpu.SemaphoreType.DMA((2, 2)),
            ],
        ),
    )(items, stat_at, back_to, received, received, stats, stats, keys, values)


HEADS = 8


class Ring:
    def __init__(self, own, right, left, sent, came, send_sem, recv_sem):
        self.own, self.sent, self.came, self.send_sem, self.recv_sem = own, sent, came, send_sem, recv_sem
        self.me = lax.axis_index("head")
        self.lanes = ((1, right, 0), (-1, left, right))

    def copy(self, by, at):
        who = {"head": lax.rem(self.me + by + HEADS, HEADS)}
        return remote(self.sent.at[at], self.came.at[at], self.send_sem.at[at], self.recv_sem.at[at], who)

    def step(self, number):
        for by, hops, base in self.lanes:
            if number <= hops:
                target = lax.rem(self.me + by * (hops + 1 - number) + HEADS, HEADS)
                value = self.own(target)
                at = base + number - 1
                if number > 1:
                    self.copy(by, at - 1).wait_recv()
                    value = value + self.came[at - 1].astype(F32)
                self.sent[at] = value.astype(BF16)
                self.copy(by, at).start()

    def result(self):
        value = self.own(self.me)
        for by, hops, base in self.lanes:
            at = base + hops - 1
            self.copy(by, at).wait_recv()
            value = value + self.came[at].astype(F32)
        return value

    def close(self):
        for by, hops, base in self.lanes:
            for at in range(base, base + hops):
                self.copy(by, at).wait_send()


class Spread:
    def __init__(self, all_parts, right, left, send_sem, recv_sem):
        self.all_parts, self.send_sem, self.recv_sem = all_parts, send_sem, recv_sem
        self.me = lax.axis_index("head")
        self.lanes = ((1, right, 0), (-1, left, right))

    def copy(self, by, number, base):
        whose = lax.rem(self.me - by * (number - 1) + HEADS, HEADS)
        who = {"head": lax.rem(self.me + by + HEADS, HEADS)}
        at = base + number - 1
        part = self.all_parts.at[whose]
        return remote(part, part, self.send_sem.at[at], self.recv_sem.at[at], who)

    def arrival(self, by, number, base):
        whose = lax.rem(self.me - by * number + HEADS, HEADS)
        who = {"head": lax.rem(self.me + by + HEADS, HEADS)}
        at = base + number - 1
        part = self.all_parts.at[whose]
        return remote(part, part, self.send_sem.at[at], self.recv_sem.at[at], who)

    def step(self, number):
        for by, hops, base in self.lanes:
            if number <= hops:
                if number > 1:
                    self.arrival(by, number - 1, base).wait_recv()
                self.copy(by, number, base).start()

    def close(self):
        for by, hops, base in self.lanes:
            self.arrival(by, hops, base).wait_recv()
            for number in range(1, hops + 1):
                self.copy(by, number, base).wait_send()


def local_slots(slots, scale, factor, fetch_ref, prompt_ref, length_ref, stat_in, q, g, k, v, dk, dv, out, dq):
    query = [q[s] for s in slots]
    grad = [live_rows(g[s], length_ref[s]) for s in slots]
    key = [k[s] for s in slots]
    value = [v[s] for s in slots]
    stats = [unpack_rows(stat_in[fetch_ref[s] // 2, lax.rem(fetch_ref[s], 2)]) for s in slots]
    lse = [jnp.where(prompt_ref[s] >= 0, a, 1e30) for s, (a, _) in zip(slots, stats)]
    delta = [jnp.where(prompt_ref[s] >= 0, a, 0.0) for s, (_, a) in zip(slots, stats)]
    scores = [dot(a, b, NT) * scale for a, b in zip(key, query)]
    grad_prob = [dot(a, b, NT) for a, b in zip(value, grad)]
    mask = causal(scores[0].shape)
    prob = [jnp.exp2(jnp.where(mask, a - b, -1e30)) for a, b in zip(scores, lse)]
    dscore = [(a * (b - c)).astype(BF16) for a, b, c in zip(prob, grad_prob, delta)]
    prob = [a.astype(BF16) for a in prob]
    part_k = [dot(a, b, NN) * factor for a, b in zip(dscore, query)]
    part_v = [dot(a, b, NN) for a, b in zip(prob, grad)]
    part_out = [dot(a, b, TN).astype(BF16) for a, b in zip(prob, value)]
    part_dq = [(dot(a, b, TN) * factor).astype(BF16) for a, b in zip(dscore, key)]
    for s, a, b, c, d in zip(slots, part_k, part_v, part_out, part_dq):
        dk[s], dv[s], out[s], dq[s] = a, b, c, d


def return_kernel(
    scale, factor, fetch_ref, stat_fetch_ref, prompt_ref, length_ref,
    back_ref, stat_ref, pdk_ref, pdv_ref, q_ref, g_ref, k_ref, v_ref,
    out_ref, dq_ref, drk_ref, drv_ref, all_k, all_v,
    q, g, k, v, pdk, pdv, dk, dv, out, dq, final, stat_in, load_sem, stat_s, stat_r, *scratch
):
    loads = [
        pltpu.make_async_copy(src, dst, load_sem.at[i])
        for i, (src, dst) in enumerate(
            ((pdk_ref, pdk), (pdv_ref, pdv), (q_ref, q), (g_ref, g), (k_ref, k), (v_ref, v))
        )
    ]
    for load in loads:
        load.start()
    head = lax.axis_index("head")
    near = everyone() + [{"head": lax.rem(head + by, HEADS)} for by in (1, HEADS - 1)]
    greet_start(near)
    greet_end(near)
    own_stat, stats = swap_stats(stat_ref, stat_in, load_sem.at[6], stat_s, stat_r)

    n = 3 + 15
    routes = []
    for half in range(2):
        part = scratch[half * n : (half + 1) * n]
        routes.append(Route(half, back_ref.at[half], final.at[half], part[0], part[1], part[2], part[3:]))
    ring_scratch = scratch[2 * n :]
    bulk = stages(routes)
    bulk[0]()

    count = q.shape[0]
    prompt_rows = pdk.shape[1] // HEADS
    slot_rows = q.shape[1] // HEADS

    def prompt_part(ref):
        return lambda t: ref[:, pl.ds(pl.multiple_of(t * prompt_rows, prompt_rows), prompt_rows), :]

    def slot_part(ref, group):
        some = slice(group * (count // GROUPS), (group + 1) * (count // GROUPS))
        return lambda t: ref[some, pl.ds(pl.multiple_of(t * slot_rows, slot_rows), slot_rows), :]

    owns = [prompt_part(pdk), prompt_part(pdv)]
    for group in range(GROUPS):
        owns += [slot_part(dk, group), slot_part(dv, group)]
    rings = []
    for i, own in enumerate(owns):
        right, left = (4, 3) if i % 2 == 0 else (3, 4)
        rings.append(Ring(own, right, left, *ring_scratch[4 * i : 4 * i + 4]))
    last = 4 * len(owns)
    spreads = [
        Spread(all_k, 4, 3, *ring_scratch[last : last + 2]),
        Spread(all_v, 3, 4, *ring_scratch[last + 2 : last + 4]),
    ]

    def ring(which, number):
        for one in rings[2 * which : 2 * which + 2]:
            one.step(number)

    def spread(number):
        for one in spreads:
            one.step(number)

    per = 5

    def local(group):
        steps = count // per // GROUPS

        def go(i, carry):
            slots = [(group * steps + i) * per + j for j in range(per)]
            local_slots(
                slots, scale, factor, stat_fetch_ref, prompt_ref, length_ref, stat_in, q, g, k, v, dk, dv, out, dq
            )
            return carry

        lax.fori_loop(0, steps, go, 0)

    loads[0].wait()
    loads[1].wait()
    ring(0, 1)
    for load in loads[2:]:
        load.wait()
    own_stat.wait()
    for copy in stats:
        copy.wait_recv()
    local(0)
    ring(1, 1)
    bulk[1]()
    ring(0, 2)
    local(1)
    ring(2, 1)
    bulk[2]()
    ring(1, 2)
    ring(0, 3)
    bulk[3]()
    ring(2, 2)
    ring(0, 4)
    bulk[4]()
    ring(1, 3)
    all_k[head] = rings[0].result().astype(BF16)
    all_v[head] = rings[1].result().astype(BF16)
    spread(1)
    ring(2, 3)
    bulk[5]()
    spread(2)
    ring(1, 4)
    spread(3)
    ring(2, 4)
    bulk[6]()
    spread(4)
    half_count = count // GROUPS
    for group in range(GROUPS):
        some = slice(group * half_count, (group + 1) * half_count)
        drk_ref[some] = rings[2 + 2 * group].result()
        drv_ref[some] = rings[3 + 2 * group].result()
    for one in spreads:
        one.close()
    bulk[7]()

    rows = q.shape[1]
    n_dp = 2 * SIDE * SIDE

    def merge(i, carry):
        for j in range(per):
            slot = i * per + j
            at = fetch_ref[slot]
            back = final[at // n_dp, lax.rem(at // (2 * SIDE), SIDE), lax.rem(at // 2, SIDE), lax.rem(at, 2)]
            row = lax.broadcasted_iota(jnp.int32, (rows, back.shape[1]), 0)
            live = row < jnp.where(prompt_ref[slot] >= 0, length_ref[slot], 0)
            both = back.astype(F32)
            out_ref[slot] = jnp.where(live, both[0:rows] + out[slot].astype(F32), 0.0).astype(BF16)
            dq_ref[slot] = jnp.where(live, both[rows:] + dq[slot].astype(F32), 0.0).astype(BF16)
        return carry

    lax.fori_loop(0, count // per, merge, 0)
    bulk[8]()
    for one in rings:
        one.close()
    for copy in stats:
        copy.wait_send()


GROUPS = 2


def give_back(fetch, stat_fetch, prompts, lengths, back, stats, pdk, pdv, queries, grads, keys, values, scale, factor):
    count, rows, dim = queries.shape
    held, length, _ = pdk.shape
    height = back.shape[-2]
    n_dp = 2 * SIDE * SIDE
    V, D = pltpu.VMEM, pltpu.SemaphoreType.DMA
    resp = (count, rows, dim)
    scratch = [V(resp, BF16)] * 4 + [V(pdk.shape, F32)] * 2 + [V(resp, F32)] * 2 + [V(resp, BF16)] * 2
    scratch += [V(back.shape, BF16)]
    scratch += [V((n_dp, 2, STAT, dim), BF16), D((7,)), D((n_dp,)), D((n_dp,))]
    for _ in range(2):
        scratch += route_scratch(height, dim, BF16) + route_sems()
    for shape in ((held, length // HEADS, dim),) * 2 + ((count // GROUPS, rows // HEADS, dim),) * (2 * GROUPS):
        scratch += [V((7,) + shape, BF16), V((7,) + shape, BF16), D((7,)), D((7,))]
    scratch += [D((7,))] * 4
    smem = pl.BlockSpec(memory_space=pltpu.SMEM)
    anywhere = pl.BlockSpec(memory_space=pl.ANY)
    vmem = pl.BlockSpec(memory_space=pltpu.VMEM)
    part = jax.ShapeDtypeStruct((count, rows // HEADS, dim), F32)
    parts = jax.ShapeDtypeStruct((HEADS, held, length // HEADS, dim), BF16)
    return pl.pallas_call(
        functools.partial(return_kernel, scale, factor),
        out_shape=(
            jax.ShapeDtypeStruct(resp, BF16),
            jax.ShapeDtypeStruct(resp, BF16),
            part,
            part,
            parts,
            parts,
        ),
        in_specs=[smem] * 4 + [anywhere] * 8,
        out_specs=(vmem, vmem, vmem, vmem, vmem, vmem),
        scratch_shapes=scratch,
        compiler_params=pltpu.CompilerParams(collective_id=2, has_side_effects=True),
    )(fetch, stat_fetch, prompts, lengths, back, stats, pdk, pdv, queries, grads, keys, values)


def body(queries, resp_keys, resp_values, prompt_keys, prompt_values, grad_out, slot_prompt, slot_length):
    slot_count, rows, dim = queries.shape
    held, length, _ = prompt_keys.shape
    factor = dim ** (-0.5)
    scale = factor * LOG2E
    n_dp = 2 * SIDE * SIDE
    items = 2 * n_dp
    x, y, core = place()
    ids = jnp.arange(slot_count, dtype=jnp.int32)
    at = jnp.arange(items, dtype=jnp.int32)
    own = jnp.where(slot_prompt >= 0, slot_prompt // held, -1)
    before = ids[None, :] < ids[:, None]
    order = jnp.sum((own[:, None] == own[None, :]) & before, axis=1, dtype=jnp.int32)
    hx, hy, hc = own // (2 * SIDE), own // 2 % SIDE, own % 2
    first, second = jnp.where(order == 0, hx, hy), jnp.where(order == 0, hy, hx)
    here_first, here_second = jnp.where(order == 0, x, y), jnp.where(order == 0, y, x)
    live = own >= 0
    target = jnp.where(live, ((order * SIDE + first) * SIDE + second) * 2 + hc, -1)
    near_first, near_second = (first - here_first + SIDE) % SIDE, (second - here_second + SIDE) % SIDE
    fetch = jnp.where(live, ((order * SIDE + near_first) * SIDE + near_second) * 2 + hc, 0)
    stat_fetch = jnp.where(live, own * 2 + order, 0)
    hit = target[None, :] == at[:, None]
    send_slot = jnp.sum(jnp.where(hit, ids[None, :], 0), axis=1, dtype=jnp.int32)
    stat_hit = jnp.where(live, stat_fetch, -1)[None, :] == at[:, None]
    stat_slot = jnp.sum(jnp.where(stat_hit, ids[None, :] + 1, 0), axis=1, dtype=jnp.int32) - 1
    half, from_core = at % 2, at // 2 % 2
    from_x, from_y = at // (4 * SIDE), at // 4 % SIDE
    back_to, received_at = [], []
    for dx, dy, to in ((0, 0, back_to), (x, y, received_at)):
        ax, ay = (from_x - dx + SIDE) % SIDE, (from_y - dy + SIDE) % SIDE
        first, second = jnp.where(half == 0, ax, ay), jnp.where(half == 0, ay, ax)
        to.append(((half * SIDE + first) * SIDE + second) * 2 + from_core)

    received, stats_in = send_out(
        send_slot, stat_slot, slot_prompt % held, slot_length, queries, grad_out, resp_keys, resp_values, scale
    )
    received = received.reshape((items,) + received.shape[4:])
    stats_in = stats_in.reshape((items,) + stats_in.shape[2:])
    item_prompt = stats_in[:, 4, 0].astype(jnp.int32)
    order_in = jnp.sum((item_prompt[:, None] == item_prompt[None, :]) & (at[None, :] < at[:, None]), axis=1, dtype=jnp.int32)
    spot = jnp.where(item_prompt >= 0, item_prompt * FANOUT + order_in, -1)
    group_hit = spot[None, :] == jnp.arange(held * FANOUT, dtype=jnp.int32)[:, None]
    group_stat = jnp.sum(jnp.where(group_hit, at[None, :], 0), axis=1, dtype=jnp.int32)
    group_item = jnp.sum(jnp.where(group_hit, received_at[0][None, :], 0), axis=1, dtype=jnp.int32)

    result, stats, pdk, pdv = holder(
        group_item, group_stat, back_to[0], received, stats_in, prompt_keys, prompt_values, scale, factor
    )
    grid = (2, SIDE, SIDE, 2)
    attn_out, grad_queries, drk, drv, all_k, all_v = give_back(
        fetch, stat_fetch, slot_prompt, slot_length, result.reshape(grid + result.shape[1:]),
        stats.reshape((n_dp, 2) + stats.shape[1:]), pdk, pdv, queries, grad_out, resp_keys, resp_values, scale, factor,
    )

    def joined(parts):
        return jnp.swapaxes(parts, 0, 1).reshape(held, length, dim).astype(F32)

    return (attn_out, grad_queries, drk, drv, joined(all_k), joined(all_v))


def solution(mesh):
    return jax.shard_map(
        body,
        mesh=mesh,
        in_specs=(
            P("dp", None, "head"),
            P("dp", None, None),
            P("dp", None, None),
            P("dp", None, None),
            P("dp", None, None),
            P("dp", None, "head"),
            P("dp"),
            P("dp"),
        ),
        out_specs=(
            P("dp", None, "head"),
            P("dp", None, "head"),
            P("dp", "head", None),
            P("dp", "head", None),
            P("dp", None, None),
            P("dp", None, None),
        ),
        check_vma=False,
    )
```

```python
import functools
import math

import jax
import jax.numpy as jnp
from jax import lax
from jax.experimental import pallas as pl
from jax.experimental.pallas import tpu as pltpu
from jax.sharding import PartitionSpec as P

FANOUT = 8
LOG2E = math.log2(math.e)
F32 = jnp.float32
BF16 = jnp.bfloat16
STAT = 16


MESH = pl.DeviceIdType.MESH
SIDE = 4

def place():
    me = lax.axis_index("dp")
    core = lax.rem(me, 2)
    y = lax.rem(me // 2, SIDE)
    x = me // (2 * SIDE)
    return x, y, core

def device(k, a, b, core):
    x, y = (a, b) if k == 0 else (b, a)
    return {"dp": (x * SIDE + y) * 2 + core}

def step_by(value, by):
    return lax.rem(value + by + SIDE, SIDE)

def everyone():
    x, y, core = place()
    me = (x * SIDE + y) * 2 + core
    return [{"dp": lax.rem(me + k, 2 * SIDE * SIDE)} for k in range(1, 2 * SIDE * SIDE)]


def greet_start(near):
    barrier = pltpu.get_barrier_semaphore()
    for who in near:
        pl.semaphore_signal(barrier, inc=1, device_id=who, device_id_type=MESH)


def greet_end(near):
    pl.semaphore_wait(pltpu.get_barrier_semaphore(), len(near))

def remote(src, dst, send, recv, who):
    return pltpu.make_async_remote_copy(src_ref=src, dst_ref=dst, send_sem=send, recv_sem=recv, device_id=who, device_id_type=MESH)

class Route:
    def __init__(self, k, send, final, mid, rel1, rel2, sems):
        self.k, self.send, self.final, self.mid, self.rel1, self.rel2 = k, send, final, mid, rel1, rel2
        x, y, self.c = place()
        self.a, self.b = (x, y) if k == 0 else (y, x)
        (self.s1, self.r1, self.s1d, self.r1d, self.s1f, self.r1f,
         self.s2, self.r2, self.s2d, self.r2d, self.s2f, self.r2f, self.s0, self.r0, self.local) = sems
    def to_a(self, by): return device(self.k, step_by(self.a, by), self.b, self.c)
    def to_b(self, by, c): return device(self.k, self.a, step_by(self.b, by), c)
    def first_direct(self, side, j):
        by = 1 if side == 0 else -1
        b = step_by(self.b, j)
        r = 3 if side == 0 else 1
        return remote(self.send.at[step_by(self.a, by), b], self.mid.at[r - 1, b], self.s1.at[side, j], self.r1.at[side, j], self.to_a(by))
    def first_far(self, side, j):
        by = 1 if side == 0 else -1
        b = 2 * side + j
        return remote(self.send.at[step_by(self.a, 2), b], self.rel1.at[side, j], self.s1d.at[side, j], self.r1d.at[side, j], self.to_a(by))
    def first_forward(self, side, j):
        by = 1 if side == 0 else -1
        b = 2 * side + j
        return remote(self.rel1.at[side, j], self.mid.at[1, b], self.s1f.at[side, j], self.r1f.at[side, j], self.to_a(by))
    def source(self, r, b):
        return self.send.at[self.a, b] if r == 0 else self.mid.at[r - 1, b]
    def second_direct(self, r, side, c):
        by = 1 if side == 0 else -1
        rb = 3 if side == 0 else 1
        return remote(self.source(r, step_by(self.b, by)).at[c], self.final.at[r, rb, self.c], self.s2.at[r, side, c], self.r2.at[r, side, self.c], self.to_b(by, c))
    def second_far(self, r):
        side = r // 2
        by = 1 if side == 0 else -1
        return remote(self.source(r, step_by(self.b, 2)), self.rel2.at[side, r % 2], self.s2d.at[r], self.r2d.at[r], self.to_b(by, self.c))
    def second_forward(self, r, c):
        side = r // 2
        by = 1 if side == 0 else -1
        return remote(self.rel2.at[side, r % 2, c], self.final.at[r, 2, self.c], self.s2f.at[r, c], self.r2f.at[r, self.c], self.to_b(by, c))
    def cross(self, r):
        return remote(self.source(r, self.b).at[1 - self.c], self.final.at[r, 0, self.c], self.s0.at[r], self.r0.at[r], self.to_b(0, 1 - self.c))
    def own(self, r):
        return pltpu.make_async_copy(self.source(r, self.b).at[self.c], self.final.at[r, 0, self.c], self.local.at[r])

def wait_second_direct(route, r, side):
    for c in range(2):
        by = 1 if side == 0 else -1
        rb = 3 if side == 0 else 1
        d = route.final.at[r, rb, c]
        remote(d, d, route.s2.at[r, side, c], route.r2.at[r, side, c], route.to_b(by, c)).wait_recv()

def wait_second_forward(route, r):
    side = r // 2
    by = 1 if side == 0 else -1
    for c in range(2):
        d = route.final.at[r, 2, c]
        remote(d, d, route.s2f.at[r, c], route.r2f.at[r, c], route.to_b(by, c)).wait_recv()

def wait_cross(route, r):
    d = route.final.at[r, 0, 1 - route.c]
    remote(d, d, route.s0.at[r], route.r0.at[r], route.to_b(0, 1 - route.c)).wait_recv()

def route_sems():
    D = pltpu.SemaphoreType.DMA
    return [D((2, 4)), D((2, 4)), D((2, 2)), D((2, 2)), D((2, 2)), D((2, 2)),
            D((4, 2, 2)), D((4, 2, 2)), D((4,)), D((4,)), D((4, 2)), D((4, 2)), D((4,)), D((4,)), D((4,))]

def route_scratch(height, dim, dtype):
    V = pltpu.VMEM
    return [V((3, 4, 2, height, dim), dtype), V((2, 2, 2, height, dim), dtype), V((2, 2, 2, height, dim), dtype)]

def stages(routes):
    started = []

    def go(copy):
        copy.start()
        started.append(copy)

    def second_near(route, r, side):
        for c in range(2):
            go(route.second_direct(r, side, c))

    def second_here(route, r):
        go(route.cross(r))
        go(route.own(r))

    def relay(route, r):
        route.second_far(r).wait_recv()
        for c in range(2):
            go(route.second_forward(r, c))

    def begin():
        for j in range(2):
            for side in range(2):
                for route in routes:
                    go(route.first_far(side, j))
        for route in routes:
            go(route.second_far(0))
            for side in range(2):
                second_near(route, 0, side)
        for side in range(2):
            for route in routes:
                go(route.first_direct(side, 2))
        for route in routes:
            second_here(route, 0)

    def forward():
        for j in range(2):
            for side in range(2):
                for route in routes:
                    route.first_far(side, j).wait_recv()
                    go(route.first_forward(side, j))
        for j in (1, 3, 0):
            for side in range(2):
                for route in routes:
                    go(route.first_direct(side, j))

    def relay_own():
        for route in routes:
            relay(route, 0)

    def turn_far():
        for side in range(2):
            for route in routes:
                route.first_direct(side, 2).wait_recv()
                go(route.second_far(3 if side == 0 else 1))

    def turn_forwarded():
        for route in routes:
            for side in range(2):
                for j in range(2):
                    route.first_forward(side, j).wait_recv()
            go(route.second_far(2))
            for side in range(2):
                second_near(route, 2, side)
            second_here(route, 2)

    def turn_near():
        for j, way in ((1, 0), (3, 1)):
            for side in range(2):
                for route in routes:
                    route.first_direct(side, j).wait_recv()
                    second_near(route, 3 if side == 0 else 1, way)
        for side in range(2):
            for route in routes:
                route.first_direct(side, 0).wait_recv()
                second_here(route, 3 if side == 0 else 1)

    def relay_rest():
        for r in (3, 1, 2):
            for route in routes:
                relay(route, r)

    def arrive():
        for r in (0, 3, 1, 2):
            for route in routes:
                for side in range(2):
                    wait_second_direct(route, r, side)
                wait_second_forward(route, r)
                wait_cross(route, r)
                route.own(r).wait()

    def close():
        for copy in started:
            if copy.is_remote:
                copy.wait_send()

    return [begin, forward, relay_own, turn_far, turn_forwarded, turn_near, relay_rest, arrive, close]


def dot(a, b, dims):
    return lax.dot_general(a, b, (dims, ((), ())), preferred_element_type=F32)


NT = ((1,), (1,))
NN = ((1,), (0,))
TN = ((0,), (0,))


def two_parts(value):
    high = value.astype(BF16)
    low = (value - high.astype(F32)).astype(BF16)
    return high.astype(F32), low.astype(F32)


def pack_rows(first, second, third=0.0):
    width = first.shape[1]
    rows = lax.broadcasted_iota(jnp.int32, (STAT, width), 0)
    a, b = two_parts(first)
    c, d = two_parts(second)
    packed = jnp.where(rows == 0, a, jnp.where(rows == 1, b, jnp.where(rows == 2, c, d)))
    return jnp.where(rows < 4, packed, third).astype(BF16)


def unpack_rows(packed):
    rows = packed.astype(F32)
    return rows[0:1] + rows[1:2], rows[2:3] + rows[3:4]


def live_rows(grad, length):
    row = lax.broadcasted_iota(jnp.int32, grad.shape, 0)
    return jnp.where(row < length, grad, jnp.zeros_like(grad))


def causal(shape):
    return lax.broadcasted_iota(jnp.int32, shape, 0) <= lax.broadcasted_iota(jnp.int32, shape, 1)


def swap_stats(stat_send, stat_in, own_sem, send_sem, recv_sem):
    x, y, core = place()
    me = (x * SIDE + y) * 2 + core
    n_dp = 2 * SIDE * SIDE
    own = pltpu.make_async_copy(stat_send.at[me], stat_in.at[me], own_sem)
    own.start()
    copies = []
    for i in range(1, n_dp):
        peer = lax.rem(me + i, n_dp)
        copy = remote(stat_send.at[peer], stat_in.at[me], send_sem.at[i], recv_sem.at[i], {"dp": peer})
        copy.start()
        copies.append(copy)
    return own, copies


def forward_slots(slots, scale, q, g, k, v):
    query = [q[s] for s in slots]
    grad = [g[s] for s in slots]
    key = [k[s] for s in slots]
    value = [v[s] for s in slots]
    scores = [dot(a, b, NT) * scale for a, b in zip(key, query)]
    grad_prob = [dot(a, b, NT) for a, b in zip(value, grad)]
    mask = causal(scores[0].shape)
    scores = [jnp.where(mask, a, -1e30) for a in scores]
    top = [jnp.max(a, axis=0, keepdims=True) for a in scores]
    exps = [jnp.exp2(a - b) for a, b in zip(scores, top)]
    total = [jnp.sum(a, axis=0, keepdims=True) for a in exps]
    row_sum = [jnp.sum(a * b, axis=0, keepdims=True) / c for a, b, c in zip(exps, grad_prob, total)]
    return [(a + jnp.log2(b), c) for a, b, c in zip(top, total, row_sum)]


def send_kernel(
    scale, held, table_ref, prompt_ref, length_ref, q_ref, g_ref, k_ref, v_ref, final_ref, stat_in, group_ref,
    q, g, k, v, packed, stat, stat_send, ids, load_sem, stat_s, stat_r, *scratch
):
    loads = [
        pltpu.make_async_copy(src, dst, load_sem.at[i])
        for i, (src, dst) in enumerate(((q_ref, q), (g_ref, g), (k_ref, k), (v_ref, v)))
    ]
    for load in loads:
        load.start()
    count, rows, _ = q.shape
    n_dp = 2 * SIDE * SIDE
    per = 5
    greet_start(everyone())
    loads[0].wait()
    loads[1].wait()

    def fill(i, carry):
        for half in range(2):
            for c in range(2):
                slot = table_ref[2, half * n_dp + i * 2 + c]
                at = (half, i // SIDE, lax.rem(i, SIDE), c)
                packed[at + (slice(0, rows), slice(None))] = q[slot]
                packed[at + (slice(rows, 2 * rows), slice(None))] = live_rows(g[slot], length_ref[slot])
        return carry

    lax.fori_loop(0, SIDE * SIDE, fill, 0)
    greet_end(everyone())
    n = 3 + 15
    routes = []
    for half in range(2):
        part = scratch[half * n : (half + 1) * n]
        routes.append(Route(half, packed.at[half], final_ref.at[half], part[0], part[1], part[2], part[3:]))
    bulk = stages(routes)
    bulk[0]()
    loads[2].wait()
    loads[3].wait()

    def forward(i, carry):
        slots = [i * per + j for j in range(per)]
        for slot, (lse, row_sum) in zip(slots, forward_slots(slots, scale, q, g, k, v)):
            lane = lax.broadcasted_iota(jnp.int32, row_sum.shape, 1)
            row_sum = jnp.where(lane < length_ref[slot], row_sum, 0.0)
            stat[slot] = pack_rows(lse, row_sum, jnp.bitwise_and(prompt_ref[slot], held - 1).astype(F32))
        return carry

    steps = count // per
    lax.fori_loop(0, steps // 2, forward, 0)
    bulk[1]()
    lax.fori_loop(steps // 2, steps, forward, 0)

    def fill_stats(i, carry):
        for half in range(2):
            slot = table_ref[3, i * 2 + half]
            row = lax.broadcasted_iota(jnp.int32, stat.shape[1:], 0)
            block = stat[jnp.maximum(slot, 0)].astype(F32)
            stat_send[i, half] = jnp.where((row >= 4) & (slot < 0), -1.0, block).astype(BF16)
        return carry

    lax.fori_loop(0, n_dp, fill_stats, 0)
    bulk[2]()
    own, copies = swap_stats(stat_send, stat_in, load_sem.at[4], stat_s, stat_r)
    for stage in bulk[3:8]:
        stage()
    own.wait()
    for copy in copies:
        copy.wait_recv()
    x, y, _ = place()

    def name(i, carry):
        for half in range(2):
            ids[pl.ds(2 * i + half, 1), :] = stat_in[i, half].astype(F32)[4:5]
        return carry

    lax.fori_loop(0, n_dp, name, 0)
    items = 2 * n_dp
    column = ids[...]
    item = lax.broadcasted_iota(jnp.int32, column.shape, 0)
    lane = lax.broadcasted_iota(jnp.int32, column.shape, 1)
    row = jnp.sum(jnp.where(item == lane, column, 0.0), axis=0, keepdims=True)
    earlier = jnp.where((column == row) & (lane < item), 1.0, 0.0)
    order = jnp.sum(earlier, axis=1, keepdims=True)
    spot = jnp.where(column >= 0.0, column * FANOUT + order, -1.0)
    hit = spot == lane.astype(F32)
    half, core = jnp.bitwise_and(item, 1), jnp.bitwise_and(jnp.right_shift(item, 1), 1)
    ax = jnp.bitwise_and(jnp.right_shift(item, 4) - x + SIDE, SIDE - 1)
    ay = jnp.bitwise_and(jnp.bitwise_and(jnp.right_shift(item, 2), SIDE - 1) - y + SIDE, SIDE - 1)
    first, second = jnp.where(half == 0, ax, ay), jnp.where(half == 0, ay, ax)
    where = ((half * SIDE + first) * SIDE + second) * 2 + core
    group_ref[0:1] = jnp.sum(jnp.where(hit, item, 0), axis=0, keepdims=True)
    group_ref[1:2] = jnp.sum(jnp.where(hit, where, 0), axis=0, keepdims=True)
    group_ref[2:] = jnp.zeros((6, group_ref.shape[1]), jnp.int32)
    bulk[8]()
    for copy in copies:
        copy.wait_send()


def send_out(held, table, prompts, lengths, queries, grads, keys, values, scale):
    count, rows, dim = queries.shape
    n_dp = 2 * SIDE * SIDE
    V, D = pltpu.VMEM, pltpu.SemaphoreType.DMA
    resp = (count, rows, dim)
    shape = (2, SIDE, SIDE, 2, 2 * rows, dim)
    scratch = [V(resp, BF16)] * 4 + [V(shape, BF16), V((count, STAT, dim), BF16), V((n_dp, 2, STAT, dim), BF16)]
    scratch += [V((2 * n_dp, 128), F32)]
    scratch += [D((5,)), D((n_dp,)), D((n_dp,))]
    for _ in range(2):
        scratch += route_scratch(2 * rows, dim, BF16) + route_sems()
    smem = pl.BlockSpec(memory_space=pltpu.SMEM)
    anywhere = pl.BlockSpec(memory_space=pl.ANY)
    return pl.pallas_call(
        functools.partial(send_kernel, scale, held),
        out_shape=(
            jax.ShapeDtypeStruct(shape, BF16),
            jax.ShapeDtypeStruct((n_dp, 2, STAT, dim), BF16),
            jax.ShapeDtypeStruct((8, 128), jnp.int32),
        ),
        in_specs=[smem] * 3 + [anywhere] * 4,
        out_specs=(anywhere, pl.BlockSpec(memory_space=pltpu.VMEM), pl.BlockSpec(memory_space=pltpu.VMEM)),
        scratch_shapes=scratch,
        compiler_params=pltpu.CompilerParams(collective_id=1, has_side_effects=True),
    )(table, prompts, lengths, queries, grads, keys, values)


PAIRS = 4
WIDE = 2 * PAIRS


def holder_kernel(scale, factor, group_ref, table_ref, *refs):
    slot_refs, stat_refs = refs[:WIDE], refs[WIDE : 2 * WIDE]
    k_ref, v_ref, out_ref, stat_ref, dk_ref, dv_ref, kt, vt, out_buf, stat_buf, out_sem, stat_sem = refs[2 * WIDE :]
    prompt, step = pl.program_id(0), pl.program_id(1)
    count = pl.num_programs(1)
    index = prompt * count + step

    @pl.when(step == 0)
    def _():
        kt[...] = jnp.transpose(k_ref[0])
        vt[...] = jnp.transpose(v_ref[0])
        dk_ref[...] = jnp.zeros_like(dk_ref)
        dv_ref[...] = jnp.zeros_like(dv_ref)

    def leaving(at, j):
        slot = lax.rem(at, 2)
        item = group_ref[0, WIDE * at + j]
        return (
            pltpu.make_async_copy(out_buf.at[slot, j], out_ref.at[table_ref[4, item]], out_sem.at[slot, j]),
            pltpu.make_async_copy(stat_buf.at[slot, j], stat_ref.at[item], stat_sem.at[slot, j]),
        )

    @pl.when(index >= 2)
    def _():
        for j in range(WIDE):
            for copy in leaving(index - 2, j):
                copy.wait()

    rows = slot_refs[0].shape[1] // 2
    pairs = [(2 * i, 2 * i + 1) for i in range(PAIRS)]

    def both(part):
        return [jnp.concatenate([slot_refs[i][0, part, :], slot_refs[j][0, part, :]], axis=0) for i, j in pairs]

    query, grad = both(slice(0, rows)), both(slice(rows, 2 * rows))
    own = [unpack_rows(ref[0]) for ref in stat_refs]
    resp_lse = [jnp.concatenate([own[i][0], own[j][0]], axis=1) for i, j in pairs]
    resp_sum = [jnp.concatenate([own[i][1], own[j][1]], axis=1) for i, j in pairs]
    slot = lax.rem(index, 2)
    chunk = 128
    parts = [slice(c, c + chunk) for c in range(0, k_ref.shape[1], chunk)]

    def products(n):
        return dot(k_ref[0], query[n], NT), dot(v_ref[0], grad[n], NT)

    def weights(n, scores, grad_prob):
        tops, exps, totals, sums = [], [], [], []
        for part in parts:
            some = scores[part] * scale
            tops.append(jnp.max(some, axis=0, keepdims=True))
            exps.append(jnp.exp2(some - tops[-1]))
            totals.append(jnp.sum(exps[-1], axis=0, keepdims=True))
            sums.append(jnp.sum(exps[-1] * grad_prob[part], axis=0, keepdims=True))
        top = functools.reduce(jnp.maximum, tops)
        shares = [jnp.exp2(a - top) for a in tops]
        total = sum(a * b for a, b in zip(shares, totals))
        row_sum = sum(a * b for a, b in zip(shares, sums))
        prefix_lse = top + jnp.log2(total)
        high = jnp.maximum(prefix_lse, resp_lse[n])
        lse = high + jnp.log2(jnp.exp2(prefix_lse - high) + jnp.exp2(resp_lse[n] - high))
        weight = jnp.exp2(prefix_lse - lse) / total
        delta = weight * row_sum + jnp.exp2(resp_lse[n] - lse) * resp_sum[n]
        probs = [a * (weight * b) for a, b in zip(exps, shares)]
        dscore = [(a * (grad_prob[part] - delta)).astype(BF16) for a, part in zip(probs, parts)]
        for m, at in enumerate(pairs[n]):
            part = slice(m * rows, (m + 1) * rows)
            stat_buf[slot, at] = pack_rows(lse[:, part], delta[:, part])
        return jnp.concatenate([a.astype(BF16) for a in probs], axis=0), jnp.concatenate(dscore, axis=0)

    def close(n, prob, dscore):
        dk_ref[0] += dot(dscore, query[n], NN)
        dv_ref[0] += dot(prob, grad[n], NN)
        out = jnp.transpose(dot(vt[...], prob, NN)).astype(BF16)
        dq = jnp.transpose(dot(kt[...], dscore, NN) * factor).astype(BF16)
        for m, at in enumerate(pairs[n]):
            part = slice(m * rows, (m + 1) * rows)
            out_buf[slot, at, 0:rows, :] = out[part]
            out_buf[slot, at, rows:, :] = dq[part]

    after = products(0)
    for n in range(PAIRS):
        now = after
        if n + 1 < PAIRS:
            after = products(n + 1)
        close(n, *weights(n, *now))
    for j in range(WIDE):
        for copy in leaving(index, j):
            copy.start()

    @pl.when(index == pl.num_programs(0) * count - 1)
    def _():
        for at in (index - 1, index):
            for j in range(WIDE):
                for copy in leaving(at, j):
                    copy.wait()


def holder(groups, table, received, stats, keys, values, scale, factor):
    count, height, dim = received.shape
    held, length, _ = keys.shape
    rows = height // 2
    steps = FANOUT // WIDE

    def one(k):
        return pl.BlockSpec((1, height, dim), lambda p, j, ids, b: (ids[1, p * FANOUT + WIDE * j + k], 0, 0))

    def stat(k):
        return pl.BlockSpec((1, STAT, dim), lambda p, j, ids, b: (ids[0, p * FANOUT + WIDE * j + k], 0, 0))

    whole = pl.BlockSpec((1, length, dim), lambda p, j, ids, b: (p, 0, 0))
    return pl.pallas_call(
        functools.partial(holder_kernel, scale, factor),
        out_shape=(
            jax.ShapeDtypeStruct((count, 2 * rows, dim), BF16),
            jax.ShapeDtypeStruct((count, STAT, dim), BF16),
            jax.ShapeDtypeStruct((held, length, dim), F32),
            jax.ShapeDtypeStruct((held, length, dim), F32),
        ),
        grid_spec=pltpu.PrefetchScalarGridSpec(
            num_scalar_prefetch=2,
            grid=(held, steps),
            in_specs=[one(k) for k in range(WIDE)] + [stat(k) for k in range(WIDE)] + [whole, whole],
            out_specs=(
                pl.BlockSpec(memory_space=pl.ANY),
                pl.BlockSpec(memory_space=pl.ANY),
                whole,
                whole,
            ),
            scratch_shapes=[
                pltpu.VMEM((dim, length), BF16),
                pltpu.VMEM((dim, length), BF16),
                pltpu.VMEM((2, WIDE, 2 * rows, dim), BF16),
                pltpu.VMEM((2, WIDE, STAT, dim), BF16),
                pltpu.SemaphoreType.DMA((2, WIDE)),
                pltpu.SemaphoreType.DMA((2, WIDE)),
            ],
        ),
    )(groups, table, *([received] * WIDE), *([stats] * WIDE), keys, values)


HEADS = 8


class Ring:
    def __init__(self, own, right, left, sent, came, send_sem, recv_sem):
        self.own, self.sent, self.came, self.send_sem, self.recv_sem = own, sent, came, send_sem, recv_sem
        self.me = lax.axis_index("head")
        self.lanes = ((1, right, 0), (-1, left, right))

    def copy(self, by, at):
        who = {"head": lax.rem(self.me + by + HEADS, HEADS)}
        return remote(self.sent.at[at], self.came.at[at], self.send_sem.at[at], self.recv_sem.at[at], who)

    def step(self, number):
        for by, hops, base in self.lanes:
            if number <= hops:
                target = lax.rem(self.me + by * (hops + 1 - number) + HEADS, HEADS)
                value = self.own(target)
                at = base + number - 1
                if number > 1:
                    self.copy(by, at - 1).wait_recv()
                    value = value + self.came[at - 1].astype(F32)
                self.sent[at] = value.astype(BF16)
                self.copy(by, at).start()

    def result(self):
        value = self.own(self.me)
        for by, hops, base in self.lanes:
            at = base + hops - 1
            self.copy(by, at).wait_recv()
            value = value + self.came[at].astype(F32)
        return value

    def close(self):
        for by, hops, base in self.lanes:
            for at in range(base, base + hops):
                self.copy(by, at).wait_send()


class Spread:
    def __init__(self, all_parts, right, left, send_sem, recv_sem):
        self.all_parts, self.send_sem, self.recv_sem = all_parts, send_sem, recv_sem
        self.me = lax.axis_index("head")
        self.lanes = ((1, right, 0), (-1, left, right))

    def copy(self, by, number, base):
        whose = lax.rem(self.me - by * (number - 1) + HEADS, HEADS)
        who = {"head": lax.rem(self.me + by + HEADS, HEADS)}
        at = base + number - 1
        part = self.all_parts.at[whose]
        return remote(part, part, self.send_sem.at[at], self.recv_sem.at[at], who)

    def arrival(self, by, number, base):
        whose = lax.rem(self.me - by * number + HEADS, HEADS)
        who = {"head": lax.rem(self.me + by + HEADS, HEADS)}
        at = base + number - 1
        part = self.all_parts.at[whose]
        return remote(part, part, self.send_sem.at[at], self.recv_sem.at[at], who)

    def step(self, number):
        for by, hops, base in self.lanes:
            if number <= hops:
                if number > 1:
                    self.arrival(by, number - 1, base).wait_recv()
                self.copy(by, number, base).start()

    def close(self):
        for by, hops, base in self.lanes:
            self.arrival(by, hops, base).wait_recv()
            for number in range(1, hops + 1):
                self.copy(by, number, base).wait_send()


def local_slots(slots, scale, factor, table_ref, prompt_ref, length_ref, stat_in, q, g, k, v, dk, dv, out, dq):
    query = [q[s] for s in slots]
    grad = [live_rows(g[s], length_ref[s]) for s in slots]
    key = [k[s] for s in slots]
    value = [v[s] for s in slots]
    stats = [unpack_rows(stat_in[table_ref[1, s] // 2, lax.rem(table_ref[1, s], 2)]) for s in slots]
    lse = [jnp.where(prompt_ref[s] >= 0, a, 1e30) for s, (a, _) in zip(slots, stats)]
    delta = [jnp.where(prompt_ref[s] >= 0, a, 0.0) for s, (_, a) in zip(slots, stats)]
    scores = [dot(a, b, NT) * scale for a, b in zip(key, query)]
    grad_prob = [dot(a, b, NT) for a, b in zip(value, grad)]
    mask = causal(scores[0].shape)
    prob = [jnp.exp2(jnp.where(mask, a - b, -1e30)) for a, b in zip(scores, lse)]
    dscore = [(a * (b - c)).astype(BF16) for a, b, c in zip(prob, grad_prob, delta)]
    prob = [a.astype(BF16) for a in prob]
    part_k = [dot(a, b, NN) * factor for a, b in zip(dscore, query)]
    part_v = [dot(a, b, NN) for a, b in zip(prob, grad)]
    part_out = [dot(a, b, TN).astype(BF16) for a, b in zip(prob, value)]
    part_dq = [(dot(a, b, TN) * factor).astype(BF16) for a, b in zip(dscore, key)]
    for s, a, b, c, d in zip(slots, part_k, part_v, part_out, part_dq):
        dk[s], dv[s], out[s], dq[s] = a, b, c, d


def return_kernel(
    scale, factor, table_ref, prompt_ref, length_ref,
    back_ref, stat_ref, pdk_ref, pdv_ref, q_ref, g_ref, k_ref, v_ref,
    final, out_ref, dq_ref, drk_ref, drv_ref, all_k, all_v,
    q, g, k, v, pdk, pdv, dk, dv, out, dq, stat_in, load_sem, stat_s, stat_r, *scratch
):
    loads = [
        pltpu.make_async_copy(src, dst, load_sem.at[i])
        for i, (src, dst) in enumerate(
            ((pdk_ref, pdk), (pdv_ref, pdv), (q_ref, q), (g_ref, g), (k_ref, k), (v_ref, v))
        )
    ]
    for load in loads:
        load.start()
    head = lax.axis_index("head")
    near = everyone() + [{"head": lax.rem(head + by, HEADS)} for by in (1, HEADS - 1)]
    greet_start(near)
    greet_end(near)
    own_stat, stats = swap_stats(stat_ref, stat_in, load_sem.at[6], stat_s, stat_r)

    n = 3 + 15
    routes = []
    for half in range(2):
        part = scratch[half * n : (half + 1) * n]
        routes.append(Route(half, back_ref.at[half], final.at[half], part[0], part[1], part[2], part[3:]))
    ring_scratch = scratch[2 * n :]
    bulk = stages(routes)
    bulk[0]()

    count = q.shape[0]
    prompt_rows = pdk.shape[1] // HEADS
    slot_rows = q.shape[1] // HEADS

    def prompt_part(ref, by):
        return lambda t: ref[:, pl.ds(pl.multiple_of(t * prompt_rows, prompt_rows), prompt_rows), :] * by

    def slot_part(ref, group):
        some = slice(group * (count // GROUPS), (group + 1) * (count // GROUPS))
        return lambda t: ref[some, pl.ds(pl.multiple_of(t * slot_rows, slot_rows), slot_rows), :]

    owns = [prompt_part(pdk, factor), prompt_part(pdv, 1.0)]
    for group in range(GROUPS):
        owns += [slot_part(dk, group), slot_part(dv, group)]
    rings = []
    for i, own in enumerate(owns):
        right, left = (4, 3) if i % 2 == 0 else (3, 4)
        rings.append(Ring(own, right, left, *ring_scratch[4 * i : 4 * i + 4]))
    last = 4 * len(owns)
    spreads = [
        Spread(all_k, 4, 3, *ring_scratch[last : last + 2]),
        Spread(all_v, 3, 4, *ring_scratch[last + 2 : last + 4]),
    ]

    def ring(which, number):
        for one in rings[2 * which : 2 * which + 2]:
            one.step(number)

    def spread(number):
        for one in spreads:
            one.step(number)

    per = 5

    def local(group):
        steps = count // per // GROUPS

        def go(i, carry):
            slots = [(group * steps + i) * per + j for j in range(per)]
            local_slots(
                slots, scale, factor, table_ref, prompt_ref, length_ref, stat_in, q, g, k, v, dk, dv, out, dq
            )
            return carry

        lax.fori_loop(0, steps, go, 0)

    loads[0].wait()
    loads[1].wait()
    ring(0, 1)
    for load in loads[2:]:
        load.wait()
    own_stat.wait()
    for copy in stats:
        copy.wait_recv()
    local(0)
    ring(1, 1)
    bulk[1]()
    ring(0, 2)
    local(1)
    leaving = [
        pltpu.make_async_copy(src, dst, load_sem.at[i]) for i, (src, dst) in enumerate(((out, out_ref), (dq, dq_ref)))
    ]
    for copy in leaving:
        copy.start()
    ring(2, 1)
    bulk[2]()
    ring(1, 2)
    ring(0, 3)
    bulk[3]()
    ring(2, 2)
    ring(0, 4)
    bulk[4]()
    ring(1, 3)
    all_k[head] = rings[0].result().astype(BF16)
    all_v[head] = rings[1].result().astype(BF16)
    spread(1)
    ring(2, 3)
    bulk[5]()
    spread(2)
    ring(1, 4)
    spread(3)
    ring(2, 4)
    bulk[6]()
    spread(4)
    half_count = count // GROUPS
    for group in range(GROUPS):
        some = slice(group * half_count, (group + 1) * half_count)
        drk_ref[some] = rings[2 + 2 * group].result()
        drv_ref[some] = rings[3 + 2 * group].result()
    for one in spreads:
        one.close()
    bulk[7]()

    for copy in leaving:
        copy.wait()
    bulk[8]()
    for one in rings:
        one.close()
    for copy in stats:
        copy.wait_send()


GROUPS = 2


def give_back(table, prompts, lengths, back, stats, pdk, pdv, queries, grads, keys, values, scale, factor):
    count, rows, dim = queries.shape
    held, length, _ = pdk.shape
    height = back.shape[-2]
    n_dp = 2 * SIDE * SIDE
    V, D = pltpu.VMEM, pltpu.SemaphoreType.DMA
    resp = (count, rows, dim)
    scratch = [V(resp, BF16)] * 4 + [V(pdk.shape, F32)] * 2 + [V(resp, F32)] * 2 + [V(resp, BF16)] * 2
    scratch += [V((n_dp, 2, STAT, dim), BF16), D((7,)), D((n_dp,)), D((n_dp,))]
    for _ in range(2):
        scratch += route_scratch(height, dim, BF16) + route_sems()
    for shape in ((held, length // HEADS, dim),) * 2 + ((count // GROUPS, rows // HEADS, dim),) * (2 * GROUPS):
        scratch += [V((7,) + shape, BF16), V((7,) + shape, BF16), D((7,)), D((7,))]
    scratch += [D((7,))] * 4
    smem = pl.BlockSpec(memory_space=pltpu.SMEM)
    anywhere = pl.BlockSpec(memory_space=pl.ANY)
    vmem = pl.BlockSpec(memory_space=pltpu.VMEM)
    part = jax.ShapeDtypeStruct((count, rows // HEADS, dim), F32)
    parts = jax.ShapeDtypeStruct((HEADS, held, length // HEADS, dim), BF16)
    return pl.pallas_call(
        functools.partial(return_kernel, scale, factor),
        out_shape=(
            jax.ShapeDtypeStruct(back.shape, BF16),
            jax.ShapeDtypeStruct(resp, BF16),
            jax.ShapeDtypeStruct(resp, BF16),
            part,
            part,
            parts,
            parts,
        ),
        in_specs=[smem] * 3 + [anywhere] * 8,
        out_specs=(anywhere, anywhere, anywhere, vmem, vmem, vmem, vmem),
        scratch_shapes=scratch,
        compiler_params=pltpu.CompilerParams(collective_id=2, has_side_effects=True),
    )(table, prompts, lengths, back, stats, pdk, pdv, queries, grads, keys, values)


def finish_kernel(per_step, table_ref, prompt_ref, length_ref, *refs):
    back_refs = refs[:per_step]
    out_part, dq_part, drk, drv, pk, pv, out_ref, dq_ref, drk_ref, drv_ref, pk_ref, pv_ref = refs[per_step:]
    rows = out_part.shape[1]
    step = pl.program_id(0)
    for j in range(per_step):
        slot = step * per_step + j
        row = lax.broadcasted_iota(jnp.int32, out_part.shape[1:], 0)
        live = row < jnp.where(prompt_ref[slot] >= 0, length_ref[slot], 0)
        back = back_refs[j]
        out = back[0, 0:rows, :].astype(F32) + out_part[j].astype(F32)
        dq = back[0, rows : 2 * rows, :].astype(F32) + dq_part[j].astype(F32)
        out_ref[j] = jnp.where(live, out, 0.0).astype(BF16)
        dq_ref[j] = jnp.where(live, dq, 0.0).astype(BF16)
    drk_ref[...] = drk[...]
    drv_ref[...] = drv[...]
    pk_ref[...] = pk[0].astype(F32)
    pv_ref[...] = pv[0].astype(F32)


def finish(table, prompts, lengths, back, out_part, dq_part, drk, drv, all_k, all_v):
    count, rows, dim = out_part.shape
    _, held, part, _ = all_k.shape
    per_step = count // HEADS
    some = pl.BlockSpec((per_step, rows, dim), lambda i, a, b, c: (i, 0, 0))
    own = pl.BlockSpec((per_step, rows // HEADS, dim), lambda i, a, b, c: (i, 0, 0))
    piece = pl.BlockSpec((1, held, part, dim), lambda i, a, b, c: (i, 0, 0, 0))
    placed = pl.BlockSpec((held, part, dim), lambda i, a, b, c: (0, i, 0))

    def one(j):
        return pl.BlockSpec((1, 2 * rows, dim), lambda i, a, b, c: (a[0, i * per_step + j], 0, 0))

    return pl.pallas_call(
        functools.partial(finish_kernel, per_step),
        out_shape=(jax.ShapeDtypeStruct((count, rows, dim), BF16),) * 2
        + (jax.ShapeDtypeStruct(drk.shape, F32),) * 2
        + (jax.ShapeDtypeStruct((held, HEADS * part, dim), F32),) * 2,
        grid_spec=pltpu.PrefetchScalarGridSpec(
            num_scalar_prefetch=3,
            grid=(HEADS,),
            in_specs=[one(j) for j in range(per_step)] + [some, some, own, own, piece, piece],
            out_specs=(some, some, own, own, placed, placed),
        ),
    )(table, prompts, lengths, *([back] * per_step), out_part, dq_part, drk, drv, all_k, all_v)


def table_kernel(held, prompt_ref, table_ref):
    x, y, _ = place()
    count = prompt_ref.shape[1]
    prompts = prompt_ref[...]
    own_row = jnp.where(prompts >= 0, jnp.right_shift(prompts, held.bit_length() - 1), -1)
    one = lax.broadcasted_iota(jnp.int32, (count, count), 0)
    two = lax.broadcasted_iota(jnp.int32, (count, count), 1)
    own_column = jnp.sum(jnp.where(one == two, own_row, 0), axis=1, keepdims=True)
    same = own_column == own_row
    order_column = jnp.sum(jnp.where(same & (two < one), 1, 0), axis=1, keepdims=True)
    order_row = jnp.sum(jnp.where(same & (one < two), 1, 0), axis=0, keepdims=True)

    def position(own, order, x_from, y_from, stand):
        hx, hy, hc = jnp.right_shift(own, 3), jnp.bitwise_and(jnp.right_shift(own, 1), 3), jnp.bitwise_and(own, 1)
        hx, hy = jnp.bitwise_and(hx - x_from, SIDE - 1), jnp.bitwise_and(hy - y_from, SIDE - 1)
        first, second = jnp.where(order == 0, hx, hy), jnp.where(order == 0, hy, hx)
        at = ((order * SIDE + first) * SIDE + second) * 2 + hc
        return jnp.where(own >= 0, at, stand)

    table_ref[...] = jnp.zeros_like(table_ref)
    table_ref[0:1, 0:count] = position(own_row, order_row, x, y, 0)
    table_ref[1:2, 0:count] = jnp.where(own_row >= 0, own_row * 2 + order_row, 0)
    items = 4 * SIDE * SIDE
    slot = lax.broadcasted_iota(jnp.int32, (count, items), 0)
    item = lax.broadcasted_iota(jnp.int32, (count, items), 1)
    target = position(own_column, order_column, 0, 0, -1)
    table_ref[2:3, 0:items] = jnp.sum(jnp.where(target == item, slot, 0), axis=0, keepdims=True)
    stat = jnp.where(own_column >= 0, own_column * 2 + order_column, -1)
    table_ref[3:4, 0:items] = jnp.sum(jnp.where(stat == item, slot + 1, 0), axis=0, keepdims=True) - 1
    item = lax.broadcasted_iota(jnp.int32, (1, items), 1)
    table_ref[4:5, 0:items] = position(jnp.right_shift(item, 1), jnp.bitwise_and(item, 1), 0, 0, 0)


def body(queries, resp_keys, resp_values, prompt_keys, prompt_values, grad_out, slot_prompt, slot_length):
    slot_count, rows, dim = queries.shape
    held, length, _ = prompt_keys.shape
    factor = dim ** (-0.5)
    scale = factor * LOG2E
    n_dp = 2 * SIDE * SIDE
    items = 2 * n_dp
    table = pl.pallas_call(
        functools.partial(table_kernel, held), out_shape=jax.ShapeDtypeStruct((8, 128), jnp.int32)
    )(slot_prompt.reshape(1, slot_count))
    received, stats_in, groups = send_out(
        held, table, slot_prompt, slot_length, queries, grad_out, resp_keys, resp_values, scale
    )
    received = received.reshape((items,) + received.shape[4:])
    stats_in = stats_in.reshape((items,) + stats_in.shape[2:])
    result, stats, pdk, pdv = holder(groups, table, received, stats_in, prompt_keys, prompt_values, scale, factor)
    grid = (2, SIDE, SIDE, 2)
    back, local_out, local_dq, drk, drv, all_k, all_v = give_back(
        table, slot_prompt, slot_length, result.reshape(grid + result.shape[1:]),
        stats.reshape((n_dp, 2) + stats.shape[1:]), pdk, pdv, queries, grad_out, resp_keys, resp_values, scale, factor,
    )
    return finish(
        table, slot_prompt, slot_length, back.reshape(result.shape), local_out, local_dq, drk, drv, all_k, all_v
    )


def solution(mesh):
    return jax.shard_map(
        body,
        mesh=mesh,
        in_specs=(
            P("dp", None, "head"),
            P("dp", None, None),
            P("dp", None, None),
            P("dp", None, None),
            P("dp", None, None),
            P("dp", None, "head"),
            P("dp"),
            P("dp"),
        ),
        out_specs=(
            P("dp", None, "head"),
            P("dp", None, "head"),
            P("dp", "head", None),
            P("dp", "head", None),
            P("dp", None, None),
            P("dp", None, None),
        ),
        check_vma=False,
    )
```

```python
import functools
import math

import jax
import jax.numpy as jnp
from jax import lax
from jax.experimental import pallas as pl
from jax.experimental.pallas import tpu as pltpu
from jax.sharding import PartitionSpec as P

FANOUT = 8
LOG2E = math.log2(math.e)
F32 = jnp.float32
BF16 = jnp.bfloat16
STAT = 16


MESH = pl.DeviceIdType.MESH
SIDE = 4

def place():
    me = lax.axis_index("dp")
    core = lax.rem(me, 2)
    y = lax.rem(me // 2, SIDE)
    x = me // (2 * SIDE)
    return x, y, core

def device(k, a, b, core):
    x, y = (a, b) if k == 0 else (b, a)
    return {"dp": (x * SIDE + y) * 2 + core}

def step_by(value, by):
    return lax.rem(value + by + SIDE, SIDE)

def everyone():
    x, y, core = place()
    me = (x * SIDE + y) * 2 + core
    return [{"dp": lax.rem(me + k, 2 * SIDE * SIDE)} for k in range(1, 2 * SIDE * SIDE)]


def greet_start(near):
    barrier = pltpu.get_barrier_semaphore()
    for who in near:
        pl.semaphore_signal(barrier, inc=1, device_id=who, device_id_type=MESH)


def greet_end(near):
    pl.semaphore_wait(pltpu.get_barrier_semaphore(), len(near))

def remote(src, dst, send, recv, who):
    return pltpu.make_async_remote_copy(src_ref=src, dst_ref=dst, send_sem=send, recv_sem=recv, device_id=who, device_id_type=MESH)

class Route:
    def __init__(self, k, send, final, mid, rel1, rel2, sems):
        self.k, self.send, self.final, self.mid, self.rel1, self.rel2 = k, send, final, mid, rel1, rel2
        x, y, self.c = place()
        self.a, self.b = (x, y) if k == 0 else (y, x)
        (self.s1, self.r1, self.s1d, self.r1d, self.s1f, self.r1f,
         self.s2, self.r2, self.s2d, self.r2d, self.s2f, self.r2f, self.s0, self.r0, self.local) = sems
    def to_a(self, by): return device(self.k, step_by(self.a, by), self.b, self.c)
    def to_b(self, by, c): return device(self.k, self.a, step_by(self.b, by), c)
    def first_direct(self, side, j):
        by = 1 if side == 0 else -1
        b = step_by(self.b, j)
        r = 3 if side == 0 else 1
        return remote(self.send.at[step_by(self.a, by), b], self.mid.at[r - 1, b], self.s1.at[side, j], self.r1.at[side, j], self.to_a(by))
    def first_far(self, side, j):
        by = 1 if side == 0 else -1
        b = 2 * side + j
        return remote(self.send.at[step_by(self.a, 2), b], self.rel1.at[side, j], self.s1d.at[side, j], self.r1d.at[side, j], self.to_a(by))
    def first_forward(self, side, j):
        by = 1 if side == 0 else -1
        b = 2 * side + j
        return remote(self.rel1.at[side, j], self.mid.at[1, b], self.s1f.at[side, j], self.r1f.at[side, j], self.to_a(by))
    def source(self, r, b):
        return self.send.at[self.a, b] if r == 0 else self.mid.at[r - 1, b]
    def second_direct(self, r, side, c):
        by = 1 if side == 0 else -1
        rb = 3 if side == 0 else 1
        return remote(self.source(r, step_by(self.b, by)).at[c], self.final.at[r, rb, self.c], self.s2.at[r, side, c], self.r2.at[r, side, self.c], self.to_b(by, c))
    def second_far(self, r):
        side = r // 2
        by = 1 if side == 0 else -1
        return remote(self.source(r, step_by(self.b, 2)), self.rel2.at[side, r % 2], self.s2d.at[r], self.r2d.at[r], self.to_b(by, self.c))
    def second_forward(self, r, c):
        side = r // 2
        by = 1 if side == 0 else -1
        return remote(self.rel2.at[side, r % 2, c], self.final.at[r, 2, self.c], self.s2f.at[r, c], self.r2f.at[r, self.c], self.to_b(by, c))
    def cross(self, r):
        return remote(self.source(r, self.b).at[1 - self.c], self.final.at[r, 0, self.c], self.s0.at[r], self.r0.at[r], self.to_b(0, 1 - self.c))
    def own(self, r):
        return pltpu.make_async_copy(self.source(r, self.b).at[self.c], self.final.at[r, 0, self.c], self.local.at[r])

def wait_second_direct(route, r, side):
    for c in range(2):
        by = 1 if side == 0 else -1
        rb = 3 if side == 0 else 1
        d = route.final.at[r, rb, c]
        remote(d, d, route.s2.at[r, side, c], route.r2.at[r, side, c], route.to_b(by, c)).wait_recv()

def wait_second_forward(route, r):
    side = r // 2
    by = 1 if side == 0 else -1
    for c in range(2):
        d = route.final.at[r, 2, c]
        remote(d, d, route.s2f.at[r, c], route.r2f.at[r, c], route.to_b(by, c)).wait_recv()

def wait_cross(route, r):
    d = route.final.at[r, 0, 1 - route.c]
    remote(d, d, route.s0.at[r], route.r0.at[r], route.to_b(0, 1 - route.c)).wait_recv()

def route_sems():
    D = pltpu.SemaphoreType.DMA
    return [D((2, 4)), D((2, 4)), D((2, 2)), D((2, 2)), D((2, 2)), D((2, 2)),
            D((4, 2, 2)), D((4, 2, 2)), D((4,)), D((4,)), D((4, 2)), D((4, 2)), D((4,)), D((4,)), D((4,))]

def route_scratch(height, dim, dtype):
    V = pltpu.VMEM
    return [V((3, 4, 2, height, dim), dtype), V((2, 2, 2, height, dim), dtype), V((2, 2, 2, height, dim), dtype)]

def stages(routes):
    started = []

    def go(copy):
        copy.start()
        started.append(copy)

    def second_near(route, r, side):
        for c in range(2):
            go(route.second_direct(r, side, c))

    def second_here(route, r):
        go(route.cross(r))
        go(route.own(r))

    def relay(route, r):
        route.second_far(r).wait_recv()
        for c in range(2):
            go(route.second_forward(r, c))

    def begin():
        for j in range(2):
            for side in range(2):
                for route in routes:
                    go(route.first_far(side, j))
        for side in range(2):
            for route in routes:
                go(route.first_direct(side, 2))
        for route in routes:
            go(route.second_far(0))
        for j in (1, 3):
            for side in range(2):
                for route in routes:
                    go(route.first_direct(side, j))
        for route in routes:
            second_here(route, 0)

    def forward():
        for j in range(2):
            for side in range(2):
                for route in routes:
                    route.first_far(side, j).wait_recv()
                    go(route.first_forward(side, j))
        for side in range(2):
            for route in routes:
                go(route.first_direct(side, 0))

    def turn_far():
        for side in range(2):
            for route in routes:
                route.first_direct(side, 2).wait_recv()
                go(route.second_far(3 if side == 0 else 1))
        for route in routes:
            relay(route, 0)
        for route in routes:
            for side in range(2):
                second_near(route, 0, side)

    def turn_forwarded():
        for route in routes:
            for side in range(2):
                for j in range(2):
                    route.first_forward(side, j).wait_recv()
            go(route.second_far(2))

    def turn_near():
        for j, way in ((1, 0), (3, 1)):
            for side in range(2):
                for route in routes:
                    route.first_direct(side, j).wait_recv()
                    second_near(route, 3 if side == 0 else 1, way)

    def relay_rest():
        for r in (3, 1):
            for route in routes:
                relay(route, r)
        for route in routes:
            for side in range(2):
                second_near(route, 2, side)

    def turn_here():
        for side in range(2):
            for route in routes:
                route.first_direct(side, 0).wait_recv()
                second_here(route, 3 if side == 0 else 1)
        for route in routes:
            second_here(route, 2)
            relay(route, 2)

    def arrive():
        for r in (0, 3, 1, 2):
            for route in routes:
                for side in range(2):
                    wait_second_direct(route, r, side)
                wait_second_forward(route, r)
                wait_cross(route, r)
                route.own(r).wait()

    def close():
        for copy in started:
            if copy.is_remote:
                copy.wait_send()

    return [begin, forward, turn_far, turn_forwarded, turn_near, relay_rest, turn_here, arrive, close]


def dot(a, b, dims):
    return lax.dot_general(a, b, (dims, ((), ())), preferred_element_type=F32)


NT = ((1,), (1,))
NN = ((1,), (0,))
TN = ((0,), (0,))


def two_parts(value):
    high = value.astype(BF16)
    low = (value - high.astype(F32)).astype(BF16)
    return high.astype(F32), low.astype(F32)


def pack_rows(first, second, third=0.0):
    width = first.shape[1]
    rows = lax.broadcasted_iota(jnp.int32, (STAT, width), 0)
    a, b = two_parts(first)
    c, d = two_parts(second)
    packed = jnp.where(rows == 0, a, jnp.where(rows == 1, b, jnp.where(rows == 2, c, d)))
    return jnp.where(rows < 4, packed, third).astype(BF16)


def unpack_rows(packed, half):
    rows = packed.astype(F32)
    rows = jnp.where(half > 0, pltpu.roll(rows, STAT - 4, 0), rows)
    return rows[0:1] + rows[1:2], rows[2:3] + rows[3:4]


def live_rows(grad, length):
    row = lax.broadcasted_iota(jnp.int32, grad.shape, 0)
    return jnp.where(row < length, grad, jnp.zeros_like(grad))


def causal(shape):
    return lax.broadcasted_iota(jnp.int32, shape, 0) <= lax.broadcasted_iota(jnp.int32, shape, 1)


def swap_stats(stat_send, stat_in, own_sem, send_sem, recv_sem):
    x, y, core = place()
    me = (x * SIDE + y) * 2 + core
    n_dp = 2 * SIDE * SIDE
    own = pltpu.make_async_copy(stat_send.at[me], stat_in.at[me], own_sem)
    own.start()
    copies = []
    for i in range(1, n_dp):
        peer = lax.rem(me + i, n_dp)
        copy = remote(stat_send.at[peer], stat_in.at[me], send_sem.at[i], recv_sem.at[i], {"dp": peer})
        copy.start()
        copies.append(copy)
    return own, copies


def forward_slots(slots, scale, q, g, k, v):
    query = [q[s] for s in slots]
    grad = [g[s] for s in slots]
    key = [k[s] for s in slots]
    value = [v[s] for s in slots]
    scores = [dot(a, b, NT) * scale for a, b in zip(key, query)]
    grad_prob = [dot(a, b, NT) for a, b in zip(value, grad)]
    mask = causal(scores[0].shape)
    scores = [jnp.where(mask, a, -1e30) for a in scores]
    top = [jnp.max(a, axis=0, keepdims=True) for a in scores]
    exps = [jnp.exp2(a - b) for a, b in zip(scores, top)]
    total = [jnp.sum(a, axis=0, keepdims=True) for a in exps]
    row_sum = [jnp.sum(a * b, axis=0, keepdims=True) / c for a, b, c in zip(exps, grad_prob, total)]
    return [(a + jnp.log2(b), c) for a, b, c in zip(top, total, row_sum)]


def send_kernel(
    scale, held, table_ref, prompt_ref, length_ref, q_ref, g_ref, k_ref, v_ref, final_ref, stat_in, group_ref,
    q, g, k, v, packed, stat, stat_send, ids, load_sem, stat_s, stat_r, *scratch
):
    loads = [
        pltpu.make_async_copy(src, dst, load_sem.at[i])
        for i, (src, dst) in enumerate(((q_ref, q), (g_ref, g), (k_ref, k), (v_ref, v)))
    ]
    for load in loads:
        load.start()
    count, rows, _ = q.shape
    n_dp = 2 * SIDE * SIDE
    per = 5
    greet_start(everyone())
    loads[0].wait()
    loads[1].wait()

    def fill(i, carry):
        for half in range(2):
            for c in range(2):
                slot = table_ref[2, half * n_dp + i * 2 + c]
                at = (half, i // SIDE, lax.rem(i, SIDE), c)
                packed[at + (slice(0, rows), slice(None))] = q[slot]
                packed[at + (slice(rows, 2 * rows), slice(None))] = live_rows(g[slot], length_ref[slot])
        return carry

    lax.fori_loop(0, SIDE * SIDE, fill, 0)
    greet_end(everyone())
    n = 3 + 15
    routes = []
    for half in range(2):
        part = scratch[half * n : (half + 1) * n]
        routes.append(Route(half, packed.at[half], final_ref.at[half], part[0], part[1], part[2], part[3:]))
    bulk = stages(routes)
    bulk[0]()
    loads[2].wait()
    loads[3].wait()

    def forward(i, carry):
        slots = [i * per + j for j in range(per)]
        for slot, (lse, row_sum) in zip(slots, forward_slots(slots, scale, q, g, k, v)):
            lane = lax.broadcasted_iota(jnp.int32, row_sum.shape, 1)
            row_sum = jnp.where(lane < length_ref[slot], row_sum, 0.0)
            stat[slot] = pack_rows(lse, row_sum, jnp.bitwise_and(prompt_ref[slot], held - 1).astype(F32))
        return carry

    steps = count // per
    lax.fori_loop(0, steps // 2, forward, 0)
    bulk[1]()
    lax.fori_loop(steps // 2, steps, forward, 0)

    def fill_stats(i, carry):
        slots = [table_ref[3, i * 2 + half] for half in range(2)]
        one, two = [stat[jnp.maximum(slot, 0)].astype(F32) for slot in slots]
        row = lax.broadcasted_iota(jnp.int32, one.shape, 0)
        name_one = jnp.where(slots[0] < 0, -1.0, one)
        name_two = jnp.where(slots[1] < 0, -1.0, two)
        names = jnp.where(row == 8, name_one, name_two)
        numbers = jnp.where(row < 4, one, pltpu.roll(two, 4, 0))
        stat_send[i] = jnp.where(row < 8, numbers, names).astype(BF16)
        return carry

    lax.fori_loop(0, n_dp, fill_stats, 0)
    own, copies = swap_stats(stat_send, stat_in, load_sem.at[4], stat_s, stat_r)
    for stage in bulk[2:8]:
        stage()
    own.wait()
    for copy in copies:
        copy.wait_recv()
    x, y, _ = place()

    def name(i, carry):
        for half in range(2):
            ids[pl.ds(2 * i + half, 1), :] = stat_in[i].astype(F32)[8 + half : 9 + half]
        return carry

    lax.fori_loop(0, n_dp, name, 0)
    items = 2 * n_dp
    column = ids[...]
    item = lax.broadcasted_iota(jnp.int32, column.shape, 0)
    lane = lax.broadcasted_iota(jnp.int32, column.shape, 1)
    row = jnp.sum(jnp.where(item == lane, column, 0.0), axis=0, keepdims=True)
    earlier = jnp.where((column == row) & (lane < item), 1.0, 0.0)
    order = jnp.sum(earlier, axis=1, keepdims=True)
    spot = jnp.where(column >= 0.0, column * FANOUT + order, -1.0)
    hit = spot == lane.astype(F32)
    half, core = jnp.bitwise_and(item, 1), jnp.bitwise_and(jnp.right_shift(item, 1), 1)
    ax = jnp.bitwise_and(jnp.right_shift(item, 4) - x + SIDE, SIDE - 1)
    ay = jnp.bitwise_and(jnp.bitwise_and(jnp.right_shift(item, 2), SIDE - 1) - y + SIDE, SIDE - 1)
    first, second = jnp.where(half == 0, ax, ay), jnp.where(half == 0, ay, ax)
    where = ((half * SIDE + first) * SIDE + second) * 2 + core
    group_ref[0:1] = jnp.sum(jnp.where(hit, item, 0), axis=0, keepdims=True)
    group_ref[1:2] = jnp.sum(jnp.where(hit, where, 0), axis=0, keepdims=True)
    group_ref[2:] = jnp.zeros((6, group_ref.shape[1]), jnp.int32)
    bulk[8]()
    for copy in copies:
        copy.wait_send()


def send_out(held, table, prompts, lengths, queries, grads, keys, values, scale):
    count, rows, dim = queries.shape
    n_dp = 2 * SIDE * SIDE
    V, D = pltpu.VMEM, pltpu.SemaphoreType.DMA
    resp = (count, rows, dim)
    shape = (2, SIDE, SIDE, 2, 2 * rows, dim)
    scratch = [V(resp, BF16)] * 4 + [V(shape, BF16), V((count, STAT, dim), BF16), V((n_dp, STAT, dim), BF16)]
    scratch += [V((2 * n_dp, 128), F32)]
    scratch += [D((5,)), D((n_dp,)), D((n_dp,))]
    for _ in range(2):
        scratch += route_scratch(2 * rows, dim, BF16) + route_sems()
    smem = pl.BlockSpec(memory_space=pltpu.SMEM)
    anywhere = pl.BlockSpec(memory_space=pl.ANY)
    return pl.pallas_call(
        functools.partial(send_kernel, scale, held),
        out_shape=(
            jax.ShapeDtypeStruct(shape, BF16),
            jax.ShapeDtypeStruct((n_dp, STAT, dim), BF16),
            jax.ShapeDtypeStruct((8, 128), jnp.int32),
        ),
        in_specs=[smem] * 3 + [anywhere] * 4,
        out_specs=(anywhere, pl.BlockSpec(memory_space=pltpu.VMEM), pl.BlockSpec(memory_space=pltpu.VMEM)),
        scratch_shapes=scratch,
        compiler_params=pltpu.CompilerParams(collective_id=1, has_side_effects=True),
    )(table, prompts, lengths, queries, grads, keys, values)


PAIRS = 4
WIDE = 2 * PAIRS


def holder_kernel(
    scale, factor, group_ref, table_ref, in_ref, stat_in, k_ref, v_ref, out_ref, stat_ref, dk_ref, dv_ref,
    kt, vt, slots_in, out_buf, in_sem, out_sem,
):
    index = pl.program_id(0)
    rows = in_ref.shape[1] // 2

    def coming(at):
        return pltpu.make_async_copy(in_ref.at[group_ref[1, at]], slots_in.at[at], in_sem.at[at])

    @pl.when(index == 0)
    def _():
        for at in range(slots_in.shape[0]):
            coming(at).start()

    kt[...] = jnp.transpose(k_ref[0])
    vt[...] = jnp.transpose(v_ref[0])
    dk_ref[...] = jnp.zeros_like(dk_ref)
    dv_ref[...] = jnp.zeros_like(dv_ref)

    def leaving(at, j):
        slot = lax.rem(at, 2)
        item = group_ref[0, WIDE * at + j]
        return pltpu.make_async_copy(out_buf.at[slot, j], out_ref.at[table_ref[4, item]], out_sem.at[slot, j])

    @pl.when(index >= 2)
    def _():
        for j in range(WIDE):
            leaving(index - 2, j).wait()

    for j in range(WIDE):
        coming(WIDE * index + j).wait()
    pairs = [(2 * i, 2 * i + 1) for i in range(PAIRS)]
    items = [group_ref[0, WIDE * index + j] for j in range(WIDE)]

    def both(part):
        return [
            jnp.concatenate([slots_in[WIDE * index + i, part, :], slots_in[WIDE * index + j, part, :]], axis=0)
            for i, j in pairs
        ]

    query, grad = both(slice(0, rows)), both(slice(rows, 2 * rows))
    own = [unpack_rows(stat_in[jnp.right_shift(item, 1)], jnp.bitwise_and(item, 1)) for item in items]
    resp_lse = [jnp.concatenate([own[i][0], own[j][0]], axis=1) for i, j in pairs]
    resp_sum = [jnp.concatenate([own[i][1], own[j][1]], axis=1) for i, j in pairs]
    slot = lax.rem(index, 2)
    chunk = 128
    parts = [slice(c, c + chunk) for c in range(0, k_ref.shape[1], chunk)]

    def products(n):
        return dot(k_ref[0], query[n], NT), dot(v_ref[0], grad[n], NT)

    def weights(n, scores, grad_prob):
        tops, exps, totals, sums = [], [], [], []
        for part in parts:
            some = scores[part] * scale
            tops.append(jnp.max(some, axis=0, keepdims=True))
            exps.append(jnp.exp2(some - tops[-1]))
            totals.append(jnp.sum(exps[-1], axis=0, keepdims=True))
            sums.append(jnp.sum(exps[-1] * grad_prob[part], axis=0, keepdims=True))
        top = functools.reduce(jnp.maximum, tops)
        shares = [jnp.exp2(a - top) for a in tops]
        total = sum(a * b for a, b in zip(shares, totals))
        row_sum = sum(a * b for a, b in zip(shares, sums))
        prefix_lse = top + jnp.log2(total)
        high = jnp.maximum(prefix_lse, resp_lse[n])
        lse = high + jnp.log2(jnp.exp2(prefix_lse - high) + jnp.exp2(resp_lse[n] - high))
        weight = jnp.exp2(prefix_lse - lse) / total
        delta = weight * row_sum + jnp.exp2(resp_lse[n] - lse) * resp_sum[n]
        probs = [a * (weight * b) for a, b in zip(exps, shares)]
        dscore = [(a * (grad_prob[part] - delta)).astype(BF16) for a, part in zip(probs, parts)]
        for m, at in enumerate(pairs[n]):
            part = slice(m * rows, (m + 1) * rows)
            block, half = jnp.right_shift(items[at], 1), jnp.bitwise_and(items[at], 1)
            numbers = pack_rows(lse[:, part], delta[:, part]).astype(F32)
            row = lax.broadcasted_iota(jnp.int32, numbers.shape, 0)
            placed = jnp.where(half > 0, pltpu.roll(numbers, 4, 0), numbers)
            mine = jnp.right_shift(row, 2) == half
            stat_ref[block] = jnp.where(mine, placed, stat_ref[block].astype(F32)).astype(BF16)
        return jnp.concatenate([a.astype(BF16) for a in probs], axis=0), jnp.concatenate(dscore, axis=0)

    def close(n, prob, dscore):
        dk_ref[0] += dot(dscore, query[n], NN)
        dv_ref[0] += dot(prob, grad[n], NN)
        out = jnp.transpose(dot(vt[...], prob, NN)).astype(BF16)
        dq = jnp.transpose(dot(kt[...], dscore, NN) * factor).astype(BF16)
        for m, at in enumerate(pairs[n]):
            part = slice(m * rows, (m + 1) * rows)
            out_buf[slot, at, 0:rows, :] = out[part]
            out_buf[slot, at, rows:, :] = dq[part]

    after = products(0)
    for n in range(PAIRS):
        now = after
        if n + 1 < PAIRS:
            after = products(n + 1)
        close(n, *weights(n, *now))
    for j in range(WIDE):
        leaving(index, j).start()

    @pl.when(index == pl.num_programs(0) - 1)
    def _():
        for at in (index - 1, index):
            for j in range(WIDE):
                leaving(at, j).wait()


def holder(groups, table, received, stats, keys, values, scale, factor):
    count, height, dim = received.shape
    held, length, _ = keys.shape
    rows = height // 2
    whole = pl.BlockSpec((1, length, dim), lambda p, ids, b: (p, 0, 0))
    small = pl.BlockSpec(stats.shape, lambda p, ids, b: (0, 0, 0))
    anywhere = pl.BlockSpec(memory_space=pl.ANY)
    return pl.pallas_call(
        functools.partial(holder_kernel, scale, factor),
        out_shape=(
            jax.ShapeDtypeStruct((count, 2 * rows, dim), BF16),
            jax.ShapeDtypeStruct(stats.shape, BF16),
            jax.ShapeDtypeStruct((held, length, dim), F32),
            jax.ShapeDtypeStruct((held, length, dim), F32),
        ),
        grid_spec=pltpu.PrefetchScalarGridSpec(
            num_scalar_prefetch=2,
            grid=(held,),
            in_specs=[anywhere, small, whole, whole],
            out_specs=(anywhere, small, whole, whole),
            scratch_shapes=[
                pltpu.VMEM((dim, length), BF16),
                pltpu.VMEM((dim, length), BF16),
                pltpu.VMEM((held * FANOUT, 2 * rows, dim), BF16),
                pltpu.VMEM((2, WIDE, 2 * rows, dim), BF16),
                pltpu.SemaphoreType.DMA((held * FANOUT,)),
                pltpu.SemaphoreType.DMA((2, WIDE)),
            ],
        ),
    )(groups, table, received, stats, keys, values)


HEADS = 8


class Ring:
    def __init__(self, own, right, left, sent, came, send_sem, recv_sem):
        self.own, self.sent, self.came, self.send_sem, self.recv_sem = own, sent, came, send_sem, recv_sem
        self.me = lax.axis_index("head")
        self.lanes = ((1, right, 0), (-1, left, right))

    def copy(self, by, at):
        who = {"head": lax.rem(self.me + by + HEADS, HEADS)}
        return remote(self.sent.at[at], self.came.at[at], self.send_sem.at[at], self.recv_sem.at[at], who)

    def step(self, number):
        for by, hops, base in self.lanes:
            if number <= hops:
                target = lax.rem(self.me + by * (hops + 1 - number) + HEADS, HEADS)
                value = self.own(target)
                at = base + number - 1
                if number > 1:
                    self.copy(by, at - 1).wait_recv()
                    value = value + self.came[at - 1].astype(F32)
                self.sent[at] = value.astype(BF16)
                self.copy(by, at).start()

    def result(self):
        value = self.own(self.me)
        for by, hops, base in self.lanes:
            at = base + hops - 1
            self.copy(by, at).wait_recv()
            value = value + self.came[at].astype(F32)
        return value

    def close(self):
        for by, hops, base in self.lanes:
            for at in range(base, base + hops):
                self.copy(by, at).wait_send()


class Spread:
    def __init__(self, all_parts, right, left, send_sem, recv_sem):
        self.all_parts, self.send_sem, self.recv_sem = all_parts, send_sem, recv_sem
        self.me = lax.axis_index("head")
        self.lanes = ((1, right, 0), (-1, left, right))

    def copy(self, by, number, base):
        whose = lax.rem(self.me - by * (number - 1) + HEADS, HEADS)
        who = {"head": lax.rem(self.me + by + HEADS, HEADS)}
        at = base + number - 1
        part = self.all_parts.at[whose]
        return remote(part, part, self.send_sem.at[at], self.recv_sem.at[at], who)

    def arrival(self, by, number, base):
        whose = lax.rem(self.me - by * number + HEADS, HEADS)
        who = {"head": lax.rem(self.me + by + HEADS, HEADS)}
        at = base + number - 1
        part = self.all_parts.at[whose]
        return remote(part, part, self.send_sem.at[at], self.recv_sem.at[at], who)

    def step(self, number):
        for by, hops, base in self.lanes:
            if number <= hops:
                if number > 1:
                    self.arrival(by, number - 1, base).wait_recv()
                self.copy(by, number, base).start()

    def close(self):
        for by, hops, base in self.lanes:
            self.arrival(by, hops, base).wait_recv()
            for number in range(1, hops + 1):
                self.copy(by, number, base).wait_send()


def local_slots(slots, scale, factor, table_ref, prompt_ref, length_ref, stat_in, q, g, k, v, dk, dv, out, dq):
    query = [q[s] for s in slots]
    grad = [live_rows(g[s], length_ref[s]) for s in slots]
    key = [k[s] for s in slots]
    value = [v[s] for s in slots]
    stats = [unpack_rows(stat_in[table_ref[1, s] // 2], lax.rem(table_ref[1, s], 2)) for s in slots]
    lse = [jnp.where(prompt_ref[s] >= 0, a, 1e30) for s, (a, _) in zip(slots, stats)]
    delta = [jnp.where(prompt_ref[s] >= 0, a, 0.0) for s, (_, a) in zip(slots, stats)]
    scores = [dot(a, b, NT) * scale for a, b in zip(key, query)]
    grad_prob = [dot(a, b, NT) for a, b in zip(value, grad)]
    mask = causal(scores[0].shape)
    prob = [jnp.exp2(jnp.where(mask, a - b, -1e30)) for a, b in zip(scores, lse)]
    dscore = [(a * (b - c)).astype(BF16) for a, b, c in zip(prob, grad_prob, delta)]
    prob = [a.astype(BF16) for a in prob]
    part_k = [dot(a, b, NN) * factor for a, b in zip(dscore, query)]
    part_v = [dot(a, b, NN) for a, b in zip(prob, grad)]
    part_out = [dot(a, b, TN).astype(BF16) for a, b in zip(prob, value)]
    part_dq = [(dot(a, b, TN) * factor).astype(BF16) for a, b in zip(dscore, key)]
    for s, a, b, c, d in zip(slots, part_k, part_v, part_out, part_dq):
        dk[s], dv[s], out[s], dq[s] = a, b, c, d


def return_kernel(
    scale, factor, table_ref, prompt_ref, length_ref,
    back_ref, stat_ref, pdk_ref, pdv_ref, q_ref, g_ref, k_ref, v_ref,
    final, out_ref, dq_ref, drk_ref, drv_ref, all_k, all_v,
    q, g, k, v, pdk, pdv, dk, dv, out, dq, stat_in, load_sem, stat_s, stat_r, *scratch
):
    loads = [
        pltpu.make_async_copy(src, dst, load_sem.at[i])
        for i, (src, dst) in enumerate(
            ((pdk_ref, pdk), (pdv_ref, pdv), (q_ref, q), (g_ref, g), (k_ref, k), (v_ref, v))
        )
    ]
    for load in loads:
        load.start()
    head = lax.axis_index("head")
    near = everyone() + [{"head": lax.rem(head + by, HEADS)} for by in (1, HEADS - 1)]
    greet_start(near)
    greet_end(near)
    own_stat, stats = swap_stats(stat_ref, stat_in, load_sem.at[6], stat_s, stat_r)

    n = 3 + 15
    routes = []
    for half in range(2):
        part = scratch[half * n : (half + 1) * n]
        routes.append(Route(half, back_ref.at[half], final.at[half], part[0], part[1], part[2], part[3:]))
    ring_scratch = scratch[2 * n :]
    bulk = stages(routes)
    bulk[0]()

    count = q.shape[0]
    prompt_rows = pdk.shape[1] // HEADS
    slot_rows = q.shape[1] // HEADS

    def prompt_part(ref, by):
        return lambda t: ref[:, pl.ds(pl.multiple_of(t * prompt_rows, prompt_rows), prompt_rows), :] * by

    def slot_part(ref, group):
        some = slice(group * (count // GROUPS), (group + 1) * (count // GROUPS))
        return lambda t: ref[some, pl.ds(pl.multiple_of(t * slot_rows, slot_rows), slot_rows), :]

    owns = [prompt_part(pdk, factor), prompt_part(pdv, 1.0)]
    for group in range(GROUPS):
        owns += [slot_part(dk, group), slot_part(dv, group)]
    rings = []
    for i, own in enumerate(owns):
        right, left = (4, 3) if i % 2 == 0 else (3, 4)
        rings.append(Ring(own, right, left, *ring_scratch[4 * i : 4 * i + 4]))
    last = 4 * len(owns)
    spreads = [
        Spread(all_k, 4, 3, *ring_scratch[last : last + 2]),
        Spread(all_v, 3, 4, *ring_scratch[last + 2 : last + 4]),
    ]

    def ring(which, number):
        for one in rings[2 * which : 2 * which + 2]:
            one.step(number)

    def spread(number):
        for one in spreads:
            one.step(number)

    per = 5

    def local(piece):
        steps = count // per // 4

        def go(i, carry):
            slots = [(piece * steps + i) * per + j for j in range(per)]
            local_slots(
                slots, scale, factor, table_ref, prompt_ref, length_ref, stat_in, q, g, k, v, dk, dv, out, dq
            )
            return carry

        lax.fori_loop(0, steps, go, 0)

    begin, forward, turn_far, turn_forwarded, turn_near, relay_rest, turn_here, arrive, close = bulk
    loads[0].wait()
    loads[1].wait()
    ring(0, 1)
    for load in loads[2:]:
        load.wait()
    own_stat.wait()
    for copy in stats:
        copy.wait_recv()
    local(0)
    ring(0, 2)
    local(1)
    ring(1, 1)
    forward()
    local(2)
    ring(0, 3)
    local(3)
    ring(2, 1)
    leaving = [
        pltpu.make_async_copy(src, dst, load_sem.at[i]) for i, (src, dst) in enumerate(((out, out_ref), (dq, dq_ref)))
    ]
    for copy in leaving:
        copy.start()
    ring(0, 4)
    ring(1, 2)
    turn_far()
    ring(2, 2)
    all_k[head] = rings[0].result().astype(BF16)
    all_v[head] = rings[1].result().astype(BF16)
    spread(1)
    ring(1, 3)
    turn_forwarded()
    ring(2, 3)
    spread(2)
    turn_near()
    ring(1, 4)
    relay_rest()
    spread(3)
    ring(2, 4)
    turn_here()
    spread(4)
    half_count = count // GROUPS
    for group in range(GROUPS):
        some = slice(group * half_count, (group + 1) * half_count)
        drk_ref[some] = rings[2 + 2 * group].result()
        drv_ref[some] = rings[3 + 2 * group].result()
    for one in spreads:
        one.close()
    arrive()
    for copy in leaving:
        copy.wait()
    close()
    for one in rings:
        one.close()
    for copy in stats:
        copy.wait_send()


GROUPS = 2


def give_back(table, prompts, lengths, back, stats, pdk, pdv, queries, grads, keys, values, scale, factor):
    count, rows, dim = queries.shape
    held, length, _ = pdk.shape
    height = back.shape[-2]
    n_dp = 2 * SIDE * SIDE
    V, D = pltpu.VMEM, pltpu.SemaphoreType.DMA
    resp = (count, rows, dim)
    scratch = [V(resp, BF16)] * 4 + [V(pdk.shape, F32)] * 2 + [V(resp, F32)] * 2 + [V(resp, BF16)] * 2
    scratch += [V((n_dp, STAT, dim), BF16), D((7,)), D((n_dp,)), D((n_dp,))]
    for _ in range(2):
        scratch += route_scratch(height, dim, BF16) + route_sems()
    for shape in ((held, length // HEADS, dim),) * 2 + ((count // GROUPS, rows // HEADS, dim),) * (2 * GROUPS):
        scratch += [V((7,) + shape, BF16), V((7,) + shape, BF16), D((7,)), D((7,))]
    scratch += [D((7,))] * 4
    smem = pl.BlockSpec(memory_space=pltpu.SMEM)
    anywhere = pl.BlockSpec(memory_space=pl.ANY)
    vmem = pl.BlockSpec(memory_space=pltpu.VMEM)
    part = jax.ShapeDtypeStruct((count, rows // HEADS, dim), F32)
    parts = jax.ShapeDtypeStruct((HEADS, held, length // HEADS, dim), BF16)
    return pl.pallas_call(
        functools.partial(return_kernel, scale, factor),
        out_shape=(
            jax.ShapeDtypeStruct(back.shape, BF16),
            jax.ShapeDtypeStruct(resp, BF16),
            jax.ShapeDtypeStruct(resp, BF16),
            part,
            part,
            parts,
            parts,
        ),
        in_specs=[smem] * 3 + [anywhere] * 8,
        out_specs=(anywhere, anywhere, anywhere, vmem, vmem, vmem, vmem),
        scratch_shapes=scratch,
        compiler_params=pltpu.CompilerParams(collective_id=2, has_side_effects=True),
    )(table, prompts, lengths, back, stats, pdk, pdv, queries, grads, keys, values)


def finish_kernel(
    per_step, table_ref, prompt_ref, length_ref, in_ref, out_part, dq_part, drk, drv, pk, pv,
    out_ref, dq_ref, drk_ref, drv_ref, pk_ref, pv_ref, back, in_sem,
):
    rows = out_part.shape[1]
    step = pl.program_id(0)

    def coming(slot):
        return pltpu.make_async_copy(in_ref.at[table_ref[0, slot]], back.at[slot], in_sem.at[slot])

    @pl.when(step == 0)
    def _():
        for slot in range(back.shape[0]):
            coming(slot).start()

    drk_ref[...] = drk[...]
    drv_ref[...] = drv[...]
    part = pk.shape[2]
    for i in range(pk.shape[0]):
        pk_ref[:, i * part : (i + 1) * part, :] = pk[i].astype(F32)
        pv_ref[:, i * part : (i + 1) * part, :] = pv[i].astype(F32)
    for j in range(per_step):
        slot = step * per_step + j
        coming(slot).wait()
        row = lax.broadcasted_iota(jnp.int32, out_part.shape[1:], 0)
        live = row < jnp.where(prompt_ref[slot] >= 0, length_ref[slot], 0)
        out = back[slot, 0:rows, :].astype(F32) + out_part[j].astype(F32)
        dq = back[slot, rows : 2 * rows, :].astype(F32) + dq_part[j].astype(F32)
        out_ref[j] = jnp.where(live, out, 0.0).astype(BF16)
        dq_ref[j] = jnp.where(live, dq, 0.0).astype(BF16)


def finish(table, prompts, lengths, back, out_part, dq_part, drk, drv, all_k, all_v):
    count, rows, dim = out_part.shape
    _, held, part, _ = all_k.shape
    steps = 4
    per_step = count // steps
    some = pl.BlockSpec((per_step, rows, dim), lambda i, a, b, c: (i, 0, 0))
    own = pl.BlockSpec((per_step, rows // HEADS, dim), lambda i, a, b, c: (i, 0, 0))
    piece = pl.BlockSpec((HEADS // steps, held, part, dim), lambda i, a, b, c: (i, 0, 0, 0))
    placed = pl.BlockSpec((held, part * HEADS // steps, dim), lambda i, a, b, c: (0, i, 0))
    return pl.pallas_call(
        functools.partial(finish_kernel, per_step),
        out_shape=(jax.ShapeDtypeStruct((count, rows, dim), BF16),) * 2
        + (jax.ShapeDtypeStruct(drk.shape, F32),) * 2
        + (jax.ShapeDtypeStruct((held, HEADS * part, dim), F32),) * 2,
        grid_spec=pltpu.PrefetchScalarGridSpec(
            num_scalar_prefetch=3,
            grid=(steps,),
            in_specs=[pl.BlockSpec(memory_space=pl.ANY), some, some, own, own, piece, piece],
            out_specs=(some, some, own, own, placed, placed),
            scratch_shapes=[pltpu.VMEM((count, 2 * rows, dim), BF16), pltpu.SemaphoreType.DMA((count,))],
        ),
    )(table, prompts, lengths, back, out_part, dq_part, drk, drv, all_k, all_v)


def table_kernel(held, prompt_ref, table_ref):
    x, y, _ = place()
    count = prompt_ref.shape[1]
    prompts = prompt_ref[...]
    own_row = jnp.where(prompts >= 0, jnp.right_shift(prompts, held.bit_length() - 1), -1)
    one = lax.broadcasted_iota(jnp.int32, (count, count), 0)
    two = lax.broadcasted_iota(jnp.int32, (count, count), 1)
    own_column = jnp.sum(jnp.where(one == two, own_row, 0), axis=1, keepdims=True)
    same = own_column == own_row
    order_column = jnp.sum(jnp.where(same & (two < one), 1, 0), axis=1, keepdims=True)
    order_row = jnp.sum(jnp.where(same & (one < two), 1, 0), axis=0, keepdims=True)

    def position(own, order, x_from, y_from, stand):
        hx, hy, hc = jnp.right_shift(own, 3), jnp.bitwise_and(jnp.right_shift(own, 1), 3), jnp.bitwise_and(own, 1)
        hx, hy = jnp.bitwise_and(hx - x_from, SIDE - 1), jnp.bitwise_and(hy - y_from, SIDE - 1)
        first, second = jnp.where(order == 0, hx, hy), jnp.where(order == 0, hy, hx)
        at = ((order * SIDE + first) * SIDE + second) * 2 + hc
        return jnp.where(own >= 0, at, stand)

    table_ref[...] = jnp.zeros_like(table_ref)
    table_ref[0:1, 0:count] = position(own_row, order_row, x, y, 0)
    table_ref[1:2, 0:count] = jnp.where(own_row >= 0, own_row * 2 + order_row, 0)
    items = 4 * SIDE * SIDE
    slot = lax.broadcasted_iota(jnp.int32, (count, items), 0)
    item = lax.broadcasted_iota(jnp.int32, (count, items), 1)
    target = position(own_column, order_column, 0, 0, -1)
    table_ref[2:3, 0:items] = jnp.sum(jnp.where(target == item, slot, 0), axis=0, keepdims=True)
    stat = jnp.where(own_column >= 0, own_column * 2 + order_column, -1)
    table_ref[3:4, 0:items] = jnp.sum(jnp.where(stat == item, slot + 1, 0), axis=0, keepdims=True) - 1
    item = lax.broadcasted_iota(jnp.int32, (1, items), 1)
    table_ref[4:5, 0:items] = position(jnp.right_shift(item, 1), jnp.bitwise_and(item, 1), 0, 0, 0)


def body(queries, resp_keys, resp_values, prompt_keys, prompt_values, grad_out, slot_prompt, slot_length):
    slot_count, rows, dim = queries.shape
    held, length, _ = prompt_keys.shape
    factor = dim ** (-0.5)
    scale = factor * LOG2E
    items = 4 * SIDE * SIDE
    table = pl.pallas_call(
        functools.partial(table_kernel, held), out_shape=jax.ShapeDtypeStruct((8, 128), jnp.int32)
    )(slot_prompt.reshape(1, slot_count))
    received, stats_in, groups = send_out(
        held, table, slot_prompt, slot_length, queries, grad_out, resp_keys, resp_values, scale
    )
    received = received.reshape((items,) + received.shape[4:])
    result, stats, pdk, pdv = holder(groups, table, received, stats_in, prompt_keys, prompt_values, scale, factor)
    grid = (2, SIDE, SIDE, 2)
    back, local_out, local_dq, drk, drv, all_k, all_v = give_back(
        table, slot_prompt, slot_length, result.reshape(grid + result.shape[1:]),
        stats, pdk, pdv, queries, grad_out, resp_keys, resp_values, scale, factor,
    )
    return finish(
        table, slot_prompt, slot_length, back.reshape(result.shape), local_out, local_dq, drk, drv, all_k, all_v
    )


def solution(mesh):
    return jax.shard_map(
        body,
        mesh=mesh,
        in_specs=(
            P("dp", None, "head"),
            P("dp", None, None),
            P("dp", None, None),
            P("dp", None, None),
            P("dp", None, None),
            P("dp", None, "head"),
            P("dp"),
            P("dp"),
        ),
        out_specs=(
            P("dp", None, "head"),
            P("dp", None, "head"),
            P("dp", "head", None),
            P("dp", "head", None),
            P("dp", None, None),
            P("dp", None, None),
        ),
        check_vma=False,
    )
```

```python
import functools
import math

import jax
import jax.numpy as jnp
from jax import lax
from jax.experimental import pallas as pl
from jax.experimental.pallas import tpu as pltpu
from jax.sharding import PartitionSpec as P

FANOUT = 8
LOG2E = math.log2(math.e)
F32 = jnp.float32
BF16 = jnp.bfloat16
STAT = 16


MESH = pl.DeviceIdType.MESH
SIDE = 4

def place():
    me = lax.axis_index("dp")
    core = lax.rem(me, 2)
    y = lax.rem(me // 2, SIDE)
    x = me // (2 * SIDE)
    return x, y, core

def device(k, a, b, core):
    x, y = (a, b) if k == 0 else (b, a)
    return {"dp": (x * SIDE + y) * 2 + core}

def step_by(value, by):
    return lax.rem(value + by + SIDE, SIDE)

def everyone():
    x, y, core = place()
    me = (x * SIDE + y) * 2 + core
    return [{"dp": lax.rem(me + k, 2 * SIDE * SIDE)} for k in range(1, 2 * SIDE * SIDE)]


def greet_start(near):
    barrier = pltpu.get_barrier_semaphore()
    for who in near:
        pl.semaphore_signal(barrier, inc=1, device_id=who, device_id_type=MESH)


def greet_end(near):
    pl.semaphore_wait(pltpu.get_barrier_semaphore(), len(near))

def remote(src, dst, send, recv, who):
    return pltpu.make_async_remote_copy(src_ref=src, dst_ref=dst, send_sem=send, recv_sem=recv, device_id=who, device_id_type=MESH)

class Route:
    def __init__(self, k, send, final, mid, rel1, rel2, sems):
        self.k, self.send, self.final, self.mid, self.rel1, self.rel2 = k, send, final, mid, rel1, rel2
        x, y, self.c = place()
        self.a, self.b = (x, y) if k == 0 else (y, x)
        (self.s1, self.r1, self.s1d, self.r1d, self.s1f, self.r1f,
         self.s2, self.r2, self.s2d, self.r2d, self.s2f, self.r2f, self.s0, self.r0, self.local) = sems
    def to_a(self, by): return device(self.k, step_by(self.a, by), self.b, self.c)
    def to_b(self, by, c): return device(self.k, self.a, step_by(self.b, by), c)
    def first_direct(self, side, j):
        by = 1 if side == 0 else -1
        b = step_by(self.b, j)
        r = 3 if side == 0 else 1
        return remote(self.send.at[step_by(self.a, by), b], self.mid.at[r - 1, b], self.s1.at[side, j], self.r1.at[side, j], self.to_a(by))
    def first_far(self, side, j):
        by = 1 if side == 0 else -1
        b = 2 * side + j
        return remote(self.send.at[step_by(self.a, 2), b], self.rel1.at[side, j], self.s1d.at[side, j], self.r1d.at[side, j], self.to_a(by))
    def first_forward(self, side, j):
        by = 1 if side == 0 else -1
        b = 2 * side + j
        return remote(self.rel1.at[side, j], self.mid.at[1, b], self.s1f.at[side, j], self.r1f.at[side, j], self.to_a(by))
    def source(self, r, b):
        return self.send.at[self.a, b] if r == 0 else self.mid.at[r - 1, b]
    def second_direct(self, r, side, c):
        by = 1 if side == 0 else -1
        rb = 3 if side == 0 else 1
        return remote(self.source(r, step_by(self.b, by)).at[c], self.final.at[r, rb, self.c], self.s2.at[r, side, c], self.r2.at[r, side, self.c], self.to_b(by, c))
    def second_far(self, r):
        side = r // 2
        by = 1 if side == 0 else -1
        return remote(self.source(r, step_by(self.b, 2)), self.rel2.at[side, r % 2], self.s2d.at[r], self.r2d.at[r], self.to_b(by, self.c))
    def second_forward(self, r, c):
        side = r // 2
        by = 1 if side == 0 else -1
        return remote(self.rel2.at[side, r % 2, c], self.final.at[r, 2, self.c], self.s2f.at[r, c], self.r2f.at[r, self.c], self.to_b(by, c))
    def cross(self, r):
        return remote(self.source(r, self.b).at[1 - self.c], self.final.at[r, 0, self.c], self.s0.at[r], self.r0.at[r], self.to_b(0, 1 - self.c))
    def own(self, r):
        return pltpu.make_async_copy(self.source(r, self.b).at[self.c], self.final.at[r, 0, self.c], self.local.at[r])

def wait_second_direct(route, r, side):
    for c in range(2):
        by = 1 if side == 0 else -1
        rb = 3 if side == 0 else 1
        d = route.final.at[r, rb, c]
        remote(d, d, route.s2.at[r, side, c], route.r2.at[r, side, c], route.to_b(by, c)).wait_recv()

def wait_second_forward(route, r):
    side = r // 2
    by = 1 if side == 0 else -1
    for c in range(2):
        d = route.final.at[r, 2, c]
        remote(d, d, route.s2f.at[r, c], route.r2f.at[r, c], route.to_b(by, c)).wait_recv()

def wait_cross(route, r):
    d = route.final.at[r, 0, 1 - route.c]
    remote(d, d, route.s0.at[r], route.r0.at[r], route.to_b(0, 1 - route.c)).wait_recv()

def route_sems():
    D = pltpu.SemaphoreType.DMA
    return [D((2, 4)), D((2, 4)), D((2, 2)), D((2, 2)), D((2, 2)), D((2, 2)),
            D((4, 2, 2)), D((4, 2, 2)), D((4,)), D((4,)), D((4, 2)), D((4, 2)), D((4,)), D((4,)), D((4,))]

def route_scratch(height, dim, dtype):
    V = pltpu.VMEM
    return [V((3, 4, 2, height, dim), dtype), V((2, 2, 2, height, dim), dtype), V((2, 2, 2, height, dim), dtype)]

def stages(routes):
    started = []

    def go(copy):
        copy.start()
        started.append(copy)

    def second_near(route, r, side):
        for c in range(2):
            go(route.second_direct(r, side, c))

    def second_here(route, r):
        go(route.cross(r))
        go(route.own(r))

    def relay(route, r):
        route.second_far(r).wait_recv()
        for c in range(2):
            go(route.second_forward(r, c))

    def begin():
        for j in range(2):
            for side in range(2):
                for route in routes:
                    go(route.first_far(side, j))
        for side in range(2):
            for route in routes:
                go(route.first_direct(side, 2))
        for route in routes:
            go(route.second_far(0))
        for j in (1, 3):
            for side in range(2):
                for route in routes:
                    go(route.first_direct(side, j))
        for route in routes:
            second_here(route, 0)

    def forward():
        for j in range(2):
            for side in range(2):
                for route in routes:
                    route.first_far(side, j).wait_recv()
                    go(route.first_forward(side, j))
        for side in range(2):
            for route in routes:
                go(route.first_direct(side, 0))

    def turn_far():
        for side in range(2):
            for route in routes:
                route.first_direct(side, 2).wait_recv()
                go(route.second_far(3 if side == 0 else 1))
        for route in routes:
            relay(route, 0)
        for route in routes:
            for side in range(2):
                second_near(route, 0, side)

    def turn_forwarded():
        for route in routes:
            for side in range(2):
                for j in range(2):
                    route.first_forward(side, j).wait_recv()
            go(route.second_far(2))

    def turn_near():
        for j, way in ((1, 0), (3, 1)):
            for side in range(2):
                for route in routes:
                    route.first_direct(side, j).wait_recv()
                    second_near(route, 3 if side == 0 else 1, way)

    def relay_rest():
        for r in (3, 1):
            for route in routes:
                relay(route, r)
        for route in routes:
            for side in range(2):
                second_near(route, 2, side)

    def turn_here():
        for side in range(2):
            for route in routes:
                route.first_direct(side, 0).wait_recv()
                second_here(route, 3 if side == 0 else 1)
        for route in routes:
            second_here(route, 2)
            relay(route, 2)

    def arrive():
        for r in (0, 3, 1, 2):
            for route in routes:
                for side in range(2):
                    wait_second_direct(route, r, side)
                wait_second_forward(route, r)
                wait_cross(route, r)
                route.own(r).wait()

    def close():
        for copy in started:
            if copy.is_remote:
                copy.wait_send()

    return [begin, forward, turn_far, turn_forwarded, turn_near, relay_rest, turn_here, arrive, close]


def dot(a, b, dims):
    return lax.dot_general(a, b, (dims, ((), ())), preferred_element_type=F32)


NT = ((1,), (1,))
NN = ((1,), (0,))
TN = ((0,), (0,))


def two_parts(value):
    high = value.astype(BF16)
    low = (value - high.astype(F32)).astype(BF16)
    return high.astype(F32), low.astype(F32)


def pack_rows(first, second, third=0.0):
    width = first.shape[1]
    rows = lax.broadcasted_iota(jnp.int32, (STAT, width), 0)
    a, b = two_parts(first)
    c, d = two_parts(second)
    packed = jnp.where(rows == 0, a, jnp.where(rows == 1, b, jnp.where(rows == 2, c, d)))
    return jnp.where(rows < 4, packed, third).astype(BF16)


def unpack_rows(packed, half):
    rows = packed.astype(F32)
    rows = jnp.where(half > 0, pltpu.roll(rows, STAT - 4, 0), rows)
    return rows[0:1] + rows[1:2], rows[2:3] + rows[3:4]


def live_rows(grad, length):
    row = lax.broadcasted_iota(jnp.int32, grad.shape, 0)
    return jnp.where(row < length, grad, jnp.zeros_like(grad))


def causal(shape):
    return lax.broadcasted_iota(jnp.int32, shape, 0) <= lax.broadcasted_iota(jnp.int32, shape, 1)


def swap_stats(stat_send, stat_in, own_sem, send_sem, recv_sem):
    x, y, core = place()
    me = (x * SIDE + y) * 2 + core
    n_dp = 2 * SIDE * SIDE
    own = pltpu.make_async_copy(stat_send.at[me], stat_in.at[me], own_sem)
    own.start()
    copies = []
    for i in range(1, n_dp):
        peer = lax.rem(me + i, n_dp)
        copy = remote(stat_send.at[peer], stat_in.at[me], send_sem.at[i], recv_sem.at[i], {"dp": peer})
        copy.start()
        copies.append(copy)
    return own, copies


def forward_slots(slots, scale, q, g, k, v):
    query = [q[s] for s in slots]
    grad = [g[s] for s in slots]
    key = [k[s] for s in slots]
    value = [v[s] for s in slots]
    scores = [dot(a, b, NT) * scale for a, b in zip(key, query)]
    grad_prob = [dot(a, b, NT) for a, b in zip(value, grad)]
    mask = causal(scores[0].shape)
    scores = [jnp.where(mask, a, -1e30) for a in scores]
    top = [jnp.max(a, axis=0, keepdims=True) for a in scores]
    exps = [jnp.exp2(a - b) for a, b in zip(scores, top)]
    total = [jnp.sum(a, axis=0, keepdims=True) for a in exps]
    row_sum = [jnp.sum(a * b, axis=0, keepdims=True) / c for a, b, c in zip(exps, grad_prob, total)]
    return [(a + jnp.log2(b), c) for a, b, c in zip(top, total, row_sum)]


def send_kernel(
    scale, held, table_ref, prompt_ref, length_ref, q_ref, g_ref, k_ref, v_ref, final_ref, stat_in, group_ref,
    q, g, k, v, packed, stat, stat_send, ids, load_sem, stat_s, stat_r, *scratch
):
    loads = [
        pltpu.make_async_copy(src, dst, load_sem.at[i])
        for i, (src, dst) in enumerate(((q_ref, q), (g_ref, g), (k_ref, k), (v_ref, v)))
    ]
    for load in loads:
        load.start()
    count, rows, _ = q.shape
    n_dp = 2 * SIDE * SIDE
    per = 5
    greet_start(everyone())
    loads[0].wait()
    loads[1].wait()

    def fill(i, carry):
        for half in range(2):
            for c in range(2):
                slot = table_ref[2, half * n_dp + i * 2 + c]
                at = (half, i // SIDE, lax.rem(i, SIDE), c)
                packed[at + (slice(0, rows), slice(None))] = q[slot]
                packed[at + (slice(rows, 2 * rows), slice(None))] = live_rows(g[slot], length_ref[slot])
        return carry

    lax.fori_loop(0, SIDE * SIDE, fill, 0)
    greet_end(everyone())
    n = 3 + 15
    routes = []
    for half in range(2):
        part = scratch[half * n : (half + 1) * n]
        routes.append(Route(half, packed.at[half], final_ref.at[half], part[0], part[1], part[2], part[3:]))
    bulk = stages(routes)
    bulk[0]()
    loads[2].wait()
    loads[3].wait()

    def forward(i, carry):
        slots = [i * per + j for j in range(per)]
        for slot, (lse, row_sum) in zip(slots, forward_slots(slots, scale, q, g, k, v)):
            lane = lax.broadcasted_iota(jnp.int32, row_sum.shape, 1)
            row_sum = jnp.where(lane < length_ref[slot], row_sum, 0.0)
            stat[slot] = pack_rows(lse, row_sum, jnp.bitwise_and(prompt_ref[slot], held - 1).astype(F32))
        return carry

    steps = count // per
    lax.fori_loop(0, steps // 2, forward, 0)
    bulk[1]()
    lax.fori_loop(steps // 2, steps, forward, 0)

    def fill_stats(i, carry):
        slots = [table_ref[3, i * 2 + half] for half in range(2)]
        one, two = [stat[jnp.maximum(slot, 0)].astype(F32) for slot in slots]
        row = lax.broadcasted_iota(jnp.int32, one.shape, 0)
        name_one = jnp.where(slots[0] < 0, -1.0, one)
        name_two = jnp.where(slots[1] < 0, -1.0, two)
        names = jnp.where(row == 8, name_one, name_two)
        numbers = jnp.where(row < 4, one, pltpu.roll(two, 4, 0))
        stat_send[i] = jnp.where(row < 8, numbers, names).astype(BF16)
        return carry

    lax.fori_loop(0, n_dp, fill_stats, 0)
    own, copies = swap_stats(stat_send, stat_in, load_sem.at[4], stat_s, stat_r)
    for stage in bulk[2:8]:
        stage()
    own.wait()
    for copy in copies:
        copy.wait_recv()
    x, y, _ = place()

    def name(i, carry):
        for half in range(2):
            ids[pl.ds(2 * i + half, 1), :] = stat_in[i].astype(F32)[8 + half : 9 + half]
        return carry

    lax.fori_loop(0, n_dp, name, 0)
    items = 2 * n_dp
    column = ids[...]
    item = lax.broadcasted_iota(jnp.int32, column.shape, 0)
    lane = lax.broadcasted_iota(jnp.int32, column.shape, 1)
    row = jnp.sum(jnp.where(item == lane, column, 0.0), axis=0, keepdims=True)
    earlier = jnp.where((column == row) & (lane < item), 1.0, 0.0)
    order = jnp.sum(earlier, axis=1, keepdims=True)
    spot = jnp.where(column >= 0.0, column * FANOUT + order, -1.0)
    hit = spot == lane.astype(F32)
    half, core = jnp.bitwise_and(item, 1), jnp.bitwise_and(jnp.right_shift(item, 1), 1)
    ax = jnp.bitwise_and(jnp.right_shift(item, 4) - x + SIDE, SIDE - 1)
    ay = jnp.bitwise_and(jnp.bitwise_and(jnp.right_shift(item, 2), SIDE - 1) - y + SIDE, SIDE - 1)
    first, second = jnp.where(half == 0, ax, ay), jnp.where(half == 0, ay, ax)
    where = ((half * SIDE + first) * SIDE + second) * 2 + core
    group_ref[0:1] = jnp.sum(jnp.where(hit, item, 0), axis=0, keepdims=True)
    group_ref[1:2] = jnp.sum(jnp.where(hit, where, 0), axis=0, keepdims=True)
    group_ref[2:] = jnp.zeros((6, group_ref.shape[1]), jnp.int32)
    bulk[8]()
    for copy in copies:
        copy.wait_send()


def send_out(held, table, prompts, lengths, queries, grads, keys, values, scale):
    count, rows, dim = queries.shape
    n_dp = 2 * SIDE * SIDE
    V, D = pltpu.VMEM, pltpu.SemaphoreType.DMA
    resp = (count, rows, dim)
    shape = (2, SIDE, SIDE, 2, 2 * rows, dim)
    scratch = [V(resp, BF16)] * 4 + [V(shape, BF16), V((count, STAT, dim), BF16), V((n_dp, STAT, dim), BF16)]
    scratch += [V((2 * n_dp, 128), F32)]
    scratch += [D((5,)), D((n_dp,)), D((n_dp,))]
    for _ in range(2):
        scratch += route_scratch(2 * rows, dim, BF16) + route_sems()
    smem = pl.BlockSpec(memory_space=pltpu.SMEM)
    anywhere = pl.BlockSpec(memory_space=pl.ANY)
    return pl.pallas_call(
        functools.partial(send_kernel, scale, held),
        out_shape=(
            jax.ShapeDtypeStruct(shape, BF16),
            jax.ShapeDtypeStruct((n_dp, STAT, dim), BF16),
            jax.ShapeDtypeStruct((8, 128), jnp.int32),
        ),
        in_specs=[smem] * 3 + [anywhere] * 4,
        out_specs=(anywhere, pl.BlockSpec(memory_space=pltpu.VMEM), pl.BlockSpec(memory_space=pltpu.VMEM)),
        scratch_shapes=scratch,
        compiler_params=pltpu.CompilerParams(collective_id=1, has_side_effects=True),
    )(table, prompts, lengths, queries, grads, keys, values)


PAIRS = 4
WIDE = 2 * PAIRS


def holder_kernel(
    scale, factor, group_ref, table_ref, in_ref, stat_in, k_ref, v_ref, out_ref, stat_ref, dk_ref, dv_ref,
    kt, vt, slots_in, out_buf, in_sem, out_sem,
):
    index = pl.program_id(0)
    rows = in_ref.shape[1] // 2

    def coming(at):
        return pltpu.make_async_copy(in_ref.at[group_ref[1, at]], slots_in.at[at], in_sem.at[at])

    @pl.when(index == 0)
    def _():
        for at in range(slots_in.shape[0]):
            coming(at).start()

    kt[...] = jnp.transpose(k_ref[0])
    vt[...] = jnp.transpose(v_ref[0])

    def leaving(at, j):
        slot = lax.rem(at, 2)
        item = group_ref[0, WIDE * at + j]
        return pltpu.make_async_copy(out_buf.at[slot, j], out_ref.at[table_ref[4, item]], out_sem.at[slot, j])

    @pl.when(index >= 2)
    def _():
        for j in range(WIDE):
            leaving(index - 2, j).wait()

    for j in range(WIDE):
        coming(WIDE * index + j).wait()
    pairs = [(2 * i, 2 * i + 1) for i in range(PAIRS)]
    items = [group_ref[0, WIDE * index + j] for j in range(WIDE)]

    def both(part):
        return [
            jnp.concatenate([slots_in[WIDE * index + i, part, :], slots_in[WIDE * index + j, part, :]], axis=0)
            for i, j in pairs
        ]

    query, grad = both(slice(0, rows)), both(slice(rows, 2 * rows))
    own = [unpack_rows(stat_in[jnp.right_shift(item, 1)], jnp.bitwise_and(item, 1)) for item in items]
    resp_lse = [jnp.concatenate([own[i][0], own[j][0]], axis=1) for i, j in pairs]
    resp_sum = [jnp.concatenate([own[i][1], own[j][1]], axis=1) for i, j in pairs]
    slot = lax.rem(index, 2)
    chunk = 128
    parts = [slice(c, c + chunk) for c in range(0, k_ref.shape[1], chunk)]

    def products(n):
        return dot(k_ref[0], query[n], NT), dot(v_ref[0], grad[n], NT)

    def weights(n, scores, grad_prob):
        tops, exps, totals, sums = [], [], [], []
        for part in parts:
            some = scores[part] * scale
            tops.append(jnp.max(some, axis=0, keepdims=True))
            exps.append(jnp.exp2(some - tops[-1]))
            totals.append(jnp.sum(exps[-1], axis=0, keepdims=True))
            sums.append(jnp.sum(exps[-1] * grad_prob[part], axis=0, keepdims=True))
        top = functools.reduce(jnp.maximum, tops)
        shares = [jnp.exp2(a - top) for a in tops]
        total = sum(a * b for a, b in zip(shares, totals))
        row_sum = sum(a * b for a, b in zip(shares, sums))
        prefix_lse = top + jnp.log2(total)
        high = jnp.maximum(prefix_lse, resp_lse[n])
        lse = high + jnp.log2(jnp.exp2(prefix_lse - high) + jnp.exp2(resp_lse[n] - high))
        weight = jnp.exp2(prefix_lse - lse) / total
        delta = weight * row_sum + jnp.exp2(resp_lse[n] - lse) * resp_sum[n]
        probs = [a * (weight * b) for a, b in zip(exps, shares)]
        dscore = [(a * (grad_prob[part] - delta)).astype(BF16) for a, part in zip(probs, parts)]
        for m, at in enumerate(pairs[n]):
            part = slice(m * rows, (m + 1) * rows)
            block, half = jnp.right_shift(items[at], 1), jnp.bitwise_and(items[at], 1)
            numbers = pack_rows(lse[:, part], delta[:, part]).astype(F32)
            row = lax.broadcasted_iota(jnp.int32, numbers.shape, 0)
            placed = jnp.where(half > 0, pltpu.roll(numbers, 4, 0), numbers)
            mine = jnp.right_shift(row, 2) == half
            stat_ref[block] = jnp.where(mine, placed, stat_ref[block].astype(F32)).astype(BF16)
        return jnp.concatenate([a.astype(BF16) for a in probs], axis=0), jnp.concatenate(dscore, axis=0)

    def close(n, prob, dscore):
        part_k, part_v = dot(dscore, query[n], NN), dot(prob, grad[n], NN)
        dk_ref[0] = part_k if n == 0 else dk_ref[0] + part_k
        dv_ref[0] = part_v if n == 0 else dv_ref[0] + part_v
        out = jnp.transpose(dot(vt[...], prob, NN)).astype(BF16)
        dq = jnp.transpose(dot(kt[...], dscore, NN) * factor).astype(BF16)
        for m, at in enumerate(pairs[n]):
            part = slice(m * rows, (m + 1) * rows)
            out_buf[slot, at, 0:rows, :] = out[part]
            out_buf[slot, at, rows:, :] = dq[part]

    after = products(0)
    for n in range(PAIRS):
        now = after
        if n + 1 < PAIRS:
            after = products(n + 1)
        close(n, *weights(n, *now))
    for j in range(WIDE):
        leaving(index, j).start()

    @pl.when(index == pl.num_programs(0) - 1)
    def _():
        for at in (index - 1, index):
            for j in range(WIDE):
                leaving(at, j).wait()


def holder(groups, table, received, stats, keys, values, scale, factor):
    count, height, dim = received.shape
    held, length, _ = keys.shape
    rows = height // 2
    whole = pl.BlockSpec((1, length, dim), lambda p, ids, b: (p, 0, 0))
    small = pl.BlockSpec(stats.shape, lambda p, ids, b: (0, 0, 0))
    anywhere = pl.BlockSpec(memory_space=pl.ANY)
    return pl.pallas_call(
        functools.partial(holder_kernel, scale, factor),
        out_shape=(
            jax.ShapeDtypeStruct((count, 2 * rows, dim), BF16),
            jax.ShapeDtypeStruct(stats.shape, BF16),
            jax.ShapeDtypeStruct((held, length, dim), F32),
            jax.ShapeDtypeStruct((held, length, dim), F32),
        ),
        grid_spec=pltpu.PrefetchScalarGridSpec(
            num_scalar_prefetch=2,
            grid=(held,),
            in_specs=[anywhere, small, whole, whole],
            out_specs=(anywhere, small, whole, whole),
            scratch_shapes=[
                pltpu.VMEM((dim, length), BF16),
                pltpu.VMEM((dim, length), BF16),
                pltpu.VMEM((held * FANOUT, 2 * rows, dim), BF16),
                pltpu.VMEM((2, WIDE, 2 * rows, dim), BF16),
                pltpu.SemaphoreType.DMA((held * FANOUT,)),
                pltpu.SemaphoreType.DMA((2, WIDE)),
            ],
        ),
        compiler_params=pltpu.CompilerParams(),
    )(groups, table, received, stats, keys, values)


HEADS = 8


class Ring:
    def __init__(self, own, right, left, sent, came, send_sem, recv_sem):
        self.own, self.sent, self.came, self.send_sem, self.recv_sem = own, sent, came, send_sem, recv_sem
        self.me = lax.axis_index("head")
        self.lanes = ((1, right, 0), (-1, left, right))

    def copy(self, by, at):
        who = {"head": lax.rem(self.me + by + HEADS, HEADS)}
        return remote(self.sent.at[at], self.came.at[at], self.send_sem.at[at], self.recv_sem.at[at], who)

    def step(self, number):
        for by, hops, base in self.lanes:
            if number <= hops:
                target = lax.rem(self.me + by * (hops + 1 - number) + HEADS, HEADS)
                value = self.own(target)
                at = base + number - 1
                if number > 1:
                    self.copy(by, at - 1).wait_recv()
                    value = value + self.came[at - 1].astype(F32)
                self.sent[at] = value.astype(BF16)
                self.copy(by, at).start()

    def result(self):
        value = self.own(self.me)
        for by, hops, base in self.lanes:
            at = base + hops - 1
            self.copy(by, at).wait_recv()
            value = value + self.came[at].astype(F32)
        return value

    def close(self):
        for by, hops, base in self.lanes:
            for at in range(base, base + hops):
                self.copy(by, at).wait_send()


class Spread:
    def __init__(self, all_parts, right, left, send_sem, recv_sem):
        self.all_parts, self.send_sem, self.recv_sem = all_parts, send_sem, recv_sem
        self.me = lax.axis_index("head")
        self.lanes = ((1, right, 0), (-1, left, right))

    def copy(self, by, number, base):
        whose = lax.rem(self.me - by * (number - 1) + HEADS, HEADS)
        who = {"head": lax.rem(self.me + by + HEADS, HEADS)}
        at = base + number - 1
        part = self.all_parts.at[whose]
        return remote(part, part, self.send_sem.at[at], self.recv_sem.at[at], who)

    def arrival(self, by, number, base):
        whose = lax.rem(self.me - by * number + HEADS, HEADS)
        who = {"head": lax.rem(self.me + by + HEADS, HEADS)}
        at = base + number - 1
        part = self.all_parts.at[whose]
        return remote(part, part, self.send_sem.at[at], self.recv_sem.at[at], who)

    def step(self, number):
        for by, hops, base in self.lanes:
            if number <= hops:
                if number > 1:
                    self.arrival(by, number - 1, base).wait_recv()
                self.copy(by, number, base).start()

    def close(self):
        for by, hops, base in self.lanes:
            self.arrival(by, hops, base).wait_recv()
            for number in range(1, hops + 1):
                self.copy(by, number, base).wait_send()


def local_slots(slots, scale, factor, table_ref, prompt_ref, length_ref, stat_in, q, g, k, v, dk, dv, out, dq):
    query = [q[s] for s in slots]
    grad = [live_rows(g[s], length_ref[s]) for s in slots]
    key = [k[s] for s in slots]
    value = [v[s] for s in slots]
    stats = [unpack_rows(stat_in[table_ref[1, s] // 2], lax.rem(table_ref[1, s], 2)) for s in slots]
    lse = [jnp.where(prompt_ref[s] >= 0, a, 1e30) for s, (a, _) in zip(slots, stats)]
    delta = [jnp.where(prompt_ref[s] >= 0, a, 0.0) for s, (_, a) in zip(slots, stats)]
    scores = [dot(a, b, NT) * scale for a, b in zip(key, query)]
    grad_prob = [dot(a, b, NT) for a, b in zip(value, grad)]
    mask = causal(scores[0].shape)
    prob = [jnp.exp2(jnp.where(mask, a - b, -1e30)) for a, b in zip(scores, lse)]
    dscore = [(a * (b - c)).astype(BF16) for a, b, c in zip(prob, grad_prob, delta)]
    prob = [a.astype(BF16) for a in prob]
    part_k = [dot(a, b, NN) * factor for a, b in zip(dscore, query)]
    part_v = [dot(a, b, NN) for a, b in zip(prob, grad)]
    part_out = [dot(a, b, TN).astype(BF16) for a, b in zip(prob, value)]
    part_dq = [(dot(a, b, TN) * factor).astype(BF16) for a, b in zip(dscore, key)]
    for s, a, b, c, d in zip(slots, part_k, part_v, part_out, part_dq):
        dk[s], dv[s], out[s], dq[s] = a, b, c, d


def return_kernel(
    scale, factor, table_ref, prompt_ref, length_ref,
    back_ref, stat_ref, pdk_ref, pdv_ref, q_ref, g_ref, k_ref, v_ref,
    final, out_ref, dq_ref, drk_ref, drv_ref, all_k, all_v,
    q, g, k, v, pdk, pdv, dk, dv, out, dq, stat_in, load_sem, stat_s, stat_r, *scratch
):
    loads = [
        pltpu.make_async_copy(src, dst, load_sem.at[i])
        for i, (src, dst) in enumerate(
            ((pdk_ref, pdk), (pdv_ref, pdv), (q_ref, q), (g_ref, g), (k_ref, k), (v_ref, v))
        )
    ]
    for load in loads:
        load.start()
    head = lax.axis_index("head")
    near = everyone() + [{"head": lax.rem(head + by, HEADS)} for by in (1, HEADS - 1)]
    greet_start(near)
    greet_end(near)
    own_stat, stats = swap_stats(stat_ref, stat_in, load_sem.at[6], stat_s, stat_r)

    n = 3 + 15
    routes = []
    for half in range(2):
        part = scratch[half * n : (half + 1) * n]
        routes.append(Route(half, back_ref.at[half], final.at[half], part[0], part[1], part[2], part[3:]))
    ring_scratch = scratch[2 * n :]
    bulk = stages(routes)
    bulk[0]()

    count = q.shape[0]
    prompt_rows = pdk.shape[1] // HEADS
    slot_rows = q.shape[1] // HEADS

    def prompt_part(ref, by):
        return lambda t: ref[:, pl.ds(pl.multiple_of(t * prompt_rows, prompt_rows), prompt_rows), :] * by

    def slot_part(ref, group):
        some = slice(group * (count // GROUPS), (group + 1) * (count // GROUPS))
        return lambda t: ref[some, pl.ds(pl.multiple_of(t * slot_rows, slot_rows), slot_rows), :]

    owns = [prompt_part(pdk, factor), prompt_part(pdv, 1.0)]
    for group in range(GROUPS):
        owns += [slot_part(dk, group), slot_part(dv, group)]
    rings = []
    for i, own in enumerate(owns):
        right, left = (4, 3) if i % 2 == 0 else (3, 4)
        rings.append(Ring(own, right, left, *ring_scratch[4 * i : 4 * i + 4]))
    last = 4 * len(owns)
    spreads = [
        Spread(all_k, 4, 3, *ring_scratch[last : last + 2]),
        Spread(all_v, 3, 4, *ring_scratch[last + 2 : last + 4]),
    ]

    def ring(which, number):
        for one in rings[2 * which : 2 * which + 2]:
            one.step(number)

    def spread(number):
        for one in spreads:
            one.step(number)

    per = 5

    def local(piece):
        steps = count // per // 4

        def go(i, carry):
            slots = [(piece * steps + i) * per + j for j in range(per)]
            local_slots(
                slots, scale, factor, table_ref, prompt_ref, length_ref, stat_in, q, g, k, v, dk, dv, out, dq
            )
            return carry

        lax.fori_loop(0, steps, go, 0)

    begin, forward, turn_far, turn_forwarded, turn_near, relay_rest, turn_here, arrive, close = bulk
    loads[0].wait()
    loads[1].wait()
    ring(0, 1)
    for load in loads[2:]:
        load.wait()
    own_stat.wait()
    for copy in stats:
        copy.wait_recv()
    local(0)
    ring(0, 2)
    local(1)
    ring(1, 1)
    forward()
    local(2)
    ring(0, 3)
    local(3)
    ring(2, 1)
    leaving = [
        pltpu.make_async_copy(src, dst, load_sem.at[i]) for i, (src, dst) in enumerate(((out, out_ref), (dq, dq_ref)))
    ]
    for copy in leaving:
        copy.start()
    ring(0, 4)
    ring(1, 2)
    turn_far()
    ring(2, 2)
    all_k[head] = rings[0].result().astype(BF16)
    all_v[head] = rings[1].result().astype(BF16)
    spread(1)
    ring(1, 3)
    turn_forwarded()
    ring(2, 3)
    spread(2)
    turn_near()
    ring(1, 4)
    relay_rest()
    spread(3)
    ring(2, 4)
    turn_here()
    spread(4)
    half_count = count // GROUPS
    for group in range(GROUPS):
        some = slice(group * half_count, (group + 1) * half_count)
        drk_ref[some] = rings[2 + 2 * group].result()
        drv_ref[some] = rings[3 + 2 * group].result()
    for one in spreads:
        one.close()
    arrive()
    for copy in leaving:
        copy.wait()
    close()
    for one in rings:
        one.close()
    for copy in stats:
        copy.wait_send()


GROUPS = 2


def give_back(table, prompts, lengths, back, stats, pdk, pdv, queries, grads, keys, values, scale, factor):
    count, rows, dim = queries.shape
    held, length, _ = pdk.shape
    height = back.shape[-2]
    n_dp = 2 * SIDE * SIDE
    V, D = pltpu.VMEM, pltpu.SemaphoreType.DMA
    resp = (count, rows, dim)
    scratch = [V(resp, BF16)] * 4 + [V(pdk.shape, F32)] * 2 + [V(resp, F32)] * 2 + [V(resp, BF16)] * 2
    scratch += [V((n_dp, STAT, dim), BF16), D((7,)), D((n_dp,)), D((n_dp,))]
    for _ in range(2):
        scratch += route_scratch(height, dim, BF16) + route_sems()
    for shape in ((held, length // HEADS, dim),) * 2 + ((count // GROUPS, rows // HEADS, dim),) * (2 * GROUPS):
        scratch += [V((7,) + shape, BF16), V((7,) + shape, BF16), D((7,)), D((7,))]
    scratch += [D((7,))] * 4
    smem = pl.BlockSpec(memory_space=pltpu.SMEM)
    anywhere = pl.BlockSpec(memory_space=pl.ANY)
    vmem = pl.BlockSpec(memory_space=pltpu.VMEM)
    part = jax.ShapeDtypeStruct((count, rows // HEADS, dim), F32)
    parts = jax.ShapeDtypeStruct((HEADS, held, length // HEADS, dim), BF16)
    return pl.pallas_call(
        functools.partial(return_kernel, scale, factor),
        out_shape=(
            jax.ShapeDtypeStruct(back.shape, BF16),
            jax.ShapeDtypeStruct(resp, BF16),
            jax.ShapeDtypeStruct(resp, BF16),
            part,
            part,
            parts,
            parts,
        ),
        in_specs=[smem] * 3 + [anywhere] * 8,
        out_specs=(anywhere, anywhere, anywhere, vmem, vmem, vmem, vmem),
        scratch_shapes=scratch,
        compiler_params=pltpu.CompilerParams(collective_id=2, has_side_effects=True),
    )(table, prompts, lengths, back, stats, pdk, pdv, queries, grads, keys, values)


def finish_kernel(
    per_step, table_ref, prompt_ref, length_ref, in_ref, out_part, dq_part, drk, drv, pk, pv,
    out_ref, dq_ref, drk_ref, drv_ref, pk_ref, pv_ref, back, in_sem,
):
    rows = out_part.shape[1]
    step = pl.program_id(0)

    def coming(slot):
        return pltpu.make_async_copy(in_ref.at[table_ref[0, slot]], back.at[slot], in_sem.at[slot])

    @pl.when(step == 0)
    def _():
        for slot in range(back.shape[0]):
            coming(slot).start()

    drk_ref[...] = drk[...]
    drv_ref[...] = drv[...]
    part = pk.shape[2]
    for i in range(pk.shape[0]):
        pk_ref[:, i * part : (i + 1) * part, :] = pk[i].astype(F32)
        pv_ref[:, i * part : (i + 1) * part, :] = pv[i].astype(F32)
    for j in range(per_step):
        slot = step * per_step + j
        coming(slot).wait()
        row = lax.broadcasted_iota(jnp.int32, out_part.shape[1:], 0)
        live = row < jnp.where(prompt_ref[slot] >= 0, length_ref[slot], 0)
        out = back[slot, 0:rows, :].astype(F32) + out_part[j].astype(F32)
        dq = back[slot, rows : 2 * rows, :].astype(F32) + dq_part[j].astype(F32)
        out_ref[j] = jnp.where(live, out, 0.0).astype(BF16)
        dq_ref[j] = jnp.where(live, dq, 0.0).astype(BF16)


def finish(table, prompts, lengths, back, out_part, dq_part, drk, drv, all_k, all_v):
    count, rows, dim = out_part.shape
    _, held, part, _ = all_k.shape
    steps = 2
    per_step = count // steps
    some = pl.BlockSpec((per_step, rows, dim), lambda i, a, b, c: (i, 0, 0))
    own = pl.BlockSpec((per_step, rows // HEADS, dim), lambda i, a, b, c: (i, 0, 0))
    piece = pl.BlockSpec((HEADS // steps, held, part, dim), lambda i, a, b, c: (i, 0, 0, 0))
    placed = pl.BlockSpec((held, part * HEADS // steps, dim), lambda i, a, b, c: (0, i, 0))
    return pl.pallas_call(
        functools.partial(finish_kernel, per_step),
        out_shape=(jax.ShapeDtypeStruct((count, rows, dim), BF16),) * 2
        + (jax.ShapeDtypeStruct(drk.shape, F32),) * 2
        + (jax.ShapeDtypeStruct((held, HEADS * part, dim), F32),) * 2,
        grid_spec=pltpu.PrefetchScalarGridSpec(
            num_scalar_prefetch=3,
            grid=(steps,),
            in_specs=[pl.BlockSpec(memory_space=pl.ANY), some, some, own, own, piece, piece],
            out_specs=(some, some, own, own, placed, placed),
            scratch_shapes=[pltpu.VMEM((count, 2 * rows, dim), BF16), pltpu.SemaphoreType.DMA((count,))],
        ),
    )(table, prompts, lengths, back, out_part, dq_part, drk, drv, all_k, all_v)


def table_kernel(held, prompt_ref, table_ref):
    x, y, _ = place()
    count = prompt_ref.shape[1]
    prompts = prompt_ref[...]
    own_row = jnp.where(prompts >= 0, jnp.right_shift(prompts, held.bit_length() - 1), -1)
    one = lax.broadcasted_iota(jnp.int32, (count, count), 0)
    two = lax.broadcasted_iota(jnp.int32, (count, count), 1)
    own_column = jnp.sum(jnp.where(one == two, own_row, 0), axis=1, keepdims=True)
    same = own_column == own_row
    order_column = jnp.sum(jnp.where(same & (two < one), 1, 0), axis=1, keepdims=True)
    order_row = jnp.sum(jnp.where(same & (one < two), 1, 0), axis=0, keepdims=True)

    def position(own, order, x_from, y_from, stand):
        hx, hy, hc = jnp.right_shift(own, 3), jnp.bitwise_and(jnp.right_shift(own, 1), 3), jnp.bitwise_and(own, 1)
        hx, hy = jnp.bitwise_and(hx - x_from, SIDE - 1), jnp.bitwise_and(hy - y_from, SIDE - 1)
        first, second = jnp.where(order == 0, hx, hy), jnp.where(order == 0, hy, hx)
        at = ((order * SIDE + first) * SIDE + second) * 2 + hc
        return jnp.where(own >= 0, at, stand)

    table_ref[...] = jnp.zeros_like(table_ref)
    table_ref[0:1, 0:count] = position(own_row, order_row, x, y, 0)
    table_ref[1:2, 0:count] = jnp.where(own_row >= 0, own_row * 2 + order_row, 0)
    items = 4 * SIDE * SIDE
    slot = lax.broadcasted_iota(jnp.int32, (count, items), 0)
    item = lax.broadcasted_iota(jnp.int32, (count, items), 1)
    target = position(own_column, order_column, 0, 0, -1)
    table_ref[2:3, 0:items] = jnp.sum(jnp.where(target == item, slot, 0), axis=0, keepdims=True)
    stat = jnp.where(own_column >= 0, own_column * 2 + order_column, -1)
    table_ref[3:4, 0:items] = jnp.sum(jnp.where(stat == item, slot + 1, 0), axis=0, keepdims=True) - 1
    item = lax.broadcasted_iota(jnp.int32, (1, items), 1)
    table_ref[4:5, 0:items] = position(jnp.right_shift(item, 1), jnp.bitwise_and(item, 1), 0, 0, 0)


def body(queries, resp_keys, resp_values, prompt_keys, prompt_values, grad_out, slot_prompt, slot_length):
    slot_count, rows, dim = queries.shape
    held, length, _ = prompt_keys.shape
    factor = dim ** (-0.5)
    scale = factor * LOG2E
    items = 4 * SIDE * SIDE
    table = pl.pallas_call(
        functools.partial(table_kernel, held), out_shape=jax.ShapeDtypeStruct((8, 128), jnp.int32)
    )(slot_prompt.reshape(1, slot_count))
    received, stats_in, groups = send_out(
        held, table, slot_prompt, slot_length, queries, grad_out, resp_keys, resp_values, scale
    )
    received = received.reshape((items,) + received.shape[4:])
    result, stats, pdk, pdv = holder(groups, table, received, stats_in, prompt_keys, prompt_values, scale, factor)
    grid = (2, SIDE, SIDE, 2)
    back, local_out, local_dq, drk, drv, all_k, all_v = give_back(
        table, slot_prompt, slot_length, result.reshape(grid + result.shape[1:]),
        stats, pdk, pdv, queries, grad_out, resp_keys, resp_values, scale, factor,
    )
    return finish(
        table, slot_prompt, slot_length, back.reshape(result.shape), local_out, local_dq, drk, drv, all_k, all_v
    )


def solution(mesh):
    return jax.shard_map(
        body,
        mesh=mesh,
        in_specs=(
            P("dp", None, "head"),
            P("dp", None, None),
            P("dp", None, None),
            P("dp", None, None),
            P("dp", None, None),
            P("dp", None, "head"),
            P("dp"),
            P("dp"),
        ),
        out_specs=(
            P("dp", None, "head"),
            P("dp", None, "head"),
            P("dp", "head", None),
            P("dp", "head", None),
            P("dp", None, None),
            P("dp", None, None),
        ),
        check_vma=False,
    )
```
